32 devices in a mesh: groups: 2 (over y), gx: 4 (over z), gy: 2 (over x), gz: 2 (over core).
Axes of the slice: x: 2, y: 2, z: 4, core: 2. Of those that a mesh axis runs over, the one named last changes fastest.
Arguments:
- heat: float32 [64, 256, 256], P('gz', ('groups', 'gx'), 'gy'), parts along dimension 1, may hold values from -6 to 6
- material: int32 [64, 256, 256], P('gz', ('groups', 'gx'), 'gy'), parts along dimension 1, may hold values from 0 to 7
- table: float32 [8], replicated, may hold values from 0.5 to 8
Outputs:
- temperature: float32 [64, 256, 256], P('gz', ('groups', 'gx'), 'gy'), parts along dimension 1
The draws below stay inside these ranges and needn't reach their ends.
There are 2 independent parts, one for each index of `groups`. The reference program is written for one: setup_inputs(seed, part) draws one part's arguments, and reference() takes and returns one part's arrays. A program takes and returns all parts, laid end to end along the dimension named above; an argument that names none is the same for every part. Nothing has to cross between parts.
All inputs are finite; a program needn't handle non-finite values.
Results may differ from the reference program's by a relative error of at most 0.0003.
Values sent between devices are 32-bit elements; how exact they have to be, the bound alone decides.
A program may use at most 64 MiB of HBM per device.

```python
import math
import jax
import jax.numpy as jnp
from jax import lax

NMAT = 8
BLOCK = 16
PRE = 2
POST = 2
NZ = 64
NX = 128
NY = 256
MZ = 4
MX = 8
MY = 16


def set_ends(values, own_key, low, high):
    longest = values.shape.index(max(values.shape))
    spots = []
    for shift in (0, 1):
        where = [jax.random.randint(jax.random.fold_in(own_key, axis), (), 0, length) for axis, length in enumerate(values.shape)]
        where[longest] = (where[longest] + shift) % values.shape[longest]
        spots.append(tuple(where))
    return values.at[spots[0]].set(low).at[spots[1]].set(high)


def block_scale(stream_key, shape, shards, least, high):
    def one(position, blocks):
        steps = jax.random.uniform(jax.random.fold_in(jax.random.fold_in(stream_key, 6), position), (blocks,), jnp.float32, least / len(shards), high / len(shards))
        return jnp.repeat(jnp.exp(steps), shape[position] // blocks).reshape((-1,) + (1,) * (len(shape) - position - 1))

    gain = one(*shards[0])
    for cut in shards[1:]:
        gain = gain * one(*cut)
    return gain


def noise(own_key, extent, width, limit, pieces=(), dtype=jnp.bfloat16):
    array = width * jax.random.normal(own_key, extent, jnp.float32)
    if pieces:
        array = array * block_scale(own_key, extent, pieces, -0.22, 0.18)
    return jnp.clip(array, -limit, limit).astype(dtype)


def setup_inputs(seed: int = 0, part: int = 0) -> dict:
    seeds = jax.random.split(jax.random.key(seed), 4)
    part_keys = jax.random.split(jax.random.fold_in(seeds[3], part), 4)
    heat = noise(part_keys[0], (NZ, NX, NY), 1.0, 6.0, ((0, 2), (1, 4), (2, 2)), jnp.float32)
    material = set_ends(jax.random.randint(part_keys[1], (NZ, NX, NY), 0, NMAT), jax.random.fold_in(part_keys[1], 1), 0, NMAT - 1).astype(jnp.int32)
    table = jnp.clip(jnp.exp(jax.random.uniform(seeds[2], (NMAT,), jnp.float32, math.log(0.5), math.log(8.0))), 0.5, 8.0)
    return dict(heat=heat, material=material, table=table)


def harmonic(center, other):
    inside = other > 0.0
    total = jnp.where(inside, center + other, 1.0)
    return jnp.where(inside, 2.0 * center * other / total, center)


def shifted(padded, dim, step, shape, margin):
    start = [margin, margin, margin]
    start[dim] = start[dim] + step
    return padded[start[0]:start[0] + shape[0], start[1]:start[1] + shape[1], start[2]:start[2] + shape[2]]


def stencil_weights(kpad, shape, margin):
    center = shifted(kpad, 0, 0, shape, margin)
    weights = []
    for dim in range(3):
        for step in (-1, 1):
            weights.append(harmonic(center, shifted(kpad, dim, step, shape, margin)))
    return weights


def neighbour_sum(weights, upad, shape, margin):
    total = None
    index = 0
    for dim in range(3):
        for step in (-1, 1):
            term = weights[index] * shifted(upad, dim, step, shape, margin)
            total = term if total is None else total + term
            index = index + 1
    return total


def sine_table(count):
    idx = jnp.arange(1, count + 1).astype(jnp.float32)
    return jnp.sin(math.pi * idx[:, None] * idx[None, :] / (count + 1))


def eigen_values(count):
    idx = jnp.arange(1, count + 1).astype(jnp.float32)
    return 2.0 - 2.0 * jnp.cos(math.pi * idx / (count + 1))


def coarse_solve(coarse, kbar):
    high = lax.Precision.HIGHEST
    sz, sx, sy = sine_table(MZ), sine_table(MX), sine_table(MY)
    hat = jnp.einsum('az,zxy->axy', sz, coarse, precision=high)
    hat = jnp.einsum('bx,axy->aby', sx, hat, precision=high)
    hat = jnp.einsum('cy,aby->abc', sy, hat, precision=high)
    denom = eigen_values(MZ)[:, None, None] + eigen_values(MX)[None, :, None] + eigen_values(MY)[None, None, :]
    hat = hat / denom
    hat = jnp.einsum('az,zxy->axy', sz, hat, precision=high)
    hat = jnp.einsum('bx,axy->aby', sx, hat, precision=high)
    hat = jnp.einsum('cy,aby->abc', sy, hat, precision=high)
    scale = BLOCK * BLOCK * 8.0 / ((MZ + 1) * (MX + 1) * (MY + 1) * kbar)
    return hat * scale


def reference(heat, material, table):
    shape = heat.shape
    kappa = jnp.zeros(shape, jnp.float32)
    for mat in range(NMAT):
        kappa = kappa + jnp.where(material == mat, table[mat], 0.0)
    weights = stencil_weights(jnp.pad(kappa, 1), shape, 1)
    diag = weights[0] + weights[1] + weights[2] + weights[3] + weights[4] + weights[5]
    parity = (lax.broadcasted_iota(jnp.int32, shape, 0) + lax.broadcasted_iota(jnp.int32, shape, 1)
              + lax.broadcasted_iota(jnp.int32, shape, 2)) % 2
    red = parity == 0
    black = parity == 1

    def sweep(field):
        for mask in (red, black):
            upad = jnp.pad(field, 1)
            field = jnp.where(mask, (heat + neighbour_sum(weights, upad, shape, 1)) / diag, field)
        return field

    field = jnp.zeros(shape, jnp.float32)
    for turn in range(PRE):
        field = sweep(field)
    upad = jnp.pad(field, 1)
    residual = heat - (diag * field - neighbour_sum(weights, upad, shape, 1))
    coarse = residual.reshape(MZ, BLOCK, MX, BLOCK, MY, BLOCK).mean(axis=(1, 3, 5))
    correction = coarse_solve(coarse, jnp.mean(table))
    fine = jnp.broadcast_to(correction[:, None, :, None, :, None], (MZ, BLOCK, MX, BLOCK, MY, BLOCK)).reshape(shape)
    field = field + fine
    for turn in range(POST):
        field = sweep(field)
    return field
```

```python
import functools
import math

import jax
import jax.numpy as jnp
import numpy as np
from jax import lax
from jax.experimental import pallas as pl
from jax.experimental.pallas import tpu as pltpu
from jax.sharding import PartitionSpec as P

BLOCK = 16
PAD = 8
DEPTH = 4
GROUP = DEPTH + 2
X_ROWS = (DEPTH, DEPTH - 1, DEPTH - 1, DEPTH - 2)
MESH = pl.DeviceIdType.MESH
HIGH = lax.Precision.HIGHEST
UNROLL = 6


def sine_rows(count):
    j = np.arange(-1, count + 1)[:, None] + 1.0
    k = np.arange(count)[None, :] + 1.0
    rows = np.sin(math.pi * j * k / (count + 1))
    rows[0] = 0.0
    rows[-1] = 0.0
    return rows


def sides_of(n_gy):
    return 0 if n_gy == 1 else 1 if n_gy == 2 else 2


def tables(shape, n_gx, n_gy, n_gz):
    nz, nx, ny = shape
    lz, lx, ly = (s // BLOCK for s in shape)
    fz, fx, fy = lz * n_gz, lx * n_gx, ly * n_gy
    cols = fz * fy
    wide = -(-cols // 128) * 128
    sz, sx, sy = sine_rows(fz), sine_rows(fx), sine_rows(fy)
    n_sides = sides_of(n_gy)
    lane = np.arange(ny)
    spread = np.zeros((n_gy, n_gz, wide, (lz + 2 + n_sides) * ny))
    gather = np.zeros((n_gy, n_gz, (2 * lz + 2) * ny, wide))
    for a in range(n_gy):
        yrow = np.floor_divide(np.arange(-1, ny + 1) + a * ny, BLOCK) + 1
        own, prev, after = sy[yrow[1:-1]], sy[yrow[:-2]], sy[yrow[2:]]
        ends = np.where((lane % BLOCK == 0)[:, None], prev - own, 0.0)
        ends = np.where((lane % BLOCK == BLOCK - 1)[:, None], after - own, ends)
        for b in range(n_gz):
            zrow = np.arange(-1, lz + 1) + b * lz + 1
            for i, row in enumerate(zrow):
                block = np.einsum("p,yq->pqy", sz[row], own).reshape(cols, -1)
                spread[a, b, :cols, i * ny : (i + 1) * ny] = block
                gather[a, b, i * ny : (i + 1) * ny, :cols] = block.T
                if 1 <= i <= lz:
                    at = (lz + 1 + i) * ny
                    block = np.einsum("p,yq->pqy", sz[row], ends).reshape(cols, -1)
                    gather[a, b, at : at + ny, :cols] = block.T
            count = (nz // 2 + DEPTH) * GROUP
            zi, c = np.arange(count) // GROUP, np.arange(count) % GROUP
            fine = np.floor_divide(2 * zi - DEPTH + b * nz, BLOCK) + 1
            for side in range(n_sides):
                high = a == 0 if n_sides == 1 else side == 1
                base = ny - 1 if high else -DEPTH - 1
                column = np.floor_divide(base + c + a * ny, BLOCK) + 1
                block = np.einsum("lp,lq->pql", sz[fine], sy[column]).reshape(cols, -1)
                at = (lz + 2 + side) * ny
                spread[a, b, :cols, at : at + count] = block
    rows = nx + 2 * PAD
    expand = np.zeros((n_gx, rows, fx))
    shrink = np.zeros((n_gx, 2, fx, nx))
    for a in range(n_gx):
        xs = np.arange(-DEPTH, nx + DEPTH) + a * nx
        expand[a, PAD - DEPTH : PAD + nx + DEPTH] = sx[np.floor_divide(xs, BLOCK) + 1]
        block = np.arange(nx) // BLOCK + a * lx + 1
        shrink[a, 0] = sx[block].T
        step = np.where(np.arange(nx) % BLOCK == 0, -1, 0) + np.where(np.arange(nx) % BLOCK == BLOCK - 1, 1, 0)
        shrink[a, 1] = (sx[block + step] - sx[block]).T
    lam = lambda n: 2.0 - 2.0 * np.cos(math.pi * (np.arange(n) + 1.0) / (n + 1))
    total = lam(fx)[:, None] + (lam(fz)[:, None] + lam(fy)[None, :]).reshape(1, -1)
    scale = np.zeros((fx, wide))
    scale[:, :cols] = BLOCK * BLOCK * 8.0 / ((fz + 1) * (fx + 1) * (fy + 1)) / total / BLOCK**3
    return [t.astype(np.float32) for t in (spread, gather, expand, shrink, scale)]


def kernel(
    sizes, shape, heat_hbm, mat_hbm, table_hbm, spread_hbm, gather_hbm, expand_hbm, shrink_hbm, scale_hbm,
    out, heat, mat, zheat, zmat, table, kh, sh, ps, xs, xr, xsb, xrb, red, black, post, sred, sblack, spost, psb, wd, hd, dg, leak,
    swd, shd, hsum, vsum, corr, spread, gather, expand, shrink, scale, got,
    in_sem, z_send, z_recv, a_send, a_recv, b_send, b_recv, gsend, grecv,
):
    n_gx, n_gy, n_gz = sizes
    nz, nx, ny = shape
    lz = nz // BLOCK
    pairs = nz // 2
    halo = DEPTH // 2
    full = nx + 2 * DEPTH
    gx, gy, gz = lax.axis_index("gx"), lax.axis_index("gy"), lax.axis_index("gz")
    count = n_gx * n_gy * n_gz
    me = (gx * n_gy + gy) * n_gz + gz
    zero = gx // n_gx
    rcp = functools.partial(pltpu.reciprocal, approx=True)

    few = count <= 32
    offsets = sorted(
        ((a, b, c) for a in range(n_gx) for b in range(n_gy) for c in range(n_gz) if a or b or c),
        key=lambda o: (-min(o[0], n_gx - o[0]), -min(o[1], n_gy - o[1]), -o[2]),
    )

    def turned(position, step, size):
        at = position + step
        return jnp.where(at >= size, at - size, at)

    def peer_of(step):
        if few:
            a, b, c = offsets[step - 1]
            at = turned(gx, a, n_gx), turned(gy, b, n_gy), turned(gz, c, n_gz)
            return (at[0] * n_gy + at[1]) * n_gz + at[2], dict(zip(("gx", "gy", "gz"), at))
        other = lax.rem(me + step, count)
        return other, {
            "gx": other // (n_gy * n_gz),
            "gy": lax.rem(other // n_gz, n_gy),
            "gz": lax.rem(other, n_gz),
        }

    def each_peer(action):
        if few:
            for step in range(1, count):
                action(step)
            return

        def one(step, carry):
            action(step)
            return carry

        lax.fori_loop(1, count, one, 0)

    inputs = [
        pltpu.make_async_copy(table_hbm, table, in_sem.at[5]),
        pltpu.make_async_copy(mat_hbm, mat, in_sem.at[6]),
        pltpu.make_async_copy(heat_hbm, heat, in_sem.at[7]),
    ]
    for copy in inputs:
        copy.start()
    barrier = pltpu.get_barrier_semaphore()

    def greet(step):
        _, where = peer_of(step)
        pl.semaphore_signal(barrier, inc=1, device_id=where, device_id_type=MESH)

    each_peer(greet)

    fetch = [
        pltpu.make_async_copy(spread_hbm.at[gy, gz], spread, in_sem.at[0]),
        pltpu.make_async_copy(gather_hbm.at[gy, gz], gather, in_sem.at[1]),
        pltpu.make_async_copy(expand_hbm.at[gx], expand, in_sem.at[2]),
        pltpu.make_async_copy(shrink_hbm.at[gx], shrink, in_sem.at[3]),
        pltpu.make_async_copy(scale_hbm, scale, in_sem.at[4]),
    ]
    for copy in fetch:
        copy.start()

    if n_gy == 1:
        strips = []
    elif n_gy == 2:
        strips = [((ny - 1) * (1 - gy), (DEPTH + 1) * gy, 1 + (DEPTH - 1) * gy, (ny - DEPTH) * (1 - gy), None, 1 - gy, 0)]
    else:
        strips = [
            (0, DEPTH + 1, DEPTH, 0, gy > 0, gy - 1, 1),
            (ny - 1, 0, 1, ny - DEPTH, gy < n_gy - 1, gy + 1, 0),
        ]

    def guarded(exists, action):
        if exists is None:
            action()
        else:
            pl.when(exists)(action)

    def both(a, b):
        return b if a is None else a if b is None else jnp.logical_and(a, b)

    def lanes(n):
        return lax.broadcasted_iota(jnp.int32, (n, ny), 1)

    def sublanes(n):
        return lax.broadcasted_iota(jnp.int32, (n, ny), 0)

    lane = lanes(full)
    even = lax.rem(lane + sublanes(full), 2) == 0
    lane_own = lanes(nx)
    even_own = lax.rem(lane_own + sublanes(nx), 2) == 0
    row_x = sublanes(full) - DEPTH
    inside_row = jnp.logical_and(row_x + gx * nx >= 0, row_x + gx * nx < n_gx * nx)
    column = lax.rem(lane, GROUP)
    zgroup = lane // GROUP
    inner_group = jnp.where(jnp.logical_and(column >= 1, column <= DEPTH), zgroup, -1)
    first_z, last_z = halo * (1 - gz), pairs + halo + halo * (1 - gz)
    in_strip = jnp.logical_and(
        jnp.logical_and(inside_row, inner_group >= 0), jnp.logical_and(zgroup >= first_z, zgroup < last_z)
    )
    low_open, high_open = gy == 0, gy == n_gy - 1

    def open_lane(n):
        at = lanes(n)
        return jnp.logical_or(
            jnp.logical_and(at == 0, low_open), jnp.logical_and(at == ny - 1, high_open)
        )

    closed = {n: jnp.where(open_lane(n), 0.0, 1.0) for n in (full, nx)}

    def rows_of(n, shift=0):
        if n == nx and shift == 0:
            return pl.ds(PAD, nx)
        return pl.ds(zero + (PAD - (n - nx) // 2 + shift), n)

    def loop(count, step, carry, unroll=UNROLL):
        return lax.fori_loop(0, count, step, carry, unroll=unroll)

    def spin(value, amount):
        return pltpu.roll(value, lax.rem(amount + 4 * ny, ny), 1)

    inputs[0].wait()
    small = lax.broadcasted_iota(jnp.int32, (8, ny), 1)
    values = jnp.full((8, ny), table[0], jnp.float32)
    for m in range(1, table.shape[0]):
        values = jnp.where(small == m, table[m], values)
    resist = rcp(values)

    def look(ids):
        parts = [
            jnp.take_along_axis(resist, ids[8 * t : 8 * t + 8], axis=1) for t in range(nx // 8)
        ]
        return jnp.concatenate(parts, axis=0)

    x_open = jnp.logical_or(
        jnp.logical_and(sublanes(nx) == 0, gx == 0), jnp.logical_and(sublanes(nx) == nx - 1, gx == n_gx - 1)
    )
    faces_open = jnp.where(x_open, 1.0, 0.0) + jnp.where(open_lane(nx), 1.0, 0.0)

    def store_pair(slab, ids0, ids1, heat0, heat1):
        r0, r1 = look(ids0), look(ids1)
        kh[1, slab, pl.ds(PAD, nx), :] = jnp.where(even_own, r0, r1)
        kh[0, slab, pl.ds(PAD, nx), :] = jnp.where(even_own, r1, r0)
        kh[2, slab, pl.ds(PAD, nx), :] = jnp.where(even_own, heat0, heat1)
        kh[3, slab, pl.ds(PAD, nx), :] = jnp.where(even_own, heat1, heat0)

    def own_pair(z, carry):
        slab = z + halo + 1
        store_pair(slab, mat[2 * z], mat[2 * z + 1], heat[2 * z], heat[2 * z + 1])
        low = jnp.where(jnp.logical_and(z == 0, gz == 0), 1.0, 0.0)
        high = jnp.where(jnp.logical_and(z == pairs - 1, gz == n_gz - 1), 1.0, 0.0)
        faces = faces_open + jnp.where(even_own, low, high)
        leak[z] = faces * rcp(kh[1, slab, pl.ds(PAD, nx), :])
        return carry

    inputs[1].wait()
    inputs[2].wait()
    loop(pairs, own_pair, 0, 4)
    for layer in range(lz):
        def add(z, total):
            return total + heat[layer * BLOCK + z]
        hsum[layer] = loop(BLOCK, add, jnp.zeros((nx, ny), jnp.float32), 4)

    blank = jnp.zeros((full, ny), jnp.float32)
    for field in (red, black, post):
        for slab in (0, 1, 2, pairs + 2 * halo - 1, pairs + 2 * halo, pairs + 2 * halo + 1):
            field[slab] = jnp.zeros((nx + 2 * PAD, ny), jnp.float32)

        def clear(z, carry):
            field[z, pl.ds(0, PAD), :] = jnp.zeros((PAD, ny), jnp.float32)
            field[z, pl.ds(PAD + nx, PAD), :] = jnp.zeros((PAD, ny), jnp.float32)
            return carry

        loop(pairs + 2 * halo + 2, clear, 0)
    for buf in (sred, sblack, spost):
        for side in range(len(strips)):
            buf[side] = jnp.zeros((nx + 2 * PAD, ny), jnp.float32)

    def calm(slab, carry):
        for a in range(2):
            for row in (PAD - DEPTH - 1, PAD + nx + DEPTH):
                kh[a, slab, pl.ds(row, 1), :] = jnp.ones((1, ny), jnp.float32)
        return carry

    loop(pairs + 2 * halo + 2, calm, 0)
    for side in range(len(strips)):
        for a in range(2):
            for row in (PAD - DEPTH - 1, PAD + nx + DEPTH):
                sh[side, a, pl.ds(row, 1), :] = jnp.ones((1, ny), jnp.float32)

    def fill(start):
        def slab(z, carry):
            for a in range(4):
                kh[a, z, pl.ds(start, DEPTH), :] = jnp.full((DEPTH, ny), 1.0 if a < 2 else 0.0, jnp.float32)
            return carry

        loop(pairs + 2 * halo + 2, slab, 0)
        for side in range(len(strips)):
            for a in range(4):
                sh[side, a, pl.ds(start, DEPTH), :] = jnp.full((DEPTH, ny), 1.0 if a < 2 else 0.0, jnp.float32)

    pl.when(gx == 0)(lambda: fill(PAD - DEPTH))
    pl.when(gx == n_gx - 1)(lambda: fill(PAD + nx))
    for side, strip_of in enumerate(strips):
        if strip_of[4] is not None:
            def vacant(side=side):
                for a in range(4):
                    sh[side, a] = jnp.full((nx + 2 * PAD, ny), 1.0 if a < 2 else 0.0, jnp.float32)

            pl.when(jnp.logical_not(strip_of[4]))(vacant)

    pl.semaphore_wait(barrier, count - 1)

    z_edge = (nz - DEPTH) * (1 - gz)
    z_copies = [
        pltpu.make_async_remote_copy(
            src_ref=src.at[pl.ds(z_edge, DEPTH)],
            dst_ref=dst,
            send_sem=z_send.at[i],
            recv_sem=z_recv.at[i],
            device_id={"gz": 1 - gz},
            device_id_type=MESH,
        )
        for i, (src, dst) in enumerate(((mat, zmat), (heat, zheat)))
    ]
    for copy in z_copies:
        copy.start()
    for copy in z_copies:
        copy.wait_recv()
    beyond = 1 + (pairs + halo) * (1 - gz)
    for z in range(halo):
        store_pair(beyond + z, zmat[2 * z], zmat[2 * z + 1], zheat[2 * z], zheat[2 * z + 1])
    wall, wall_own = halo + (pairs + 1) * gz, halo + 1 + (pairs - 1) * gz
    for a in range(2):
        kh[a, wall, pl.ds(PAD, nx), :] = kh[1 - a, wall_own, pl.ds(PAD, nx), :]

    def gather_strip(value, z, col0, pack):
        n = value.shape[0]
        return jnp.where(inner_group[:n] == z, spin(value, z * GROUP + 1 - col0), pack)

    def pack_all(z, packs):
        z = z + 1 - gz
        result = []
        for (_, _, _, col0, _, _, _), pack in zip(strips, packs):
            result.append(tuple(
                gather_strip(kh[a, z + 1, pl.ds(PAD, nx), :], z, col0, pack[a]) for a in range(4)
            ))
        return tuple(result)

    ones, nothing = jnp.ones((nx, ny), jnp.float32), jnp.zeros((nx, ny), jnp.float32)
    packs = loop(pairs + halo + 1, pack_all, tuple((ones, ones, nothing, nothing) for _ in strips))
    for side, pack in enumerate(packs):
        for a in range(4):
            ps[side, a, pl.ds(PAD, nx), :] = pack[a]

    def x_side(step):
        return (gx > 0) if step < 0 else (gx < n_gx - 1)

    def x_rows(step, n):
        if step > 0:
            return pl.ds(PAD + nx - n, n), pl.ds(PAD - n, n)
        return pl.ds(PAD, n), pl.ds(PAD + nx, n)

    def messages(x_parts, y_src, y_dst, send, recv, landing):
        at = 0

        def make(src, dst, exists, where):
            nonlocal at
            copy = pltpu.make_async_remote_copy(
                src_ref=src, dst_ref=dst, send_sem=send.at[at], recv_sem=recv.at[at], device_id=where, device_id_type=MESH
            )
            at += 1
            return exists, copy

        if n_gx > 1:
            for step in (1, -1):
                to = -step if landing else step
                src, dst = x_parts
                face = (1 - step) // 2
                yield make(src.at[face], dst.at[face], x_side(to), {"gx": gx + to})
        for side, (_, _, _, _, exists, there, other) in enumerate(strips):
            mine = side if not landing else side
            target = side if landing else other
            slot = at
            lanes_dst = y_dst.at[target]
            own = pl.ds(PAD, nx)
            yield exists, pltpu.make_async_remote_copy(
                src_ref=y_src.at[mine].at[(*y_lead(y_src), own)],
                dst_ref=lanes_dst.at[(*y_lead(y_src), own)],
                send_sem=send.at[slot],
                recv_sem=recv.at[y_slot(slot, side, other, landing)],
                device_id={"gy": there},
                device_id_type=MESH,
            )
            at += 1
            if n_gx > 1:
                for step in (1, -1):
                    to = -step if landing else step
                    src, dst = x_rows(step, DEPTH)
                    yield both(exists, x_side(to)), pltpu.make_async_remote_copy(
                        src_ref=y_src.at[mine].at[(*y_lead(y_src), src)],
                        dst_ref=lanes_dst.at[(*y_lead(y_src), dst)],
                        send_sem=send.at[at],
                        recv_sem=recv.at[y_slot(at, side, other, landing)],
                        device_id={"gx": gx + to, "gy": there},
                        device_id_type=MESH,
                    )
                    at += 1

    stride = 3 if n_gx > 1 else 1

    def y_lead(ref):
        return (slice(None),) if len(ref.shape) == 4 else ()

    def y_slot(at, side, other, landing):
        if len(strips) < 2 or landing:
            return at
        return at + (other - side) * stride

    fields_a = [(kh.at[a], n) for a, n in enumerate(X_ROWS)]
    fields_b = [(post, DEPTH)]

    def x_pack(buf, fields, first, many):
        def slab(i, carry):
            for face, step in enumerate((1, -1)):
                at = i * sum(n for _, n in fields)
                for ref, n in fields:
                    src, _ = x_rows(step, n)
                    buf[face, pl.ds(at, n), :] = ref[i + first, src, :]
                    at = at + n
            return carry

        if n_gx > 1:
            loop(many, slab, 0)

    def x_unpack(buf, fields, first, many):
        for face, step in enumerate((1, -1)):
            def slab(i, carry):
                at = i * sum(n for _, n in fields)
                for ref, n in fields:
                    _, dst = x_rows(step, n)
                    ref[i + first, dst, :] = buf[face, pl.ds(at, n), :]
                    at = at + n
                return carry

            def side(slab=slab):
                loop(many, slab, 0)

            if n_gx > 1:
                pl.when(x_side(-step))(side)

    x_pack(xs, fields_a, 2 - gz, pairs + halo + 1)
    a_args = ((xs, xr), ps, sh, a_send, a_recv)
    for exists, copy in messages(*a_args, False):
        guarded(exists, copy.start)
    for exists, copy in messages(*a_args, True):
        guarded(exists, copy.wait_recv)
    x_unpack(xr, fields_a, 2 - gz, pairs + halo + 1)

    def mirror(outer, inner):
        def slab(z, carry):
            for a in range(2):
                kh[a, z + 1, outer, :] = kh[1 - a, z + 1, inner, :]
            return carry

        loop(pairs + 2 * halo, slab, 0)
        for side in range(len(strips)):
            for a in range(2):
                sh[side, a, outer, :] = sh[side, 1 - a, inner, :]

    pl.when(gx == 0)(lambda: mirror(pl.ds(PAD - 1, 1), pl.ds(PAD, 1)))
    pl.when(gx == n_gx - 1)(lambda: mirror(pl.ds(PAD + nx, 1), pl.ds(PAD + nx - 1, 1)))

    def own_columns(value, z, packs):
        result = []
        n = value.shape[0]
        for (edge, own, _, _, _, _, _), pack in zip(strips, packs):
            to = z * GROUP + own
            result.append(jnp.where(lane[:n] == to, spin(value, to - edge), pack))
        return tuple(result)

    def own_mask(own):
        return jnp.logical_and(column == own, zgroup < pairs + 2 * halo)

    def own_resist(z, packs):
        z = z + 1 - gz
        return tuple(own_columns(kh[a, z + 1, rows_of(full), :], z, packs[a]) for a in range(2))

    ones = jnp.ones((full, ny), jnp.float32)
    packs = loop(pairs + halo + 1, own_resist, (tuple(ones for _ in strips),) * 2)
    for side, (_, own, _, _, _, _, _) in enumerate(strips):
        for a in range(2):
            here = sh.at[side, a]
            here[rows_of(full), :] = jnp.where(own_mask(own), packs[a][side], here[rows_of(full), :])

    def halos_of(refs, n):
        return [ref[rows_of(n), :] for ref in refs]

    def beside(value, halos, z, walls):
        n = value.shape[0]
        low, high = pltpu.roll(value, 1, 1), pltpu.roll(value, ny - 1, 1)
        ends = [
            spin(near_by, edge - (z * GROUP + adj))
            for near_by, (edge, _, adj, _, _, _, _) in zip(halos, strips)
        ]
        if len(ends) == 2:
            first, last = ends
        elif ends:
            first = last = ends[0]
        else:
            first = last = value
        if walls is None:
            first = first * closed[n]
            last = first if len(ends) < 2 else last * closed[n]
        else:
            is_open = open_lane(n)
            first = jnp.where(is_open, walls, first)
            last = first if len(ends) < 2 else jnp.where(is_open, walls, last)
        return jnp.where(lane[:n] == 0, first, low), jnp.where(lane[:n] == ny - 1, last, high)

    def around(field, color, z, n, halos, walls=None):
        here = z + 1
        evens = even if n == full else even_own
        same = field[here, rows_of(n), :]
        before, after = field[here - 1, rows_of(n), :], field[here + 1, rows_of(n), :]
        low, high = beside(same, halos, z, walls)
        return (
            same,
            jnp.where(evens, before, after) if color == 0 else jnp.where(evens, after, before),
            field[here, rows_of(n, -1), :],
            field[here, rows_of(n, 1), :],
            low,
            high,
        )

    def strip_around(ref, color):
        same = ref[rows_of(full), :]
        before, after = pltpu.roll(same, GROUP, 1), pltpu.roll(same, ny - GROUP, 1)
        return (
            same,
            jnp.where(even, after, before) if color == 0 else jnp.where(even, before, after),
            ref[rows_of(full, -1), :],
            ref[rows_of(full, 1), :],
            pltpu.roll(same, 1, 1),
            pltpu.roll(same, ny - 1, 1),
        )

    def shares(center, others):
        parts = [rcp(center + other) for other in others]
        total = parts[0]
        for part in parts[1:]:
            total = total + part
        return parts, total

    def strip_weigh(color):
        for side in range(len(strips)):
            a = 1 - color
            center = sh[side, a, rows_of(full), :]
            parts, total = shares(center, strip_around(sh.at[side, 1 - a], color))
            inverse = jnp.where(in_strip, rcp(total), 0.0)
            if strips[side][4] is not None:
                inverse = jnp.where(strips[side][4], inverse, 0.0)
            for face in range(6):
                swd[side, color, face] = parts[face] * inverse
            shd[side, color] = sh[side, 2 + color, rows_of(full), :] * (0.5 * inverse)

    def weigh(color):
        a = 1 - color
        halos = halos_of([sh.at[side, 1 - a] for side in range(len(strips))], full)

        def step(i, packs):
            z = i + halo * (1 - gz)
            center = kh[a, z + 1, rows_of(full), :]
            parts, total = shares(center, around(kh.at[1 - a], color, z, full, halos, center))
            inverse = jnp.where(inside_row, rcp(total), 0.0)
            for face in range(6):
                wd[color, face, z] = parts[face] * inverse
            ratio = kh[2 + color, z + 1, rows_of(full), :] * (0.5 * inverse)
            hd[color, z] = ratio
            if color == 1:
                dg[z] = total[DEPTH : DEPTH + nx] * 2.0
                return packs
            red[z + 1, rows_of(full), :] = ratio
            return own_columns(ratio, z, packs)

        return loop(pairs + halo, step, tuple(blank for _ in strips))

    for color in range(2):
        strip_weigh(color)
    packs = weigh(0)
    for side, (_, own, _, _, _, _, _) in enumerate(strips):
        sred[side, rows_of(full), :] = jnp.where(own_mask(own), packs[side], shd[side, 0])
    weigh(1)

    def weights_of(color, z, n):
        cut = pl.ds(0, full) if n == full else pl.ds(DEPTH, nx)
        return hd[color, z, cut, :], [wd[color, face, z, cut, :] for face in range(6)]

    def total_of(source, weights, others):
        result = source
        for weight, other in zip(weights, others):
            result = result + weight * other
        return result

    def stage(color, src, strip_src, dst, strip_dst, reach):
        halos = halos_of([strip_src.at[side] for side in range(len(strips))], full)

        def step(i, packs):
            z = i + halo - reach * gz
            source, weights = weights_of(color, z, full)
            value = total_of(source, weights, around(src, color, z, full, halos))
            dst[z + 1, rows_of(full), :] = value
            return own_columns(value, z, packs)

        packs = loop(pairs + reach, step, tuple(blank for _ in strips))
        for side, (_, own, _, _, _, _, _) in enumerate(strips):
            value = total_of(
                shd[side, color],
                [swd[side, color, face] for face in range(6)],
                strip_around(strip_src.at[side], color),
            )
            strip_dst[side, rows_of(full), :] = jnp.where(own_mask(own), packs[side], value)

    stage(1, red, sred, black, sblack, 2)
    stage(0, black, sblack, red, sred, 2)

    halos = halos_of([sred.at[side] for side in range(len(strips))], nx)
    low_lane = lax.rem(lane_own, BLOCK) == 0
    tiles = BLOCK // 8
    picks = lambda low, high: jnp.concatenate(
        [(low if t % tiles == 0 else high)[8 * t : 8 * t + 8] for t in range(nx // 8)], axis=0
    )
    none = jnp.zeros((nx, ny), jnp.float32)
    sums = []
    for layer in range(lz):
        def flow(i, carry):
            own_sum, x_sum, y_sum = carry
            z = i + layer * (BLOCK // 2) + halo
            source, weights = weights_of(1, z, nx)
            others = around(red, 1, z, nx, halos)
            value = total_of(source, weights, others)
            post[z + 1, pl.ds(PAD, nx), :] = value
            own_sum = own_sum + leak[z - halo] * others[0]
            scaled = value * dg[z]
            spare = dg[z]
            x_part = (value - picks(others[2], others[3])) * picks(weights[2], weights[3])
            y_part = (value - jnp.where(low_lane, others[4], others[5])) * jnp.where(low_lane, weights[4], weights[5])
            return own_sum, x_sum + spare * x_part, y_sum + spare * y_part

        sums.append(loop(BLOCK // 2, flow, (none, none, none), 4))

    z_from, z_to = halo + 1 + (pairs - halo) * (1 - gz), 1 + (pairs + halo) * gz
    z_back = 1 + (pairs + halo) * (1 - gz)
    own = pl.ds(PAD, nx)
    z_copy = [
        pltpu.make_async_remote_copy(
            src_ref=post.at[pl.ds(z_from, halo), own],
            dst_ref=post.at[pl.ds(to, halo), own],
            send_sem=z_send.at[2],
            recv_sem=z_recv.at[2],
            device_id={"gz": 1 - gz},
            device_id_type=MESH,
        )
        for to in (z_to, z_back)
    ]
    z_copy[0].start()

    totals = [none, *(hsum[layer] - sums[layer][0] for layer in range(lz)), none]
    for layer in range(lz):
        for late in range(2):
            z = halo + layer * (BLOCK // 2) + (BLOCK // 2 - 1) * late
            beyond_z = red[z + 2, own, :] if late else red[z, own, :]
            flux = dg[z] * wd[1, 1, z, pl.ds(DEPTH, nx), :] * (post[z + 1, own, :] - beyond_z)
            flux = jnp.where(even_own, flux, 0.0) if late else jnp.where(even_own, 0.0, flux)
            totals[layer + 1] = totals[layer + 1] - flux
            to = layer + 2 if late else layer
            totals[to] = totals[to] + flux
    for i, value in enumerate((*totals, *(s[2] for s in sums))):
        vsum[:, i * ny : (i + 1) * ny] = value
    for copy in fetch:
        copy.wait()
    part = jnp.dot(shrink[0], vsum[...], precision=HIGH, preferred_element_type=jnp.float32)
    for layer in range(lz):
        vsum[:, layer * ny : (layer + 1) * ny] = sums[layer][1]
    bent = jnp.dot(shrink[1], vsum[:, : lz * ny], precision=HIGH, preferred_element_type=jnp.float32)
    here = gather.at[pl.ds(ny, lz * ny)]
    part = jnp.dot(part, gather[...], precision=HIGH, preferred_element_type=jnp.float32)
    part = part + jnp.dot(bent, here[...], precision=HIGH, preferred_element_type=jnp.float32)
    got[me] = part

    def gathering(step, start):
        other, where = peer_of(step)
        copy = pltpu.make_async_remote_copy(
            src_ref=got.at[me],
            dst_ref=got.at[me if start else other],
            send_sem=gsend.at[step],
            recv_sem=grecv.at[me if start else other],
            device_id=where,
            device_id_type=MESH,
        )
        return copy

    each_peer(lambda step: gathering(step, True).start())

    z_copy[1].wait_recv()

    def pack_post(z, packs):
        z = z + halo * (1 - gz)
        value = post[z + 1, own, :]
        return tuple(gather_strip(value, z, s[3], pack) for s, pack in zip(strips, packs))

    packs = loop(pairs + halo, pack_post, tuple(none for _ in strips))
    for side, pack in enumerate(packs):
        psb[side, own, :] = pack
    x_pack(xsb, fields_b, 1 + halo * (1 - gz), pairs + halo)
    b_args = ((xsb, xrb), psb, spost, b_send, b_recv)
    for exists, copy in messages(*b_args, False):
        guarded(exists, copy.start)

    each_peer(lambda step: gathering(step, False).wait_recv())
    if count <= 32:
        hat = got[0]
        for i in range(1, count):
            hat = hat + got[i]
    else:
        hat = lax.fori_loop(1, count, lambda i, acc: acc + got[i], got[0])
    kbar = table[0]
    for m in range(1, table.shape[0]):
        kbar = kbar + table[m]
    kbar = kbar / table.shape[0]
    hat = hat * scale[...] / kbar
    hat = jnp.dot(hat, spread[...], precision=HIGH, preferred_element_type=jnp.float32)
    rise = jnp.dot(expand[...], hat, precision=HIGH, preferred_element_type=jnp.float32)
    for i in range(corr.shape[0]):
        corr[i] = rise[:, i * ny : (i + 1) * ny]

    z_copy[0].wait_send()
    for exists, copy in messages(*b_args, False):
        guarded(exists, copy.wait_send)
    for exists, copy in messages(*b_args, True):
        guarded(exists, copy.wait_recv)
    x_unpack(xrb, fields_b, 1 + halo * (1 - gz), pairs + halo)

    def correct(i, packs):
        z = i + halo * (1 - gz)
        layer = (z + BLOCK // 2 - halo) // (BLOCK // 2)
        value = post[z + 1, rows_of(full), :]
        value = value + corr[layer, rows_of(full), :]
        post[z + 1, rows_of(full), :] = value
        return own_columns(value, z, packs)

    packs = loop(pairs + halo, correct, tuple(blank for _ in strips))
    for side, (_, own_c, _, _, exists, _, _) in enumerate(strips):
        value = spost[side, rows_of(full), :] + corr[lz + 2 + side, rows_of(full), :]
        value = jnp.where(in_strip, value, 0.0)
        if exists is not None:
            value = jnp.where(exists, value, 0.0)
        spost[side, rows_of(full), :] = jnp.where(own_mask(own_c), packs[side], value)

    stage(0, post, spost, red, sred, 2)
    stage(1, red, sred, black, sblack, 2)
    stage(0, black, sblack, red, sred, 2)

    halos = halos_of([sred.at[side] for side in range(len(strips))], nx)

    def finish(i, carry):
        z = i + halo
        source, weights = weights_of(1, z, nx)
        others = around(red, 1, z, nx, halos)
        last = total_of(source, weights, others)
        out[2 * i] = jnp.where(even_own, others[0], last)
        out[2 * i + 1] = jnp.where(even_own, last, others[0])
        return carry

    loop(pairs, finish, 0, 4)

    for copy in z_copies:
        copy.wait_send()
    for exists, copy in messages(*a_args, False):
        guarded(exists, copy.wait_send)
    each_peer(lambda step: gathering(step, True).wait_send())


def per_device(sizes, heat, material, table):
    shape = heat.shape
    nz, nx, ny = shape
    n_gx, n_gy, n_gz = sizes
    assert n_gz == 2
    consts = tables(shape, *sizes)
    spread, gather, expand, shrink, scale = consts
    count = n_gx * n_gy * n_gz
    rows = nx + 2 * PAD
    full = nx + 2 * DEPTH
    sides = max(sides_of(n_gy), 1)
    pairs = nz // 2
    lz = nz // BLOCK
    deep = pairs + DEPTH
    f32 = jnp.float32
    vmem = pl.BlockSpec(memory_space=pltpu.VMEM)
    hbm = pl.BlockSpec(memory_space=pltpu.HBM)
    field = pltpu.VMEM((deep + 2, rows, ny), f32)
    strip = pltpu.VMEM((sides, rows, ny), f32)
    sems = pltpu.SemaphoreType.DMA
    return pl.pallas_call(
        functools.partial(kernel, sizes, shape),
        out_shape=pltpu.VMEM(shape, f32),
        in_specs=[hbm] * 8,
        out_specs=vmem,
        scratch_shapes=[
            pltpu.VMEM(shape, f32),
            pltpu.VMEM(shape, jnp.int32),
            pltpu.VMEM((DEPTH, nx, ny), f32),
            pltpu.VMEM((DEPTH, nx, ny), jnp.int32),
            pltpu.SMEM(table.shape, f32),
            pltpu.VMEM((4, deep + 2, rows, ny), f32),
            pltpu.VMEM((sides, 4, rows, ny), f32),
            pltpu.VMEM((sides, 4, rows, ny), f32),
            *[pltpu.VMEM((2, (deep - DEPTH // 2 + 1) * sum(X_ROWS), ny), f32)] * 2,
            *[pltpu.VMEM((2, (deep - DEPTH // 2) * DEPTH, ny), f32)] * 2,
            field, field, field,
            strip, strip, strip, strip,
            pltpu.VMEM((2, 6, deep, full, ny), f32),
            pltpu.VMEM((2, deep, full, ny), f32),
            pltpu.VMEM((deep, nx, ny), f32),
            pltpu.VMEM((pairs, nx, ny), f32),
            pltpu.VMEM((sides, 2, 6, full, ny), f32),
            pltpu.VMEM((sides, 2, full, ny), f32),
            pltpu.VMEM((lz, nx, ny), f32),
            pltpu.VMEM((nx, gather.shape[2]), f32),
            pltpu.VMEM((spread.shape[3] // ny, rows, ny), f32),
            pltpu.VMEM(spread.shape[2:], f32),
            pltpu.VMEM(gather.shape[2:], f32),
            pltpu.VMEM(expand.shape[1:], f32),
            pltpu.VMEM(shrink.shape[1:], f32),
            pltpu.VMEM(scale.shape, f32),
            pltpu.VMEM((count, *scale.shape), f32),
            sems((8,)),
            sems((3,)),
            sems((3,)),
            sems((12,)),
            sems((12,)),
            sems((8,)),
            sems((8,)),
            sems((count,)),
            sems((count,)),
        ],
        compiler_params=pltpu.CompilerParams(
            collective_id=0, has_side_effects=True, vmem_limit_bytes=64 * 1024 * 1024 - 3 * nz * nx * ny * 2
        ),
    )(heat, material, table, *(jnp.asarray(c) for c in consts))


def solution(mesh):
    sizes = (mesh.shape["gx"], mesh.shape["gy"], mesh.shape["gz"])
    spec = P("gz", ("groups", "gx"), "gy")
    return jax.shard_map(
        functools.partial(per_device, sizes),
        mesh=mesh,
        in_specs=(spec, spec, P()),
        out_specs=spec,
        check_vma=False,
    )
```

```python
import functools
import math

import jax
import jax.numpy as jnp
import numpy as np
from jax import lax
from jax.experimental import pallas as pl
from jax.experimental.pallas import tpu as pltpu
from jax.sharding import PartitionSpec as P

BLOCK = 16
PAD = 8
DEPTH = 4
GROUP = DEPTH + 2
X_ROWS = (DEPTH, DEPTH - 1, DEPTH - 1, DEPTH - 2)
MESH = pl.DeviceIdType.MESH
HIGH = lax.Precision.HIGHEST
UNROLL = 6


def sine_rows(count):
    j = np.arange(-1, count + 1)[:, None] + 1.0
    k = np.arange(count)[None, :] + 1.0
    rows = np.sin(math.pi * j * k / (count + 1))
    rows[0] = 0.0
    rows[-1] = 0.0
    return rows


def sides_of(n_gy):
    return 0 if n_gy == 1 else 1 if n_gy == 2 else 2


def tables(shape, n_gx, n_gy, n_gz):
    nz, nx, ny = shape
    lz, lx, ly = (s // BLOCK for s in shape)
    fz, fx, fy = lz * n_gz, lx * n_gx, ly * n_gy
    cols = fz * fy
    wide = -(-cols // 128) * 128
    sz, sx, sy = sine_rows(fz), sine_rows(fx), sine_rows(fy)
    n_sides = sides_of(n_gy)
    lane = np.arange(ny)
    spread = np.zeros((n_gy, n_gz, wide, (lz + 2 + n_sides) * ny))
    gather = np.zeros((n_gy, n_gz, (2 * lz + 2) * ny, wide))
    for a in range(n_gy):
        yrow = np.floor_divide(np.arange(-1, ny + 1) + a * ny, BLOCK) + 1
        own, prev, after = sy[yrow[1:-1]], sy[yrow[:-2]], sy[yrow[2:]]
        ends = np.where((lane % BLOCK == 0)[:, None], prev - own, 0.0)
        ends = np.where((lane % BLOCK == BLOCK - 1)[:, None], after - own, ends)
        for b in range(n_gz):
            zrow = np.arange(-1, lz + 1) + b * lz + 1
            for i, row in enumerate(zrow):
                block = np.einsum("p,yq->pqy", sz[row], own).reshape(cols, -1)
                spread[a, b, :cols, i * ny : (i + 1) * ny] = block
                gather[a, b, i * ny : (i + 1) * ny, :cols] = block.T
                if 1 <= i <= lz:
                    at = (lz + 1 + i) * ny
                    block = np.einsum("p,yq->pqy", sz[row], ends).reshape(cols, -1)
                    gather[a, b, at : at + ny, :cols] = block.T
            count = (nz // 2 + DEPTH) * GROUP
            zi, c = np.arange(count) // GROUP, np.arange(count) % GROUP
            fine = np.floor_divide(2 * zi - DEPTH + b * nz, BLOCK) + 1
            for side in range(n_sides):
                high = a == 0 if n_sides == 1 else side == 1
                base = ny - 1 if high else -DEPTH - 1
                column = np.floor_divide(base + c + a * ny, BLOCK) + 1
                block = np.einsum("lp,lq->pql", sz[fine], sy[column]).reshape(cols, -1)
                at = (lz + 2 + side) * ny
                spread[a, b, :cols, at : at + count] = block
    rows = nx + 2 * PAD
    expand = np.zeros((n_gx, rows, fx))
    shrink = np.zeros((n_gx, 2, fx, nx))
    for a in range(n_gx):
        xs = np.arange(-DEPTH, nx + DEPTH) + a * nx
        expand[a, PAD - DEPTH : PAD + nx + DEPTH] = sx[np.floor_divide(xs, BLOCK) + 1]
        block = np.arange(nx) // BLOCK + a * lx + 1
        shrink[a, 0] = sx[block].T
        step = np.where(np.arange(nx) % BLOCK == 0, -1, 0) + np.where(np.arange(nx) % BLOCK == BLOCK - 1, 1, 0)
        shrink[a, 1] = (sx[block + step] - sx[block]).T
    lam = lambda n: 2.0 - 2.0 * np.cos(math.pi * (np.arange(n) + 1.0) / (n + 1))
    total = lam(fx)[:, None] + (lam(fz)[:, None] + lam(fy)[None, :]).reshape(1, -1)
    scale = np.zeros((fx, wide))
    scale[:, :cols] = BLOCK * BLOCK * 8.0 / ((fz + 1) * (fx + 1) * (fy + 1)) / total / BLOCK**3
    return [t.astype(np.float32) for t in (spread, gather, expand, shrink, scale)]


def kernel(
    sizes, shape, heat_hbm, mat_hbm, table_hbm, spread_hbm, gather_hbm, expand_hbm, shrink_hbm, scale_hbm,
    out, heat, mat, zheat, zmat, table, kh, sh, ps, pe, re, oc, xs, xr, xs2, xr2, xsb, xrb, red, black, post, sred, sblack, spost, psb, wd, hd, dg, leak,
    swd, shd, hsum, vsum, corr, spread, gather, expand, shrink, scale, got,
    in_sem, z_send, z_recv, a_send, a_recv, e_send, e_recv, b_send, b_recv, gsend, grecv,
):
    n_gx, n_gy, n_gz = sizes
    nz, nx, ny = shape
    lz = nz // BLOCK
    pairs = nz // 2
    halo = DEPTH // 2
    full = nx + 2 * DEPTH
    gx, gy, gz = lax.axis_index("gx"), lax.axis_index("gy"), lax.axis_index("gz")
    count = n_gx * n_gy * n_gz
    me = (gx * n_gy + gy) * n_gz + gz
    zero = gx // n_gx
    rcp = functools.partial(pltpu.reciprocal, approx=True)

    few = count <= 32
    offsets = sorted(
        ((a, b, c) for a in range(n_gx) for b in range(n_gy) for c in range(n_gz) if a or b or c),
        key=lambda o: (-min(o[0], n_gx - o[0]), -min(o[1], n_gy - o[1]), -o[2]),
    )

    def turned(position, step, size):
        at = position + step
        return jnp.where(at >= size, at - size, at)

    def peer_of(step):
        if few:
            a, b, c = offsets[step - 1]
            at = turned(gx, a, n_gx), turned(gy, b, n_gy), turned(gz, c, n_gz)
            return (at[0] * n_gy + at[1]) * n_gz + at[2], dict(zip(("gx", "gy", "gz"), at))
        other = lax.rem(me + step, count)
        return other, {
            "gx": other // (n_gy * n_gz),
            "gy": lax.rem(other // n_gz, n_gy),
            "gz": lax.rem(other, n_gz),
        }

    def each_peer(action):
        if few:
            for step in range(1, count):
                action(step)
            return

        def one(step, carry):
            action(step)
            return carry

        lax.fori_loop(1, count, one, 0)

    inputs = [
        pltpu.make_async_copy(table_hbm, table, in_sem.at[5]),
        pltpu.make_async_copy(mat_hbm, mat, in_sem.at[6]),
        pltpu.make_async_copy(heat_hbm, heat, in_sem.at[7]),
    ]
    for copy in inputs:
        copy.start()
    barrier = pltpu.get_barrier_semaphore()

    def greet(step):
        _, where = peer_of(step)
        pl.semaphore_signal(barrier, inc=1, device_id=where, device_id_type=MESH)

    each_peer(greet)

    fetch = [
        pltpu.make_async_copy(spread_hbm.at[gy, gz], spread, in_sem.at[0]),
        pltpu.make_async_copy(gather_hbm.at[gy, gz], gather, in_sem.at[1]),
        pltpu.make_async_copy(expand_hbm.at[gx], expand, in_sem.at[2]),
        pltpu.make_async_copy(shrink_hbm.at[gx], shrink, in_sem.at[3]),
        pltpu.make_async_copy(scale_hbm, scale, in_sem.at[4]),
    ]
    for copy in fetch:
        copy.start()

    if n_gy == 1:
        strips = []
    elif n_gy == 2:
        strips = [((ny - 1) * (1 - gy), (DEPTH + 1) * gy, 1 + (DEPTH - 1) * gy, (ny - DEPTH) * (1 - gy), None, 1 - gy, 0)]
    else:
        strips = [
            (0, DEPTH + 1, DEPTH, 0, gy > 0, gy - 1, 1),
            (ny - 1, 0, 1, ny - DEPTH, gy < n_gy - 1, gy + 1, 0),
        ]

    def guarded(exists, action):
        if exists is None:
            action()
        else:
            pl.when(exists)(action)

    def both(a, b):
        return b if a is None else a if b is None else jnp.logical_and(a, b)

    def lanes(n):
        return lax.broadcasted_iota(jnp.int32, (n, ny), 1)

    def sublanes(n):
        return lax.broadcasted_iota(jnp.int32, (n, ny), 0)

    lane = lanes(full)
    even = lax.rem(lane + sublanes(full), 2) == 0
    lane_own = lanes(nx)
    even_own = lax.rem(lane_own + sublanes(nx), 2) == 0
    row_x = sublanes(full) - DEPTH
    inside_row = jnp.logical_and(row_x + gx * nx >= 0, row_x + gx * nx < n_gx * nx)
    column = lax.rem(lane, GROUP)
    zgroup = lane // GROUP
    inner_group = jnp.where(jnp.logical_and(column >= 1, column <= DEPTH), zgroup, -1)
    first_z, last_z = halo * (1 - gz), pairs + halo + halo * (1 - gz)
    in_strip = jnp.logical_and(
        jnp.logical_and(inside_row, inner_group >= 0), jnp.logical_and(zgroup >= first_z, zgroup < last_z)
    )
    low_open, high_open = gy == 0, gy == n_gy - 1

    def open_lane(n):
        at = lanes(n)
        return jnp.logical_or(
            jnp.logical_and(at == 0, low_open), jnp.logical_and(at == ny - 1, high_open)
        )

    closed = {n: jnp.where(open_lane(n), 0.0, 1.0) for n in (full, nx)}

    def rows_of(n, shift=0):
        if n == nx and shift == 0:
            return pl.ds(PAD, nx)
        return pl.ds(zero + (PAD - (n - nx) // 2 + shift), n)

    def loop(count, step, carry, unroll=UNROLL):
        return lax.fori_loop(0, count, step, carry, unroll=unroll)

    def spin(value, amount):
        return pltpu.roll(value, lax.rem(amount + 4 * ny, ny), 1)

    inputs[0].wait()
    small = lax.broadcasted_iota(jnp.int32, (8, ny), 1)
    values = jnp.full((8, ny), table[0], jnp.float32)
    for m in range(1, table.shape[0]):
        values = jnp.where(small == m, table[m], values)
    resist = rcp(values)

    def look(ids):
        parts = [
            jnp.take_along_axis(resist, ids[8 * t : 8 * t + 8], axis=1) for t in range(nx // 8)
        ]
        return jnp.concatenate(parts, axis=0)

    x_open = jnp.logical_or(
        jnp.logical_and(sublanes(nx) == 0, gx == 0), jnp.logical_and(sublanes(nx) == nx - 1, gx == n_gx - 1)
    )
    faces_open = jnp.where(x_open, 1.0, 0.0) + jnp.where(open_lane(nx), 1.0, 0.0)

    def store_pair(slab, ids0, ids1, heat0, heat1):
        r0, r1 = look(ids0), look(ids1)
        values = (
            jnp.where(even_own, r1, r0),
            jnp.where(even_own, r0, r1),
            jnp.where(even_own, heat0, heat1),
            jnp.where(even_own, heat1, heat0),
        )
        for a, value in enumerate(values):
            kh[a, slab, pl.ds(PAD, nx), :] = value
        return values

    def gather_strip(value, z, col0, pack):
        n = value.shape[0]
        return jnp.where(inner_group[:n] == z, spin(value, z * GROUP + 1 - col0), pack)

    def own_pair(z, packs):
        values = store_pair(z + halo + 1, mat[2 * z], mat[2 * z + 1], heat[2 * z], heat[2 * z + 1])
        return tuple(
            tuple(gather_strip(value, z + halo, at[3], old) for value, old in zip(values, pack))
            for at, pack in zip(strips, packs)
        )

    inputs[1].wait()
    inputs[2].wait()
    ones, nothing = jnp.ones((nx, ny), jnp.float32), jnp.zeros((nx, ny), jnp.float32)
    packs = loop(pairs, own_pair, tuple((ones, ones, nothing, nothing) for _ in strips), 4)
    for side, pack in enumerate(packs):
        for a in range(4):
            ps[side, a, pl.ds(PAD, nx), :] = pack[a]

    def x_side(step):
        return (gx > 0) if step < 0 else (gx < n_gx - 1)

    def x_rows(step, n):
        if step > 0:
            return pl.ds(PAD + nx - n, n), pl.ds(PAD - n, n)
        return pl.ds(PAD, n), pl.ds(PAD + nx, n)

    def messages(x_parts, y_src, y_dst, send, recv, landing):
        at = 0

        def make(src, dst, exists, where):
            nonlocal at
            copy = pltpu.make_async_remote_copy(
                src_ref=src, dst_ref=dst, send_sem=send.at[at], recv_sem=recv.at[at], device_id=where, device_id_type=MESH
            )
            at += 1
            return exists, copy

        if n_gx > 1:
            for step in (1, -1):
                to = -step if landing else step
                src, dst = x_parts
                face = (1 - step) // 2
                yield make(src.at[face], dst.at[face], x_side(to), {"gx": gx + to})
        for side, (_, _, _, _, exists, there, other) in enumerate(strips):
            mine = side if not landing else side
            target = side if landing else other
            slot = at
            lanes_dst = y_dst.at[target]
            own = pl.ds(PAD, nx)
            yield exists, pltpu.make_async_remote_copy(
                src_ref=y_src.at[mine].at[(*y_lead(y_src), own)],
                dst_ref=lanes_dst.at[(*y_lead(y_src), own)],
                send_sem=send.at[slot],
                recv_sem=recv.at[y_slot(slot, side, other, landing)],
                device_id={"gy": there},
                device_id_type=MESH,
            )
            at += 1
            if n_gx > 1:
                for step in (1, -1):
                    to = -step if landing else step
                    src, dst = x_rows(step, DEPTH)
                    yield both(exists, x_side(to)), pltpu.make_async_remote_copy(
                        src_ref=y_src.at[mine].at[(*y_lead(y_src), src)],
                        dst_ref=lanes_dst.at[(*y_lead(y_src), dst)],
                        send_sem=send.at[at],
                        recv_sem=recv.at[y_slot(at, side, other, landing)],
                        device_id={"gx": gx + to, "gy": there},
                        device_id_type=MESH,
                    )
                    at += 1

    stride = 3 if n_gx > 1 else 1

    def y_lead(ref):
        return (slice(None),) if len(ref.shape) == 4 else ()

    def y_slot(at, side, other, landing):
        if len(strips) < 2 or landing:
            return at
        return at + (other - side) * stride

    fields_a = [(kh.at[a], n) for a, n in enumerate(X_ROWS)]
    fields_b = [(post, DEPTH)]

    def x_pack(buf, fields, first, many):
        def slab(i, carry):
            for face, step in enumerate((1, -1)):
                at = i * sum(n for _, n in fields)
                for ref, n in fields:
                    src, _ = x_rows(step, n)
                    buf[face, pl.ds(at, n), :] = ref[i + first, src, :]
                    at = at + n
            return carry

        if n_gx > 1:
            loop(many, slab, 0)

    def x_unpack(buf, fields, first, many):
        for face, step in enumerate((1, -1)):
            def slab(i, carry):
                at = i * sum(n for _, n in fields)
                for ref, n in fields:
                    _, dst = x_rows(step, n)
                    ref[i + first, dst, :] = buf[face, pl.ds(at, n), :]
                    at = at + n
                return carry

            def side(slab=slab):
                loop(many, slab, 0)

            if n_gx > 1:
                pl.when(x_side(-step))(side)

    def own_columns(value, z, packs):
        result = []
        n = value.shape[0]
        for (edge, own, _, _, _, _, _), pack in zip(strips, packs):
            to = z * GROUP + own
            result.append(jnp.where(lane[:n] == to, spin(value, to - edge), pack))
        return tuple(result)

    def own_mask(own):
        return jnp.logical_and(column == own, zgroup < pairs + 2 * halo)

    x_pack(xs, fields_a, halo + 1, pairs)
    a_args = ((xs, xr), ps, sh, a_send, a_recv)
    e_args = ((xs2, xr2), pe, re, e_send, e_recv)
    pl.semaphore_wait(barrier, count - 1)

    z_edge = (nz - DEPTH) * (1 - gz)
    z_copies = [
        pltpu.make_async_remote_copy(
            src_ref=src.at[pl.ds(z_edge, DEPTH)],
            dst_ref=dst,
            send_sem=z_send.at[i],
            recv_sem=z_recv.at[i],
            device_id={"gz": 1 - gz},
            device_id_type=MESH,
        )
        for i, (src, dst) in enumerate(((mat, zmat), (heat, zheat)))
    ]
    for copy in z_copies:
        copy.start()
    for exists, copy in messages(*a_args, False):
        guarded(exists, copy.start)
    for copy in z_copies:
        copy.wait_recv()
    beyond = 1 + (pairs + halo) * (1 - gz)
    packs = [nothing for _ in strips]
    for g in range(halo):
        values = store_pair(beyond + g, zmat[2 * g], zmat[2 * g + 1], zheat[2 * g], zheat[2 * g + 1])
        for side, at in enumerate(strips):
            for a in range(4):
                to = a * (ny // 4) + g * GROUP + 1
                here = jnp.logical_and(lane_own >= to, lane_own < to + DEPTH)
                packs[side] = jnp.where(here, spin(values[a], to - at[3]), packs[side])
    for side, pack in enumerate(packs):
        pe[side, pl.ds(PAD, nx), :] = pack
    x_pack(xs2, fields_a, beyond, halo)
    for exists, copy in messages(*e_args, False):
        guarded(exists, copy.start)

    blank = jnp.zeros((full, ny), jnp.float32)
    for field in (red, black, post):
        for slab in (0, 1 + (pairs + halo) * gz, 2 + (pairs + halo) * gz, pairs + 2 * halo + 1):
            field[slab] = jnp.zeros((nx + 2 * PAD, ny), jnp.float32)

        def clear(z, carry):
            field[z, pl.ds(0, PAD), :] = jnp.zeros((PAD, ny), jnp.float32)
            field[z, pl.ds(PAD + nx, PAD), :] = jnp.zeros((PAD, ny), jnp.float32)
            return carry

        loop(pairs + 2 * halo + 2, clear, 0)
    for side in range(len(strips)):
        for buf in (sred, sblack):
            buf[side] = jnp.zeros((nx + 2 * PAD, ny), jnp.float32)
        for row in (PAD - DEPTH - 1, PAD + nx + DEPTH):
            spost[side, pl.ds(row, 1), :] = jnp.zeros((1, ny), jnp.float32)

    def calm(slab, carry):
        for a in range(2):
            for row in (PAD - DEPTH - 1, PAD + nx + DEPTH):
                kh[a, slab, pl.ds(row, 1), :] = jnp.ones((1, ny), jnp.float32)
        return carry

    loop(pairs + 2 * halo + 2, calm, 0)
    for side in range(len(strips)):
        for a in range(2):
            for row in (PAD - DEPTH - 1, PAD + nx + DEPTH):
                sh[side, a, pl.ds(row, 1), :] = jnp.ones((1, ny), jnp.float32)

    def fill(start):
        def slab(z, carry):
            for a in range(4):
                kh[a, z, pl.ds(start, DEPTH), :] = jnp.full((DEPTH, ny), 1.0 if a < 2 else 0.0, jnp.float32)
            return carry

        loop(pairs + 2 * halo + 2, slab, 0)
        for side in range(len(strips)):
            for a in range(4):
                sh[side, a, pl.ds(start, DEPTH), :] = jnp.full((DEPTH, ny), 1.0 if a < 2 else 0.0, jnp.float32)

    pl.when(gx == 0)(lambda: fill(PAD - DEPTH))
    pl.when(gx == n_gx - 1)(lambda: fill(PAD + nx))
    for side, strip_of in enumerate(strips):
        if strip_of[4] is not None:
            def vacant(side=side):
                for a in range(4):
                    sh[side, a] = jnp.full((nx + 2 * PAD, ny), 1.0 if a < 2 else 0.0, jnp.float32)

            pl.when(jnp.logical_not(strip_of[4]))(vacant)

    def losses(z, carry):
        low = jnp.where(jnp.logical_and(z == 0, gz == 0), 1.0, 0.0)
        high = jnp.where(jnp.logical_and(z == pairs - 1, gz == n_gz - 1), 1.0, 0.0)
        faces = faces_open + jnp.where(even_own, low, high)
        leak[z] = faces * rcp(kh[1, z + halo + 1, pl.ds(PAD, nx), :])
        return carry

    loop(pairs, losses, 0, 4)
    for layer in range(lz):
        def add(z, total):
            return total + heat[layer * BLOCK + z]
        hsum[layer] = loop(BLOCK, add, jnp.zeros((nx, ny), jnp.float32), 4)

    def own_resist(rows):
        def step(z, packs):
            z = z + halo * (1 - gz)
            return tuple(own_columns(kh[a, z + 1, rows, :], z, packs[a]) for a in range(2))

        fresh = jnp.ones((rows.size, ny), jnp.float32)
        packs = loop(pairs + halo, step, (tuple(fresh for _ in strips),) * 2)
        for side in range(len(strips)):
            for a in range(2):
                oc[side, a, rows, :] = packs[a][side]

    own_resist(pl.ds(PAD, nx))

    for args in (a_args, e_args):
        for exists, copy in messages(*args, True):
            guarded(exists, copy.wait_recv)
    x_unpack(xr, fields_a, halo + 1, pairs)
    x_unpack(xr2, fields_a, beyond, halo)
    own_resist(pl.ds(zero + (PAD - DEPTH), 8))
    own_resist(pl.ds(zero + (PAD + nx + DEPTH - 8), 8))
    wall, wall_own = halo + (pairs + 1) * gz, halo + 1 + (pairs - 1) * gz
    for a in range(2):
        kh[a, wall, rows_of(full), :] = kh[1 - a, wall_own, rows_of(full), :]
    x_first = beyond - 1
    came = jnp.logical_and(zgroup >= x_first, zgroup < x_first + halo)
    for side, at in enumerate(strips):
        extra = re[side, rows_of(full), :]
        whole = []
        for a in range(4):
            value = jnp.where(came, spin(extra, x_first * GROUP - a * (ny // 4)), sh[side, a, rows_of(full), :])
            if a < 2:
                value = jnp.where(own_mask(at[1]), oc[side, a, rows_of(full), :], value)
            whole.append(value)
        for a in range(4):
            value = whole[a]
            if a < 2:
                value = jnp.where(zgroup == wall - 1, spin(whole[1 - a], GROUP * (2 * gz - 1)), value)
            sh[side, a, rows_of(full), :] = value

    def mirror(outer, inner):
        def slab(z, carry):
            for a in range(2):
                kh[a, z + 1, outer, :] = kh[1 - a, z + 1, inner, :]
            return carry

        loop(pairs + 2 * halo, slab, 0)
        for side in range(len(strips)):
            for a in range(2):
                sh[side, a, outer, :] = sh[side, 1 - a, inner, :]

    pl.when(gx == 0)(lambda: mirror(pl.ds(PAD - 1, 1), pl.ds(PAD, 1)))
    pl.when(gx == n_gx - 1)(lambda: mirror(pl.ds(PAD + nx, 1), pl.ds(PAD + nx - 1, 1)))

    def halos_of(refs, n):
        return [ref[rows_of(n), :] for ref in refs]

    def beside(value, halos, z, walls):
        n = value.shape[0]
        low, high = pltpu.roll(value, 1, 1), pltpu.roll(value, ny - 1, 1)
        ends = [
            spin(near_by, edge - (z * GROUP + adj))
            for near_by, (edge, _, adj, _, _, _, _) in zip(halos, strips)
        ]
        if len(ends) == 2:
            first, last = ends
        elif ends:
            first = last = ends[0]
        else:
            first = last = value
        if walls is None:
            first = first * closed[n]
            last = first if len(ends) < 2 else last * closed[n]
        else:
            is_open = open_lane(n)
            first = jnp.where(is_open, walls, first)
            last = first if len(ends) < 2 else jnp.where(is_open, walls, last)
        return jnp.where(lane[:n] == 0, first, low), jnp.where(lane[:n] == ny - 1, last, high)

    def around(field, color, z, n, halos, walls=None):
        here = z + 1
        evens = even if n == full else even_own
        same = field[here, rows_of(n), :]
        before, after = field[here - 1, rows_of(n), :], field[here + 1, rows_of(n), :]
        low, high = beside(same, halos, z, walls)
        return (
            same,
            jnp.where(evens, before, after) if color == 0 else jnp.where(evens, after, before),
            field[here, rows_of(n, -1), :],
            field[here, rows_of(n, 1), :],
            low,
            high,
        )

    def strip_around(ref, color):
        same = ref[rows_of(full), :]
        before, after = pltpu.roll(same, GROUP, 1), pltpu.roll(same, ny - GROUP, 1)
        return (
            same,
            jnp.where(even, after, before) if color == 0 else jnp.where(even, before, after),
            ref[rows_of(full, -1), :],
            ref[rows_of(full, 1), :],
            pltpu.roll(same, 1, 1),
            pltpu.roll(same, ny - 1, 1),
        )

    def shares(center, others):
        parts = [rcp(center + other) for other in others]
        total = parts[0]
        for part in parts[1:]:
            total = total + part
        return parts, total

    def strip_weigh(color):
        for side in range(len(strips)):
            a = 1 - color
            center = sh[side, a, rows_of(full), :]
            parts, total = shares(center, strip_around(sh.at[side, 1 - a], color))
            inverse = jnp.where(in_strip, rcp(total), 0.0)
            if strips[side][4] is not None:
                inverse = jnp.where(strips[side][4], inverse, 0.0)
            for face in range(6):
                swd[side, color, face] = parts[face] * inverse
            shd[side, color] = sh[side, 2 + color, rows_of(full), :] * (0.5 * inverse)

    def weigh(color):
        a = 1 - color
        halos = halos_of([sh.at[side, 1 - a] for side in range(len(strips))], full)

        def step(i, packs):
            z = i + halo * (1 - gz)
            center = kh[a, z + 1, rows_of(full), :]
            parts, total = shares(center, around(kh.at[1 - a], color, z, full, halos, center))
            inverse = jnp.where(inside_row, rcp(total), 0.0)
            for face in range(6):
                wd[color, face, z] = parts[face] * inverse
            ratio = kh[2 + color, z + 1, rows_of(full), :] * (0.5 * inverse)
            hd[color, z] = ratio
            if color == 1:
                dg[z] = total[DEPTH : DEPTH + nx] * 2.0
                return packs
            red[z + 1, rows_of(full), :] = ratio
            return own_columns(ratio, z, packs)

        return loop(pairs + halo, step, tuple(blank for _ in strips))

    for color in range(2):
        strip_weigh(color)
    packs = weigh(0)
    for side, (_, own, _, _, _, _, _) in enumerate(strips):
        sred[side, rows_of(full), :] = jnp.where(own_mask(own), packs[side], shd[side, 0])
    weigh(1)

    def weights_of(color, z, n):
        cut = pl.ds(0, full) if n == full else pl.ds(DEPTH, nx)
        return hd[color, z, cut, :], [wd[color, face, z, cut, :] for face in range(6)]

    def total_of(source, weights, others):
        result = source
        for weight, other in zip(weights, others):
            result = result + weight * other
        return result

    def stage(color, src, strip_src, dst, strip_dst, reach):
        halos = halos_of([strip_src.at[side] for side in range(len(strips))], full)

        def step(i, packs):
            z = i + halo - reach * gz
            source, weights = weights_of(color, z, full)
            value = total_of(source, weights, around(src, color, z, full, halos))
            dst[z + 1, rows_of(full), :] = value
            return own_columns(value, z, packs)

        packs = loop(pairs + reach, step, tuple(blank for _ in strips))
        for side, (_, own, _, _, _, _, _) in enumerate(strips):
            value = total_of(
                shd[side, color],
                [swd[side, color, face] for face in range(6)],
                strip_around(strip_src.at[side], color),
            )
            strip_dst[side, rows_of(full), :] = jnp.where(own_mask(own), packs[side], value)

    stage(1, red, sred, black, sblack, 2)
    stage(0, black, sblack, red, sred, 2)

    halos = halos_of([sred.at[side] for side in range(len(strips))], nx)
    low_lane = lax.rem(lane_own, BLOCK) == 0
    tiles = BLOCK // 8
    picks = lambda low, high: jnp.concatenate(
        [(low if t % tiles == 0 else high)[8 * t : 8 * t + 8] for t in range(nx // 8)], axis=0
    )
    none = jnp.zeros((nx, ny), jnp.float32)
    sums = []
    for layer in range(lz):
        def flow(i, carry):
            own_sum, x_sum, y_sum = carry
            z = i + layer * (BLOCK // 2) + halo
            source, weights = weights_of(1, z, nx)
            others = around(red, 1, z, nx, halos)
            value = total_of(source, weights, others)
            post[z + 1, pl.ds(PAD, nx), :] = value
            own_sum = own_sum + leak[z - halo] * others[0]
            scaled = value * dg[z]
            spare = dg[z]
            x_part = (value - picks(others[2], others[3])) * picks(weights[2], weights[3])
            y_part = (value - jnp.where(low_lane, others[4], others[5])) * jnp.where(low_lane, weights[4], weights[5])
            return own_sum, x_sum + spare * x_part, y_sum + spare * y_part

        sums.append(loop(BLOCK // 2, flow, (none, none, none), 4))

    z_from, z_to = halo + 1 + (pairs - halo) * (1 - gz), 1 + (pairs + halo) * gz
    z_back = 1 + (pairs + halo) * (1 - gz)
    own = pl.ds(PAD, nx)
    z_copy = [
        pltpu.make_async_remote_copy(
            src_ref=post.at[pl.ds(z_from, halo), own],
            dst_ref=post.at[pl.ds(to, halo), own],
            send_sem=z_send.at[2],
            recv_sem=z_recv.at[2],
            device_id={"gz": 1 - gz},
            device_id_type=MESH,
        )
        for to in (z_to, z_back)
    ]
    z_copy[0].start()

    totals = [none, *(hsum[layer] - sums[layer][0] for layer in range(lz)), none]
    for layer in range(lz):
        for late in range(2):
            z = halo + layer * (BLOCK // 2) + (BLOCK // 2 - 1) * late
            beyond_z = red[z + 2, own, :] if late else red[z, own, :]
            flux = dg[z] * wd[1, 1, z, pl.ds(DEPTH, nx), :] * (post[z + 1, own, :] - beyond_z)
            flux = jnp.where(even_own, flux, 0.0) if late else jnp.where(even_own, 0.0, flux)
            totals[layer + 1] = totals[layer + 1] - flux
            to = layer + 2 if late else layer
            totals[to] = totals[to] + flux
    for i, value in enumerate((*totals, *(s[2] for s in sums))):
        vsum[:, i * ny : (i + 1) * ny] = value
    for copy in fetch:
        copy.wait()
    part = jnp.dot(shrink[0], vsum[...], precision=HIGH, preferred_element_type=jnp.float32)
    for layer in range(lz):
        vsum[:, layer * ny : (layer + 1) * ny] = sums[layer][1]
    bent = jnp.dot(shrink[1], vsum[:, : lz * ny], precision=HIGH, preferred_element_type=jnp.float32)
    here = gather.at[pl.ds(ny, lz * ny)]
    part = jnp.dot(part, gather[...], precision=HIGH, preferred_element_type=jnp.float32)
    part = part + jnp.dot(bent, here[...], precision=HIGH, preferred_element_type=jnp.float32)
    got[me] = part

    def gathering(step, start):
        other, where = peer_of(step)
        copy = pltpu.make_async_remote_copy(
            src_ref=got.at[me],
            dst_ref=got.at[me if start else other],
            send_sem=gsend.at[step],
            recv_sem=grecv.at[me if start else other],
            device_id=where,
            device_id_type=MESH,
        )
        return copy

    each_peer(lambda step: gathering(step, True).start())

    z_copy[1].wait_recv()

    def pack_post(z, packs):
        z = z + halo * (1 - gz)
        value = post[z + 1, own, :]
        return tuple(gather_strip(value, z, s[3], pack) for s, pack in zip(strips, packs))

    packs = loop(pairs + halo, pack_post, tuple(none for _ in strips))
    for side, pack in enumerate(packs):
        psb[side, own, :] = pack
    x_pack(xsb, fields_b, 1 + halo * (1 - gz), pairs + halo)
    b_args = ((xsb, xrb), psb, spost, b_send, b_recv)
    for exists, copy in messages(*b_args, False):
        guarded(exists, copy.start)

    each_peer(lambda step: gathering(step, False).wait_recv())
    if count <= 32:
        hat = got[0]
        for i in range(1, count):
            hat = hat + got[i]
    else:
        hat = lax.fori_loop(1, count, lambda i, acc: acc + got[i], got[0])
    kbar = table[0]
    for m in range(1, table.shape[0]):
        kbar = kbar + table[m]
    kbar = kbar / table.shape[0]
    hat = hat * scale[...] / kbar
    hat = jnp.dot(hat, spread[...], precision=HIGH, preferred_element_type=jnp.float32)
    rise = jnp.dot(expand[...], hat, precision=HIGH, preferred_element_type=jnp.float32)
    for i in range(corr.shape[0]):
        corr[i] = rise[:, i * ny : (i + 1) * ny]

    z_copy[0].wait_send()
    for exists, copy in messages(*b_args, False):
        guarded(exists, copy.wait_send)
    for exists, copy in messages(*b_args, True):
        guarded(exists, copy.wait_recv)
    x_unpack(xrb, fields_b, 1 + halo * (1 - gz), pairs + halo)

    def correct(i, packs):
        z = i + halo * (1 - gz)
        layer = (z + BLOCK // 2 - halo) // (BLOCK // 2)
        value = post[z + 1, rows_of(full), :]
        value = value + corr[layer, rows_of(full), :]
        post[z + 1, rows_of(full), :] = value
        return own_columns(value, z, packs)

    packs = loop(pairs + halo, correct, tuple(blank for _ in strips))
    for side, (_, own_c, _, _, exists, _, _) in enumerate(strips):
        value = spost[side, rows_of(full), :] + corr[lz + 2 + side, rows_of(full), :]
        value = jnp.where(in_strip, value, 0.0)
        if exists is not None:
            value = jnp.where(exists, value, 0.0)
        spost[side, rows_of(full), :] = jnp.where(own_mask(own_c), packs[side], value)

    stage(0, post, spost, red, sred, 2)
    stage(1, red, sred, black, sblack, 2)
    stage(0, black, sblack, red, sred, 2)

    halos = halos_of([sred.at[side] for side in range(len(strips))], nx)

    def finish(i, carry):
        z = i + halo
        source, weights = weights_of(1, z, nx)
        others = around(red, 1, z, nx, halos)
        last = total_of(source, weights, others)
        out[2 * i] = jnp.where(even_own, others[0], last)
        out[2 * i + 1] = jnp.where(even_own, last, others[0])
        return carry

    loop(pairs, finish, 0, 4)

    for copy in z_copies:
        copy.wait_send()
    for args in (a_args, e_args):
        for exists, copy in messages(*args, False):
            guarded(exists, copy.wait_send)
    each_peer(lambda step: gathering(step, True).wait_send())


def per_device(sizes, heat, material, table):
    shape = heat.shape
    nz, nx, ny = shape
    n_gx, n_gy, n_gz = sizes
    assert n_gz == 2
    consts = tables(shape, *sizes)
    spread, gather, expand, shrink, scale = consts
    count = n_gx * n_gy * n_gz
    rows = nx + 2 * PAD
    full = nx + 2 * DEPTH
    sides = max(sides_of(n_gy), 1)
    pairs = nz // 2
    lz = nz // BLOCK
    deep = pairs + DEPTH
    f32 = jnp.float32
    vmem = pl.BlockSpec(memory_space=pltpu.VMEM)
    hbm = pl.BlockSpec(memory_space=pltpu.HBM)
    field = pltpu.VMEM((deep + 2, rows, ny), f32)
    strip = pltpu.VMEM((sides, rows, ny), f32)
    sems = pltpu.SemaphoreType.DMA
    return pl.pallas_call(
        functools.partial(kernel, sizes, shape),
        out_shape=pltpu.VMEM(shape, f32),
        in_specs=[hbm] * 8,
        out_specs=vmem,
        scratch_shapes=[
            pltpu.VMEM(shape, f32),
            pltpu.VMEM(shape, jnp.int32),
            pltpu.VMEM((DEPTH, nx, ny), f32),
            pltpu.VMEM((DEPTH, nx, ny), jnp.int32),
            pltpu.SMEM(table.shape, f32),
            pltpu.VMEM((4, deep + 2, rows, ny), f32),
            pltpu.VMEM((sides, 4, rows, ny), f32),
            pltpu.VMEM((sides, 4, rows, ny), f32),
            strip, strip,
            pltpu.VMEM((sides, 2, rows, ny), f32),
            *[pltpu.VMEM((2, pairs * sum(X_ROWS), ny), f32)] * 2,
            *[pltpu.VMEM((2, DEPTH // 2 * sum(X_ROWS), ny), f32)] * 2,
            *[pltpu.VMEM((2, (deep - DEPTH // 2) * DEPTH, ny), f32)] * 2,
            field, field, field,
            strip, strip, strip, strip,
            pltpu.VMEM((2, 6, deep, full, ny), f32),
            pltpu.VMEM((2, deep, full, ny), f32),
            pltpu.VMEM((deep, nx, ny), f32),
            pltpu.VMEM((pairs, nx, ny), f32),
            pltpu.VMEM((sides, 2, 6, full, ny), f32),
            pltpu.VMEM((sides, 2, full, ny), f32),
            pltpu.VMEM((lz, nx, ny), f32),
            pltpu.VMEM((nx, gather.shape[2]), f32),
            pltpu.VMEM((spread.shape[3] // ny, rows, ny), f32),
            pltpu.VMEM(spread.shape[2:], f32),
            pltpu.VMEM(gather.shape[2:], f32),
            pltpu.VMEM(expand.shape[1:], f32),
            pltpu.VMEM(shrink.shape[1:], f32),
            pltpu.VMEM(scale.shape, f32),
            pltpu.VMEM((count, *scale.shape), f32),
            sems((8,)),
            sems((3,)),
            sems((3,)),
            sems((8,)),
            sems((8,)),
            sems((8,)),
            sems((8,)),
            sems((8,)),
            sems((8,)),
            sems((count,)),
            sems((count,)),
        ],
        compiler_params=pltpu.CompilerParams(
            collective_id=0, has_side_effects=True, vmem_limit_bytes=64 * 1024 * 1024 - 3 * nz * nx * ny * 2
        ),
    )(heat, material, table, *(jnp.asarray(c) for c in consts))


def solution(mesh):
    sizes = (mesh.shape["gx"], mesh.shape["gy"], mesh.shape["gz"])
    spec = P("gz", ("groups", "gx"), "gy")
    return jax.shard_map(
        functools.partial(per_device, sizes),
        mesh=mesh,
        in_specs=(spec, spec, P()),
        out_specs=spec,
        check_vma=False,
    )
```

```python
import functools
import math

import jax
import jax.numpy as jnp
import numpy as np
from jax import lax
from jax.experimental import pallas as pl
from jax.experimental.pallas import tpu as pltpu
from jax.sharding import PartitionSpec as P

BLOCK = 16
PAD = 8
DEPTH = 4
GROUP = DEPTH + 2
X_ROWS = (DEPTH, DEPTH - 1, DEPTH - 1, DEPTH - 2)
MESH = pl.DeviceIdType.MESH
HIGH = lax.Precision.HIGHEST
UNROLL = 18
WEIGH_UNROLL = 9
FLOW_UNROLL = 8
FINISH_UNROLL = 16


def sine_rows(count):
    j = np.arange(-1, count + 1)[:, None] + 1.0
    k = np.arange(count)[None, :] + 1.0
    rows = np.sin(math.pi * j * k / (count + 1))
    rows[0] = 0.0
    rows[-1] = 0.0
    return rows


def sides_of(n_gy):
    return 0 if n_gy == 1 else 1 if n_gy == 2 else 2


def tables(shape, n_gx, n_gy, n_gz):
    nz, nx, ny = shape
    lz, lx, ly = (s // BLOCK for s in shape)
    fz, fx, fy = lz * n_gz, lx * n_gx, ly * n_gy
    cols = fz * fy
    wide = -(-cols // 128) * 128
    sz, sx, sy = sine_rows(fz), sine_rows(fx), sine_rows(fy)
    n_sides = sides_of(n_gy)
    lane = np.arange(ny)
    spread = np.zeros((n_gy, n_gz, wide, (lz + 2 + n_sides) * ny))
    gather = np.zeros((n_gy, n_gz, (2 * lz + 2) * ny, wide))
    for a in range(n_gy):
        yrow = np.floor_divide(np.arange(-1, ny + 1) + a * ny, BLOCK) + 1
        own, prev, after = sy[yrow[1:-1]], sy[yrow[:-2]], sy[yrow[2:]]
        ends = np.where((lane % BLOCK == 0)[:, None], prev - own, 0.0)
        ends = np.where((lane % BLOCK == BLOCK - 1)[:, None], after - own, ends)
        for b in range(n_gz):
            zrow = np.arange(-1, lz + 1) + b * lz + 1
            for i, row in enumerate(zrow):
                block = np.einsum("p,yq->pqy", sz[row], own).reshape(cols, -1)
                spread[a, b, :cols, i * ny : (i + 1) * ny] = block
                gather[a, b, i * ny : (i + 1) * ny, :cols] = block.T
                if 1 <= i <= lz:
                    at = (lz + 1 + i) * ny
                    block = np.einsum("p,yq->pqy", sz[row], ends).reshape(cols, -1)
                    gather[a, b, at : at + ny, :cols] = block.T
            count = (nz // 2 + DEPTH) * GROUP
            zi, c = np.arange(count) // GROUP, np.arange(count) % GROUP
            fine = np.floor_divide(2 * zi - DEPTH + b * nz, BLOCK) + 1
            for side in range(n_sides):
                high = a == 0 if n_sides == 1 else side == 1
                base = ny - 1 if high else -DEPTH - 1
                column = np.floor_divide(base + c + a * ny, BLOCK) + 1
                block = np.einsum("lp,lq->pql", sz[fine], sy[column]).reshape(cols, -1)
                at = (lz + 2 + side) * ny
                spread[a, b, :cols, at : at + count] = block
    rows = nx + 2 * PAD
    expand = np.zeros((n_gx, rows, fx))
    shrink = np.zeros((n_gx, 2, fx, nx))
    for a in range(n_gx):
        xs = np.arange(-DEPTH, nx + DEPTH) + a * nx
        expand[a, PAD - DEPTH : PAD + nx + DEPTH] = sx[np.floor_divide(xs, BLOCK) + 1]
        block = np.arange(nx) // BLOCK + a * lx + 1
        shrink[a, 0] = sx[block].T
        step = np.where(np.arange(nx) % BLOCK == 0, -1, 0) + np.where(np.arange(nx) % BLOCK == BLOCK - 1, 1, 0)
        shrink[a, 1] = (sx[block + step] - sx[block]).T
    lam = lambda n: 2.0 - 2.0 * np.cos(math.pi * (np.arange(n) + 1.0) / (n + 1))
    total = lam(fx)[:, None] + (lam(fz)[:, None] + lam(fy)[None, :]).reshape(1, -1)
    scale = np.zeros((fx, wide))
    scale[:, :cols] = BLOCK * BLOCK * 8.0 / ((fz + 1) * (fx + 1) * (fy + 1)) / total / BLOCK**3
    return [t.astype(np.float32) for t in (spread, gather, expand, shrink, scale)]


def kernel(
    sizes, shape, heat_hbm, mat_hbm, table_hbm, spread_hbm, gather_hbm, expand_hbm, shrink_hbm, scale_hbm,
    out, heat, mat, zheat, zmat, table, kh, sh, ps, pe, re, oc, xs, xr, xs2, xr2, xsb, xrb, red, black, post, sred, sblack, spost, psb, wd, hd, dg, leak,
    swd, shd, hsum, vsum, corr, spread, gather, expand, shrink, scale, got,
    in_sem, z_send, z_recv, a_send, a_recv, e_send, e_recv, b_send, b_recv, gsend, grecv,
):
    n_gx, n_gy, n_gz = sizes
    nz, nx, ny = shape
    lz = nz // BLOCK
    pairs = nz // 2
    halo = DEPTH // 2
    full = nx + 2 * DEPTH
    gx, gy, gz = lax.axis_index("gx"), lax.axis_index("gy"), lax.axis_index("gz")
    count = n_gx * n_gy * n_gz
    me = (gx * n_gy + gy) * n_gz + gz
    zero = gx // n_gx
    rcp = functools.partial(pltpu.reciprocal, approx=True)

    few = count <= 32
    offsets = sorted(
        ((a, b, c) for a in range(n_gx) for b in range(n_gy) for c in range(n_gz) if a or b or c),
        key=lambda o: (-min(o[0], n_gx - o[0]), -min(o[1], n_gy - o[1]), -o[2]),
    )

    def turned(position, step, size):
        at = position + step
        return jnp.where(at >= size, at - size, at)

    def peer_of(step):
        if few:
            a, b, c = offsets[step - 1]
            at = turned(gx, a, n_gx), turned(gy, b, n_gy), turned(gz, c, n_gz)
            return (at[0] * n_gy + at[1]) * n_gz + at[2], dict(zip(("gx", "gy", "gz"), at))
        other = lax.rem(me + step, count)
        return other, {
            "gx": other // (n_gy * n_gz),
            "gy": lax.rem(other // n_gz, n_gy),
            "gz": lax.rem(other, n_gz),
        }

    def each_peer(action):
        if few:
            for step in range(1, count):
                action(step)
            return

        def one(step, carry):
            action(step)
            return carry

        lax.fori_loop(1, count, one, 0)

    inputs = [
        pltpu.make_async_copy(table_hbm, table, in_sem.at[5]),
        pltpu.make_async_copy(mat_hbm, mat, in_sem.at[6]),
        pltpu.make_async_copy(heat_hbm, heat, in_sem.at[7]),
    ]
    for copy in inputs:
        copy.start()
    barrier = pltpu.get_barrier_semaphore()

    def greet(step):
        _, where = peer_of(step)
        pl.semaphore_signal(barrier, inc=1, device_id=where, device_id_type=MESH)

    each_peer(greet)

    fetch = [
        pltpu.make_async_copy(spread_hbm.at[gy, gz], spread, in_sem.at[0]),
        pltpu.make_async_copy(gather_hbm.at[gy, gz], gather, in_sem.at[1]),
        pltpu.make_async_copy(expand_hbm.at[gx], expand, in_sem.at[2]),
        pltpu.make_async_copy(shrink_hbm.at[gx], shrink, in_sem.at[3]),
        pltpu.make_async_copy(scale_hbm, scale, in_sem.at[4]),
    ]
    for copy in fetch:
        copy.start()

    if n_gy == 1:
        strips = []
    elif n_gy == 2:
        strips = [((ny - 1) * (1 - gy), (DEPTH + 1) * gy, 1 + (DEPTH - 1) * gy, (ny - DEPTH) * (1 - gy), None, 1 - gy, 0)]
    else:
        strips = [
            (0, DEPTH + 1, DEPTH, 0, gy > 0, gy - 1, 1),
            (ny - 1, 0, 1, ny - DEPTH, gy < n_gy - 1, gy + 1, 0),
        ]

    def guarded(exists, action):
        if exists is None:
            action()
        else:
            pl.when(exists)(action)

    def both(a, b):
        return b if a is None else a if b is None else jnp.logical_and(a, b)

    def lanes(n):
        return lax.broadcasted_iota(jnp.int32, (n, ny), 1)

    def sublanes(n):
        return lax.broadcasted_iota(jnp.int32, (n, ny), 0)

    lane = lanes(full)
    even = lax.rem(lane + sublanes(full), 2) == 0
    lane_own = lanes(nx)
    even_own = lax.rem(lane_own + sublanes(nx), 2) == 0
    row_x = sublanes(full) - DEPTH
    inside_row = jnp.logical_and(row_x + gx * nx >= 0, row_x + gx * nx < n_gx * nx)
    column = lax.rem(lane, GROUP)
    zgroup = lane // GROUP
    inner_group = jnp.where(jnp.logical_and(column >= 1, column <= DEPTH), zgroup, -1)
    first_z, last_z = halo * (1 - gz), pairs + halo + halo * (1 - gz)
    in_strip = jnp.logical_and(
        jnp.logical_and(inside_row, inner_group >= 0), jnp.logical_and(zgroup >= first_z, zgroup < last_z)
    )
    low_open, high_open = gy == 0, gy == n_gy - 1

    def open_lane(n):
        at = lanes(n)
        return jnp.logical_or(
            jnp.logical_and(at == 0, low_open), jnp.logical_and(at == ny - 1, high_open)
        )

    closed = {n: jnp.where(open_lane(n), 0.0, 1.0) for n in (full, nx)}

    def rows_of(n, shift=0):
        if n == nx and shift == 0:
            return pl.ds(PAD, nx)
        return pl.ds(zero + (PAD - (n - nx) // 2 + shift), n)

    def loop(count, step, carry, unroll=UNROLL):
        return lax.fori_loop(0, count, step, carry, unroll=unroll)

    def spin(value, amount):
        return pltpu.roll(value, lax.rem(amount + 4 * ny, ny), 1)

    inputs[0].wait()
    small = lax.broadcasted_iota(jnp.int32, (8, ny), 1)
    values = jnp.full((8, ny), table[0], jnp.float32)
    for m in range(1, table.shape[0]):
        values = jnp.where(small == m, table[m], values)
    resist = rcp(values)

    def look(ids):
        parts = [
            jnp.take_along_axis(resist, ids[8 * t : 8 * t + 8], axis=1) for t in range(nx // 8)
        ]
        return jnp.concatenate(parts, axis=0)

    x_open = jnp.logical_or(
        jnp.logical_and(sublanes(nx) == 0, gx == 0), jnp.logical_and(sublanes(nx) == nx - 1, gx == n_gx - 1)
    )
    faces_open = jnp.where(x_open, 1.0, 0.0) + jnp.where(open_lane(nx), 1.0, 0.0)

    def store_pair(slab, ids0, ids1, heat0, heat1):
        r0, r1 = look(ids0), look(ids1)
        values = (
            jnp.where(even_own, r1, r0),
            jnp.where(even_own, r0, r1),
            jnp.where(even_own, heat0, heat1),
            jnp.where(even_own, heat1, heat0),
        )
        for a, value in enumerate(values):
            kh[a, slab, pl.ds(PAD, nx), :] = value
        return values

    def gather_strip(value, z, col0, pack):
        n = value.shape[0]
        return jnp.where(inner_group[:n] == z, spin(value, z * GROUP + 1 - col0), pack)

    def own_pair(z, packs):
        values = store_pair(z + halo + 1, mat[2 * z], mat[2 * z + 1], heat[2 * z], heat[2 * z + 1])
        return tuple(
            tuple(gather_strip(value, z + halo, at[3], old) for value, old in zip(values, pack))
            for at, pack in zip(strips, packs)
        )

    inputs[1].wait()
    inputs[2].wait()
    ones, nothing = jnp.ones((nx, ny), jnp.float32), jnp.zeros((nx, ny), jnp.float32)
    packs = loop(pairs, own_pair, tuple((ones, ones, nothing, nothing) for _ in strips), 4)
    for side, pack in enumerate(packs):
        for a in range(4):
            ps[side, a, pl.ds(PAD, nx), :] = pack[a]

    def x_side(step):
        return (gx > 0) if step < 0 else (gx < n_gx - 1)

    def x_rows(step, n):
        if step > 0:
            return pl.ds(PAD + nx - n, n), pl.ds(PAD - n, n)
        return pl.ds(PAD, n), pl.ds(PAD + nx, n)

    def messages(x_parts, y_src, y_dst, send, recv, landing):
        at = 0

        def make(src, dst, exists, where):
            nonlocal at
            copy = pltpu.make_async_remote_copy(
                src_ref=src, dst_ref=dst, send_sem=send.at[at], recv_sem=recv.at[at], device_id=where, device_id_type=MESH
            )
            at += 1
            return exists, copy

        if n_gx > 1:
            for step in (1, -1):
                to = -step if landing else step
                src, dst = x_parts
                face = (1 - step) // 2
                yield make(src.at[face], dst.at[face], x_side(to), {"gx": gx + to})
        for side, (_, _, _, _, exists, there, other) in enumerate(strips):
            mine = side if not landing else side
            target = side if landing else other
            slot = at
            lanes_dst = y_dst.at[target]
            own = pl.ds(PAD, nx)
            yield exists, pltpu.make_async_remote_copy(
                src_ref=y_src.at[mine].at[(*y_lead(y_src), own)],
                dst_ref=lanes_dst.at[(*y_lead(y_src), own)],
                send_sem=send.at[slot],
                recv_sem=recv.at[y_slot(slot, side, other, landing)],
                device_id={"gy": there},
                device_id_type=MESH,
            )
            at += 1
            if n_gx > 1:
                for step in (1, -1):
                    to = -step if landing else step
                    src, dst = x_rows(step, DEPTH)
                    yield both(exists, x_side(to)), pltpu.make_async_remote_copy(
                        src_ref=y_src.at[mine].at[(*y_lead(y_src), src)],
                        dst_ref=lanes_dst.at[(*y_lead(y_src), dst)],
                        send_sem=send.at[at],
                        recv_sem=recv.at[y_slot(at, side, other, landing)],
                        device_id={"gx": gx + to, "gy": there},
                        device_id_type=MESH,
                    )
                    at += 1

    stride = 3 if n_gx > 1 else 1

    def y_lead(ref):
        return (slice(None),) if len(ref.shape) == 4 else ()

    def y_slot(at, side, other, landing):
        if len(strips) < 2 or landing:
            return at
        return at + (other - side) * stride

    fields_a = [(kh.at[a], n) for a, n in enumerate(X_ROWS)]
    fields_b = [(post, DEPTH)]

    def x_pack(buf, fields, first, many):
        def slab(i, carry):
            for face, step in enumerate((1, -1)):
                at = i * sum(n for _, n in fields)
                for ref, n in fields:
                    src, _ = x_rows(step, n)
                    buf[face, pl.ds(at, n), :] = ref[i + first, src, :]
                    at = at + n
            return carry

        if n_gx > 1:
            loop(many, slab, 0)

    def x_unpack(buf, fields, first, many):
        for face, step in enumerate((1, -1)):
            def slab(i, carry):
                at = i * sum(n for _, n in fields)
                for ref, n in fields:
                    _, dst = x_rows(step, n)
                    ref[i + first, dst, :] = buf[face, pl.ds(at, n), :]
                    at = at + n
                return carry

            def side(slab=slab):
                loop(many, slab, 0)

            if n_gx > 1:
                pl.when(x_side(-step))(side)

    def own_columns(value, z, packs):
        result = []
        n = value.shape[0]
        for (edge, own, _, _, _, _, _), pack in zip(strips, packs):
            to = z * GROUP + own
            result.append(jnp.where(lane[:n] == to, spin(value, to - edge), pack))
        return tuple(result)

    def own_mask(own):
        return jnp.logical_and(column == own, zgroup < pairs + 2 * halo)

    x_pack(xs, fields_a, halo + 1, pairs)
    a_args = ((xs, xr), ps, sh, a_send, a_recv)
    e_args = ((xs2, xr2), pe, re, e_send, e_recv)
    pl.semaphore_wait(barrier, count - 1)

    z_edge = (nz - DEPTH) * (1 - gz)
    z_copies = [
        pltpu.make_async_remote_copy(
            src_ref=src.at[pl.ds(z_edge, DEPTH)],
            dst_ref=dst,
            send_sem=z_send.at[i],
            recv_sem=z_recv.at[i],
            device_id={"gz": 1 - gz},
            device_id_type=MESH,
        )
        for i, (src, dst) in enumerate(((mat, zmat), (heat, zheat)))
    ]
    for copy in z_copies:
        copy.start()
    for exists, copy in messages(*a_args, False):
        guarded(exists, copy.start)
    for copy in z_copies:
        copy.wait_recv()
    beyond = 1 + (pairs + halo) * (1 - gz)
    packs = [nothing for _ in strips]
    for g in range(halo):
        values = store_pair(beyond + g, zmat[2 * g], zmat[2 * g + 1], zheat[2 * g], zheat[2 * g + 1])
        for side, at in enumerate(strips):
            for a in range(4):
                to = a * (ny // 4) + g * GROUP + 1
                here = jnp.logical_and(lane_own >= to, lane_own < to + DEPTH)
                packs[side] = jnp.where(here, spin(values[a], to - at[3]), packs[side])
    for side, pack in enumerate(packs):
        pe[side, pl.ds(PAD, nx), :] = pack
    x_pack(xs2, fields_a, beyond, halo)
    for exists, copy in messages(*e_args, False):
        guarded(exists, copy.start)

    blank = jnp.zeros((full, ny), jnp.float32)
    for field in (red, black, post):
        for slab in (0, 1 + (pairs + halo) * gz, 2 + (pairs + halo) * gz, pairs + 2 * halo + 1):
            field[slab] = jnp.zeros((nx + 2 * PAD, ny), jnp.float32)

        def clear(z, carry):
            field[z, pl.ds(0, PAD), :] = jnp.zeros((PAD, ny), jnp.float32)
            field[z, pl.ds(PAD + nx, PAD), :] = jnp.zeros((PAD, ny), jnp.float32)
            return carry

        loop(pairs + 2 * halo + 2, clear, 0)
    for side in range(len(strips)):
        for buf in (sred, sblack):
            buf[side] = jnp.zeros((nx + 2 * PAD, ny), jnp.float32)
        for row in (PAD - DEPTH - 1, PAD + nx + DEPTH):
            spost[side, pl.ds(row, 1), :] = jnp.zeros((1, ny), jnp.float32)

    def calm(slab, carry):
        for a in range(2):
            for row in (PAD - DEPTH - 1, PAD + nx + DEPTH):
                kh[a, slab, pl.ds(row, 1), :] = jnp.ones((1, ny), jnp.float32)
        return carry

    loop(pairs + 2 * halo + 2, calm, 0)
    for side in range(len(strips)):
        for a in range(2):
            for row in (PAD - DEPTH - 1, PAD + nx + DEPTH):
                sh[side, a, pl.ds(row, 1), :] = jnp.ones((1, ny), jnp.float32)

    def fill(start):
        def slab(z, carry):
            for a in range(4):
                kh[a, z, pl.ds(start, DEPTH), :] = jnp.full((DEPTH, ny), 1.0 if a < 2 else 0.0, jnp.float32)
            return carry

        loop(pairs + 2 * halo + 2, slab, 0)
        for side in range(len(strips)):
            for a in range(4):
                sh[side, a, pl.ds(start, DEPTH), :] = jnp.full((DEPTH, ny), 1.0 if a < 2 else 0.0, jnp.float32)

    pl.when(gx == 0)(lambda: fill(PAD - DEPTH))
    pl.when(gx == n_gx - 1)(lambda: fill(PAD + nx))
    for side, strip_of in enumerate(strips):
        if strip_of[4] is not None:
            def vacant(side=side):
                for a in range(4):
                    sh[side, a] = jnp.full((nx + 2 * PAD, ny), 1.0 if a < 2 else 0.0, jnp.float32)

            pl.when(jnp.logical_not(strip_of[4]))(vacant)

    def losses(z, carry):
        low = jnp.where(jnp.logical_and(z == 0, gz == 0), 1.0, 0.0)
        high = jnp.where(jnp.logical_and(z == pairs - 1, gz == n_gz - 1), 1.0, 0.0)
        faces = faces_open + jnp.where(even_own, low, high)
        leak[z] = faces * rcp(kh[1, z + halo + 1, pl.ds(PAD, nx), :])
        return carry

    loop(pairs, losses, 0, 4)
    for layer in range(lz):
        def add(z, total):
            return total + heat[layer * BLOCK + z]
        hsum[layer] = loop(BLOCK, add, jnp.zeros((nx, ny), jnp.float32), 4)

    def own_resist(rows):
        def step(z, packs):
            z = z + halo * (1 - gz)
            return tuple(own_columns(kh[a, z + 1, rows, :], z, packs[a]) for a in range(2))

        fresh = jnp.ones((rows.size, ny), jnp.float32)
        packs = loop(pairs + halo, step, (tuple(fresh for _ in strips),) * 2)
        for side in range(len(strips)):
            for a in range(2):
                oc[side, a, rows, :] = packs[a][side]

    own_resist(pl.ds(PAD, nx))

    for args in (a_args, e_args):
        for exists, copy in messages(*args, True):
            guarded(exists, copy.wait_recv)
    x_unpack(xr, fields_a, halo + 1, pairs)
    x_unpack(xr2, fields_a, beyond, halo)
    own_resist(pl.ds(zero + (PAD - DEPTH), 8))
    own_resist(pl.ds(zero + (PAD + nx + DEPTH - 8), 8))
    wall, wall_own = halo + (pairs + 1) * gz, halo + 1 + (pairs - 1) * gz
    for a in range(2):
        kh[a, wall, rows_of(full), :] = kh[1 - a, wall_own, rows_of(full), :]
    x_first = beyond - 1
    came = jnp.logical_and(zgroup >= x_first, zgroup < x_first + halo)
    for side, at in enumerate(strips):
        extra = re[side, rows_of(full), :]
        whole = []
        for a in range(4):
            value = jnp.where(came, spin(extra, x_first * GROUP - a * (ny // 4)), sh[side, a, rows_of(full), :])
            if a < 2:
                value = jnp.where(own_mask(at[1]), oc[side, a, rows_of(full), :], value)
            whole.append(value)
        for a in range(4):
            value = whole[a]
            if a < 2:
                value = jnp.where(zgroup == wall - 1, spin(whole[1 - a], GROUP * (2 * gz - 1)), value)
            sh[side, a, rows_of(full), :] = value

    def mirror(outer, inner):
        def slab(z, carry):
            for a in range(2):
                kh[a, z + 1, outer, :] = kh[1 - a, z + 1, inner, :]
            return carry

        loop(pairs + 2 * halo, slab, 0)
        for side in range(len(strips)):
            for a in range(2):
                sh[side, a, outer, :] = sh[side, 1 - a, inner, :]

    pl.when(gx == 0)(lambda: mirror(pl.ds(PAD - 1, 1), pl.ds(PAD, 1)))
    pl.when(gx == n_gx - 1)(lambda: mirror(pl.ds(PAD + nx, 1), pl.ds(PAD + nx - 1, 1)))

    wide, inner = [(True, t) for t in range(full // 8)], [(False, t) for t in range(nx // 8)]
    even8, lane8, column_step = even_own[:8], lane_own[:8], lax.rem(lane_own[:8], BLOCK) == 0
    open8 = open_lane(8)
    closed8 = jnp.where(open8, 0.0, 1.0)

    def at(tile, shift=0):
        deep, t = tile
        if not deep and shift == 0:
            return pl.ds(PAD + 8 * t, 8)
        return pl.ds(zero + (PAD - (DEPTH if deep else 0) + 8 * t + shift), 8)

    def cut(tile):
        deep, t = tile
        return pl.ds(8 * t, 8) if deep else pl.ds(zero + (DEPTH + 8 * t), 8)

    def halos_of(refs, tiles):
        return [[ref[at(tile), :] for ref in refs] for tile in tiles]

    def beside(value, halos, z, walls):
        low, high = pltpu.roll(value, 1, 1), pltpu.roll(value, ny - 1, 1)
        ends = [
            spin(near_by, edge - (z * GROUP + adj))
            for near_by, (edge, _, adj, _, _, _, _) in zip(halos, strips)
        ]
        ends = ends or [value]
        if walls is None:
            ends = [end * closed8 for end in ends]
        else:
            ends = [jnp.where(open8, walls, end) for end in ends]
        return jnp.where(lane8 == 0, ends[0], low), jnp.where(lane8 == ny - 1, ends[-1], high)

    def around(field, color, z, tile, halos, walls=None):
        here = z + 1
        same = field[here, at(tile), :]
        before, after = field[here - 1, at(tile), :], field[here + 1, at(tile), :]
        low, high = beside(same, halos, z, walls)
        return (
            same,
            jnp.where(even8, before, after) if color == 0 else jnp.where(even8, after, before),
            field[here, at(tile, -1), :],
            field[here, at(tile, 1), :],
            low,
            high,
        )

    def tile_packs(values, z, packs):
        return tuple(own_columns(value, z, pack) for value, pack in zip(values, packs))

    blank8 = jnp.zeros((8, ny), jnp.float32)
    no_packs = tuple(tuple(blank8 for _ in strips) for _ in wide)

    def joined(packs, side):
        return jnp.concatenate([pack[side] for pack in packs], axis=0)

    def strip_around(ref, color):
        same = ref[rows_of(full), :]
        before, after = pltpu.roll(same, GROUP, 1), pltpu.roll(same, ny - GROUP, 1)
        return (
            same,
            jnp.where(even, after, before) if color == 0 else jnp.where(even, before, after),
            ref[rows_of(full, -1), :],
            ref[rows_of(full, 1), :],
            pltpu.roll(same, 1, 1),
            pltpu.roll(same, ny - 1, 1),
        )

    def shares(center, others):
        parts = [rcp(center + other) for other in others]
        total = parts[0]
        for part in parts[1:]:
            total = total + part
        return parts, total

    def strip_weigh(color):
        for side in range(len(strips)):
            a = 1 - color
            center = sh[side, a, rows_of(full), :]
            parts, total = shares(center, strip_around(sh.at[side, 1 - a], color))
            inverse = jnp.where(in_strip, rcp(total), 0.0)
            if strips[side][4] is not None:
                inverse = jnp.where(strips[side][4], inverse, 0.0)
            for face in range(6):
                swd[side, color, face] = parts[face] * inverse
            shd[side, color] = sh[side, 2 + color, rows_of(full), :] * (0.5 * inverse)

    def weigh(color):
        a = 1 - color
        halos = halos_of([sh.at[side, 1 - a] for side in range(len(strips))], wide)

        def step(i, packs):
            z = i + halo * (1 - gz)
            ratios = []
            for tile in wide:
                t = tile[1]
                center = kh[a, z + 1, at(tile), :]
                parts, total = shares(center, around(kh.at[1 - a], color, z, tile, halos[t], center))
                inverse = rcp(total)
                if t in (0, len(wide) - 1):
                    inverse = jnp.where(inside_row[8 * t : 8 * t + 8], inverse, 0.0)
                for face in range(6):
                    wd[color, face, z, cut(tile), :] = parts[face] * inverse
                ratio = kh[2 + color, z + 1, at(tile), :] * (0.5 * inverse)
                hd[color, z, cut(tile), :] = ratio
                if color == 1:
                    dg[z, cut(tile), :] = total * 2.0
                else:
                    red[z + 1, at(tile), :] = ratio
                    ratios.append(ratio)
            return packs if color == 1 else tile_packs(ratios, z, packs)

        return loop(pairs + halo, step, no_packs, WEIGH_UNROLL)

    for color in range(2):
        strip_weigh(color)
    packs = weigh(0)
    for side, (_, own, _, _, _, _, _) in enumerate(strips):
        sred[side, rows_of(full), :] = jnp.where(own_mask(own), joined(packs, side), shd[side, 0])
    weigh(1)

    def weights_of(color, z, tile):
        return hd[color, z, cut(tile), :], [wd[color, face, z, cut(tile), :] for face in range(6)]

    def total_of(source, weights, others):
        result = source
        for weight, other in zip(weights, others):
            result = result + weight * other
        return result

    def stage(color, src, strip_src, dst, strip_dst, reach):
        halos = halos_of([strip_src.at[side] for side in range(len(strips))], wide)

        def step(i, packs):
            first = i + halo - reach * gz
            values = []
            for z in [first + k for k in range(pairs + reach)]:
                values.append([])
                for tile in wide:
                    source, weights = weights_of(color, z, tile)
                    values[-1].append(total_of(source, weights, around(src, color, z, tile, halos[tile[1]])))
            for k, row in enumerate(values):
                for tile, value in zip(wide, row):
                    dst[first + k + 1, at(tile), :] = value
            for k, row in enumerate(values):
                packs = tile_packs(row, first + k, packs)
            return packs

        packs = step(0, no_packs)
        for side, (_, own, _, _, _, _, _) in enumerate(strips):
            value = total_of(
                shd[side, color],
                [swd[side, color, face] for face in range(6)],
                strip_around(strip_src.at[side], color),
            )
            strip_dst[side, rows_of(full), :] = jnp.where(own_mask(own), joined(packs, side), value)

    stage(1, red, sred, black, sblack, 2)
    stage(0, black, sblack, red, sred, 2)

    halos = halos_of([sred.at[side] for side in range(len(strips))], inner)
    tiles = BLOCK // 8
    none = jnp.zeros((nx, ny), jnp.float32)
    sums = []
    for layer in range(lz):
        def flow(i, carry):
            z = i + layer * (BLOCK // 2) + halo
            result = []
            for tile, (own_sum, x_sum, y_sum) in zip(inner, carry):
                t = tile[1]
                source, weights = weights_of(1, z, tile)
                others = around(red, 1, z, tile, halos[t])
                value = total_of(source, weights, others)
                post[z + 1, at(tile), :] = value
                spare = dg[z, cut(tile), :]
                face = 2 if t % tiles == 0 else 3
                own_sum = own_sum + leak[z - halo, pl.ds(8 * t, 8), :] * others[0]
                if t % tiles in (0, tiles - 1):
                    x_sum = x_sum + spare * ((value - others[face]) * weights[face])
                aside, weight = (
                    jnp.where(column_step, pair[0], pair[1]) for pair in (others[4:], weights[4:])
                )
                y_sum = y_sum + spare * ((value - aside) * weight)
                result.append((own_sum, x_sum, y_sum))
            return tuple(result)

        parts = loop(BLOCK // 2, flow, tuple((blank8,) * 3 for _ in inner), FLOW_UNROLL)
        sums.append(tuple(jnp.concatenate([part[i] for part in parts], axis=0) for i in range(3)))

    z_from, z_to = halo + 1 + (pairs - halo) * (1 - gz), 1 + (pairs + halo) * gz
    z_back = 1 + (pairs + halo) * (1 - gz)
    own = pl.ds(PAD, nx)
    z_copy = [
        pltpu.make_async_remote_copy(
            src_ref=post.at[pl.ds(z_from, halo), own],
            dst_ref=post.at[pl.ds(to, halo), own],
            send_sem=z_send.at[2],
            recv_sem=z_recv.at[2],
            device_id={"gz": 1 - gz},
            device_id_type=MESH,
        )
        for to in (z_to, z_back)
    ]
    z_copy[0].start()

    totals = [none, *(hsum[layer] - sums[layer][0] for layer in range(lz)), none]
    for layer in range(lz):
        for late in range(2):
            z = halo + layer * (BLOCK // 2) + (BLOCK // 2 - 1) * late
            beyond_z = red[z + 2, own, :] if late else red[z, own, :]
            deep_rows = pl.ds(zero + DEPTH, nx)
            flux = dg[z, deep_rows, :] * wd[1, 1, z, deep_rows, :] * (post[z + 1, own, :] - beyond_z)
            flux = jnp.where(even_own, flux, 0.0) if late else jnp.where(even_own, 0.0, flux)
            totals[layer + 1] = totals[layer + 1] - flux
            to = layer + 2 if late else layer
            totals[to] = totals[to] + flux
    for i, value in enumerate((*totals, *(s[2] for s in sums))):
        vsum[:, i * ny : (i + 1) * ny] = value
    for copy in fetch:
        copy.wait()
    part = jnp.dot(shrink[0], vsum[...], precision=HIGH, preferred_element_type=jnp.float32)
    for layer in range(lz):
        vsum[:, layer * ny : (layer + 1) * ny] = sums[layer][1]
    bent = jnp.dot(shrink[1], vsum[:, : lz * ny], precision=HIGH, preferred_element_type=jnp.float32)
    here = gather.at[pl.ds(ny, lz * ny)]
    part = jnp.dot(part, gather[...], precision=HIGH, preferred_element_type=jnp.float32)
    part = part + jnp.dot(bent, here[...], precision=HIGH, preferred_element_type=jnp.float32)
    got[me] = part

    def gathering(step, start):
        other, where = peer_of(step)
        copy = pltpu.make_async_remote_copy(
            src_ref=got.at[me],
            dst_ref=got.at[me if start else other],
            send_sem=gsend.at[step],
            recv_sem=grecv.at[me if start else other],
            device_id=where,
            device_id_type=MESH,
        )
        return copy

    each_peer(lambda step: gathering(step, True).start())

    z_copy[1].wait_recv()

    def pack_post(z, packs):
        z = z + halo * (1 - gz)
        value = post[z + 1, own, :]
        return tuple(gather_strip(value, z, s[3], pack) for s, pack in zip(strips, packs))

    packs = loop(pairs + halo, pack_post, tuple(none for _ in strips))
    for side, pack in enumerate(packs):
        psb[side, own, :] = pack
    x_pack(xsb, fields_b, 1 + halo * (1 - gz), pairs + halo)
    b_args = ((xsb, xrb), psb, spost, b_send, b_recv)
    for exists, copy in messages(*b_args, False):
        guarded(exists, copy.start)

    each_peer(lambda step: gathering(step, False).wait_recv())
    if count <= 32:
        hat = got[0]
        for i in range(1, count):
            hat = hat + got[i]
    else:
        hat = lax.fori_loop(1, count, lambda i, acc: acc + got[i], got[0])
    kbar = table[0]
    for m in range(1, table.shape[0]):
        kbar = kbar + table[m]
    kbar = kbar / table.shape[0]
    hat = hat * scale[...] / kbar
    hat = jnp.dot(hat, spread[...], precision=HIGH, preferred_element_type=jnp.float32)
    rise = jnp.dot(expand[...], hat, precision=HIGH, preferred_element_type=jnp.float32)
    for i in range(corr.shape[0]):
        corr[i] = rise[:, i * ny : (i + 1) * ny]

    z_copy[0].wait_send()
    for exists, copy in messages(*b_args, False):
        guarded(exists, copy.wait_send)
    for exists, copy in messages(*b_args, True):
        guarded(exists, copy.wait_recv)
    x_unpack(xrb, fields_b, 1 + halo * (1 - gz), pairs + halo)

    def correct(i, packs):
        z = i + halo * (1 - gz)
        layer = (z + BLOCK // 2 - halo) // (BLOCK // 2)
        value = post[z + 1, rows_of(full), :]
        value = value + corr[layer, rows_of(full), :]
        post[z + 1, rows_of(full), :] = value
        return own_columns(value, z, packs)

    packs = loop(pairs + halo, correct, tuple(blank for _ in strips))
    for side, (_, own_c, _, _, exists, _, _) in enumerate(strips):
        value = spost[side, rows_of(full), :] + corr[lz + 2 + side, rows_of(full), :]
        value = jnp.where(in_strip, value, 0.0)
        if exists is not None:
            value = jnp.where(exists, value, 0.0)
        spost[side, rows_of(full), :] = jnp.where(own_mask(own_c), packs[side], value)

    stage(0, post, spost, red, sred, 2)
    stage(1, red, sred, black, sblack, 2)
    stage(0, black, sblack, red, sred, 2)

    halos = halos_of([sred.at[side] for side in range(len(strips))], inner)

    def finish(i, carry):
        z = i + halo
        for tile in inner:
            source, weights = weights_of(1, z, tile)
            others = around(red, 1, z, tile, halos[tile[1]])
            last = total_of(source, weights, others)
            rows = pl.ds(8 * tile[1], 8)
            out[2 * i, rows, :] = jnp.where(even8, others[0], last)
            out[2 * i + 1, rows, :] = jnp.where(even8, last, others[0])
        return carry

    loop(pairs, finish, 0, FINISH_UNROLL)

    for copy in z_copies:
        copy.wait_send()
    for args in (a_args, e_args):
        for exists, copy in messages(*args, False):
            guarded(exists, copy.wait_send)
    each_peer(lambda step: gathering(step, True).wait_send())


def per_device(sizes, heat, material, table):
    shape = heat.shape
    nz, nx, ny = shape
    n_gx, n_gy, n_gz = sizes
    assert n_gz == 2
    consts = tables(shape, *sizes)
    spread, gather, expand, shrink, scale = consts
    count = n_gx * n_gy * n_gz
    rows = nx + 2 * PAD
    full = nx + 2 * DEPTH
    sides = max(sides_of(n_gy), 1)
    pairs = nz // 2
    lz = nz // BLOCK
    deep = pairs + DEPTH
    f32 = jnp.float32
    vmem = pl.BlockSpec(memory_space=pltpu.VMEM)
    hbm = pl.BlockSpec(memory_space=pltpu.HBM)
    field = pltpu.VMEM((deep + 2, rows, ny), f32)
    strip = pltpu.VMEM((sides, rows, ny), f32)
    sems = pltpu.SemaphoreType.DMA
    return pl.pallas_call(
        functools.partial(kernel, sizes, shape),
        out_shape=pltpu.VMEM(shape, f32),
        in_specs=[hbm] * 8,
        out_specs=vmem,
        scratch_shapes=[
            pltpu.VMEM(shape, f32),
            pltpu.VMEM(shape, jnp.int32),
            pltpu.VMEM((DEPTH, nx, ny), f32),
            pltpu.VMEM((DEPTH, nx, ny), jnp.int32),
            pltpu.SMEM(table.shape, f32),
            pltpu.VMEM((4, deep + 2, rows, ny), f32),
            pltpu.VMEM((sides, 4, rows, ny), f32),
            pltpu.VMEM((sides, 4, rows, ny), f32),
            strip, strip,
            pltpu.VMEM((sides, 2, rows, ny), f32),
            *[pltpu.VMEM((2, pairs * sum(X_ROWS), ny), f32)] * 2,
            *[pltpu.VMEM((2, DEPTH // 2 * sum(X_ROWS), ny), f32)] * 2,
            *[pltpu.VMEM((2, (deep - DEPTH // 2) * DEPTH, ny), f32)] * 2,
            field, field, field,
            strip, strip, strip, strip,
            pltpu.VMEM((2, 6, deep, full, ny), f32),
            pltpu.VMEM((2, deep, full, ny), f32),
            pltpu.VMEM((deep, full, ny), f32),
            pltpu.VMEM((pairs, nx, ny), f32),
            pltpu.VMEM((sides, 2, 6, full, ny), f32),
            pltpu.VMEM((sides, 2, full, ny), f32),
            pltpu.VMEM((lz, nx, ny), f32),
            pltpu.VMEM((nx, gather.shape[2]), f32),
            pltpu.VMEM((spread.shape[3] // ny, rows, ny), f32),
            pltpu.VMEM(spread.shape[2:], f32),
            pltpu.VMEM(gather.shape[2:], f32),
            pltpu.VMEM(expand.shape[1:], f32),
            pltpu.VMEM(shrink.shape[1:], f32),
            pltpu.VMEM(scale.shape, f32),
            pltpu.VMEM((count, *scale.shape), f32),
            sems((8,)),
            sems((3,)),
            sems((3,)),
            sems((8,)),
            sems((8,)),
            sems((8,)),
            sems((8,)),
            sems((8,)),
            sems((8,)),
            sems((count,)),
            sems((count,)),
        ],
        compiler_params=pltpu.CompilerParams(
            collective_id=0, has_side_effects=True, vmem_limit_bytes=64 * 1024 * 1024 - 3 * nz * nx * ny * 2
        ),
    )(heat, material, table, *(jnp.asarray(c) for c in consts))


def solution(mesh):
    sizes = (mesh.shape["gx"], mesh.shape["gy"], mesh.shape["gz"])
    spec = P("gz", ("groups", "gx"), "gy")
    return jax.shard_map(
        functools.partial(per_device, sizes),
        mesh=mesh,
        in_specs=(spec, spec, P()),
        out_specs=spec,
        check_vma=False,
    )
```

```python
import functools
import math

import jax
import jax.numpy as jnp
import numpy as np
from jax import lax
from jax.experimental import pallas as pl
from jax.experimental.pallas import tpu as pltpu
from jax.sharding import PartitionSpec as P

BLOCK = 16
PAD = 8
DEPTH = 4
GROUP = DEPTH + 2
X_ROWS = (DEPTH, DEPTH - 1, DEPTH - 1, DEPTH - 2)
MESH = pl.DeviceIdType.MESH
HIGH = lax.Precision.HIGHEST
UNROLL = 18
RELAYS = 3
WEIGH_UNROLL = 9
FLOW_UNROLL = 8
FINISH_UNROLL = 16


def sine_rows(count):
    j = np.arange(-1, count + 1)[:, None] + 1.0
    k = np.arange(count)[None, :] + 1.0
    rows = np.sin(math.pi * j * k / (count + 1))
    rows[0] = 0.0
    rows[-1] = 0.0
    return rows


def split(table):
    first = table.astype(jnp.bfloat16)
    return np.stack([first, (table - first.astype(np.float32)).astype(jnp.bfloat16)], axis=-3)


def times(value, pair):
    rows = value.shape[0]
    first = value.astype(jnp.bfloat16).astype(jnp.float32)
    both = jnp.concatenate([first, value - first], axis=0).astype(jnp.bfloat16)
    main = jnp.dot(both, pair[0], preferred_element_type=jnp.float32)
    rest = jnp.dot(both, pair[1], preferred_element_type=jnp.float32)
    return main[:rows] + main[rows:] + rest[:rows]


def sides_of(n_gy):
    return 0 if n_gy == 1 else 1 if n_gy == 2 else 2


def tables(shape, n_gx, n_gy, n_gz):
    nz, nx, ny = shape
    lz, lx, ly = (s // BLOCK for s in shape)
    fz, fx, fy = lz * n_gz, lx * n_gx, ly * n_gy
    cols = fz * fy
    wide = -(-cols // 128) * 128
    sz, sx, sy = sine_rows(fz), sine_rows(fx), sine_rows(fy)
    n_sides = sides_of(n_gy)
    lane = np.arange(ny)
    spread = np.zeros((n_gy, n_gz, wide, (lz + 2 + n_sides) * ny))
    gather = np.zeros((n_gy, n_gz, (2 * lz + 2) * ny, wide))
    for a in range(n_gy):
        yrow = np.floor_divide(np.arange(-1, ny + 1) + a * ny, BLOCK) + 1
        own, prev, after = sy[yrow[1:-1]], sy[yrow[:-2]], sy[yrow[2:]]
        ends = np.where((lane % BLOCK == 0)[:, None], prev - own, 0.0)
        ends = np.where((lane % BLOCK == BLOCK - 1)[:, None], after - own, ends)
        for b in range(n_gz):
            zrow = np.arange(-1, lz + 1) + b * lz + 1
            for i, row in enumerate(zrow):
                block = np.einsum("p,yq->pqy", sz[row], own).reshape(cols, -1)
                spread[a, b, :cols, i * ny : (i + 1) * ny] = block
                gather[a, b, i * ny : (i + 1) * ny, :cols] = block.T
                if 1 <= i <= lz:
                    at = (lz + 1 + i) * ny
                    block = np.einsum("p,yq->pqy", sz[row], ends).reshape(cols, -1)
                    gather[a, b, at : at + ny, :cols] = block.T
            count = (nz // 2 + DEPTH) * GROUP
            zi, c = np.arange(count) // GROUP, np.arange(count) % GROUP
            fine = np.floor_divide(2 * zi - DEPTH + b * nz, BLOCK) + 1
            for side in range(n_sides):
                high = a == 0 if n_sides == 1 else side == 1
                base = ny - 1 if high else -DEPTH - 1
                column = np.floor_divide(base + c + a * ny, BLOCK) + 1
                block = np.einsum("lp,lq->pql", sz[fine], sy[column]).reshape(cols, -1)
                at = (lz + 2 + side) * ny
                spread[a, b, :cols, at : at + count] = block
    rows = nx + 2 * PAD
    expand = np.zeros((n_gx, rows, fx))
    shrink = np.zeros((n_gx, 2, fx, nx))
    for a in range(n_gx):
        xs = np.arange(-DEPTH, nx + DEPTH) + a * nx
        expand[a, PAD - DEPTH : PAD + nx + DEPTH] = sx[np.floor_divide(xs, BLOCK) + 1]
        block = np.arange(nx) // BLOCK + a * lx + 1
        shrink[a, 0] = sx[block].T
        step = np.where(np.arange(nx) % BLOCK == 0, -1, 0) + np.where(np.arange(nx) % BLOCK == BLOCK - 1, 1, 0)
        shrink[a, 1] = (sx[block + step] - sx[block]).T
    lam = lambda n: 2.0 - 2.0 * np.cos(math.pi * (np.arange(n) + 1.0) / (n + 1))
    total = lam(fx)[:, None] + (lam(fz)[:, None] + lam(fy)[None, :]).reshape(1, -1)
    scale = np.zeros((fx, wide))
    scale[:, :cols] = BLOCK * BLOCK * 8.0 / ((fz + 1) * (fx + 1) * (fy + 1)) / total / BLOCK**3
    spread, gather, expand, shrink, scale = (t.astype(np.float32) for t in (spread, gather, expand, shrink, scale))
    return split(spread), split(gather), expand, shrink, scale


def kernel(
    sizes, shape, heat_hbm, mat_hbm, table_hbm, spread_hbm, gather_hbm, expand_hbm, shrink_hbm, scale_hbm,
    out, heat, mat, zheat, zmat, table, kh, sh, ps, pe, re, oc, xs, xr, xs2, xr2, xsb, xrb, red, black, post, sred, sblack, spost, psb, wd, hd, dg, leak,
    swd, shd, hsum, vsum, corr, spread, gather, expand, shrink, scale, got,
    in_sem, z_send, z_recv, a_send, a_recv, e_send, e_recv, b_send, b_recv, gsend, grecv, relays,
):
    n_gx, n_gy, n_gz = sizes
    nz, nx, ny = shape
    lz = nz // BLOCK
    pairs = nz // 2
    halo = DEPTH // 2
    full = nx + 2 * DEPTH
    gx, gy, gz = lax.axis_index("gx"), lax.axis_index("gy"), lax.axis_index("gz")
    count = n_gx * n_gy * n_gz
    me = (gx * n_gy + gy) * n_gz + gz
    zero = gx // n_gx
    rcp = functools.partial(pltpu.reciprocal, approx=True)

    few = count <= 32
    offsets = sorted(
        ((a, b, c) for a in range(n_gx) for b in range(n_gy) for c in range(n_gz) if a or b or c),
        key=lambda o: (-min(o[0], n_gx - o[0]), -min(o[1], n_gy - o[1]), -o[2]),
    )

    def turned(position, step, size):
        at = position + step
        return jnp.where(at >= size, at - size, at)

    def peer_of(step):
        if few:
            a, b, c = offsets[step - 1]
            at = turned(gx, a, n_gx), turned(gy, b, n_gy), turned(gz, c, n_gz)
            return (at[0] * n_gy + at[1]) * n_gz + at[2], dict(zip(("gx", "gy", "gz"), at))
        other = lax.rem(me + step, count)
        return other, {
            "gx": other // (n_gy * n_gz),
            "gy": lax.rem(other // n_gz, n_gy),
            "gz": lax.rem(other, n_gz),
        }

    def each_peer(action):
        if few:
            for step in range(1, count):
                action(step)
            return

        def one(step, carry):
            action(step)
            return carry

        lax.fori_loop(1, count, one, 0)

    inputs = [
        pltpu.make_async_copy(table_hbm, table, in_sem.at[5]),
        pltpu.make_async_copy(mat_hbm, mat, in_sem.at[6]),
        pltpu.make_async_copy(heat_hbm, heat, in_sem.at[7]),
    ]
    for copy in inputs:
        copy.start()
    barrier = pltpu.get_barrier_semaphore()

    def greet(step):
        _, where = peer_of(step)
        pl.semaphore_signal(barrier, inc=1, device_id=where, device_id_type=MESH)

    near = n_gx <= RELAYS + 1 and n_gy == 2
    friends = [(None, {"gz": 1 - gz}), (None, {"gy": 1 - gy})]
    for step in (-1, 1):
        beside_x = (gx > 0) if step < 0 else (gx < n_gx - 1)
        friends.append((beside_x, {"gx": gx + step}))
        friends.append((beside_x, {"gx": gx + step, "gy": 1 - gy}))
    n_friends = 2 + 2 * (jnp.where(gx > 0, 1, 0) + jnp.where(gx < n_gx - 1, 1, 0))

    def tell(sem):
        for exists, where in friends:
            def signal(where=where):
                pl.semaphore_signal(sem, inc=1, device_id=where, device_id_type=MESH)

            if exists is None:
                signal()
            else:
                pl.when(exists)(signal)

    def relay(step):
        if near:
            if step > 0:
                pl.semaphore_wait(relays.at[step - 1], n_friends)
            if step < RELAYS:
                tell(relays.at[step])

    if near:
        tell(barrier)
    else:
        each_peer(greet)

    fetch = [
        pltpu.make_async_copy(spread_hbm.at[gy, gz], spread, in_sem.at[0]),
        pltpu.make_async_copy(gather_hbm.at[gy, gz], gather, in_sem.at[1]),
        pltpu.make_async_copy(expand_hbm.at[gx], expand, in_sem.at[2]),
        pltpu.make_async_copy(shrink_hbm.at[gx], shrink, in_sem.at[3]),
        pltpu.make_async_copy(scale_hbm, scale, in_sem.at[4]),
    ]
    for copy in fetch:
        copy.start()

    if n_gy == 1:
        strips = []
    elif n_gy == 2:
        strips = [((ny - 1) * (1 - gy), (DEPTH + 1) * gy, 1 + (DEPTH - 1) * gy, (ny - DEPTH) * (1 - gy), None, 1 - gy, 0)]
    else:
        strips = [
            (0, DEPTH + 1, DEPTH, 0, gy > 0, gy - 1, 1),
            (ny - 1, 0, 1, ny - DEPTH, gy < n_gy - 1, gy + 1, 0),
        ]

    def guarded(exists, action):
        if exists is None:
            action()
        else:
            pl.when(exists)(action)

    def both(a, b):
        return b if a is None else a if b is None else jnp.logical_and(a, b)

    def lanes(n):
        return lax.broadcasted_iota(jnp.int32, (n, ny), 1)

    def sublanes(n):
        return lax.broadcasted_iota(jnp.int32, (n, ny), 0)

    lane = lanes(full)
    even = lax.rem(lane + sublanes(full), 2) == 0
    lane_own = lanes(nx)
    even_own = lax.rem(lane_own + sublanes(nx), 2) == 0
    row_x = sublanes(full) - DEPTH
    inside_row = jnp.logical_and(row_x + gx * nx >= 0, row_x + gx * nx < n_gx * nx)
    column = lax.rem(lane, GROUP)
    zgroup = lane // GROUP
    inner_group = jnp.where(jnp.logical_and(column >= 1, column <= DEPTH), zgroup, -1)
    first_z, last_z = halo * (1 - gz), pairs + halo + halo * (1 - gz)
    in_strip = jnp.logical_and(
        jnp.logical_and(inside_row, inner_group >= 0), jnp.logical_and(zgroup >= first_z, zgroup < last_z)
    )
    low_open, high_open = gy == 0, gy == n_gy - 1

    def open_lane(n):
        at = lanes(n)
        return jnp.logical_or(
            jnp.logical_and(at == 0, low_open), jnp.logical_and(at == ny - 1, high_open)
        )

    closed = {n: jnp.where(open_lane(n), 0.0, 1.0) for n in (full, nx)}

    def rows_of(n, shift=0):
        if n == nx and shift == 0:
            return pl.ds(PAD, nx)
        return pl.ds(zero + (PAD - (n - nx) // 2 + shift), n)

    def loop(count, step, carry, unroll=UNROLL):
        return lax.fori_loop(0, count, step, carry, unroll=unroll)

    def spin(value, amount):
        return pltpu.roll(value, lax.rem(amount + 4 * ny, ny), 1)

    inputs[0].wait()
    small = lax.broadcasted_iota(jnp.int32, (8, ny), 1)
    values = jnp.full((8, ny), table[0], jnp.float32)
    for m in range(1, table.shape[0]):
        values = jnp.where(small == m, table[m], values)
    resist = rcp(values)

    def look(ids):
        parts = [
            jnp.take_along_axis(resist, ids[8 * t : 8 * t + 8], axis=1) for t in range(nx // 8)
        ]
        return jnp.concatenate(parts, axis=0)

    x_open = jnp.logical_or(
        jnp.logical_and(sublanes(nx) == 0, gx == 0), jnp.logical_and(sublanes(nx) == nx - 1, gx == n_gx - 1)
    )
    faces_open = jnp.where(x_open, 1.0, 0.0) + jnp.where(open_lane(nx), 1.0, 0.0)

    def store_pair(slab, ids0, ids1, heat0, heat1):
        r0, r1 = look(ids0), look(ids1)
        values = (
            jnp.where(even_own, r1, r0),
            jnp.where(even_own, r0, r1),
            jnp.where(even_own, heat0, heat1),
            jnp.where(even_own, heat1, heat0),
        )
        for a, value in enumerate(values):
            kh[a, slab, pl.ds(PAD, nx), :] = value
        return values

    def gather_strip(value, z, col0, pack):
        n = value.shape[0]
        return jnp.where(inner_group[:n] == z, spin(value, z * GROUP + 1 - col0), pack)

    def own_pair(z, packs):
        values = store_pair(z + halo + 1, mat[2 * z], mat[2 * z + 1], heat[2 * z], heat[2 * z + 1])
        return tuple(
            tuple(gather_strip(value, z + halo, at[3], old) for value, old in zip(values, pack))
            for at, pack in zip(strips, packs)
        )

    inputs[1].wait()
    inputs[2].wait()
    ones, nothing = jnp.ones((nx, ny), jnp.float32), jnp.zeros((nx, ny), jnp.float32)
    packs = loop(pairs, own_pair, tuple((ones, ones, nothing, nothing) for _ in strips), 4)
    for side, pack in enumerate(packs):
        for a in range(4):
            ps[side, a, pl.ds(PAD, nx), :] = pack[a]

    def x_side(step):
        return (gx > 0) if step < 0 else (gx < n_gx - 1)

    def x_rows(step, n):
        if step > 0:
            return pl.ds(PAD + nx - n, n), pl.ds(PAD - n, n)
        return pl.ds(PAD, n), pl.ds(PAD + nx, n)

    def messages(x_parts, y_src, y_dst, send, recv, landing):
        at = 0

        def make(src, dst, exists, where):
            nonlocal at
            copy = pltpu.make_async_remote_copy(
                src_ref=src, dst_ref=dst, send_sem=send.at[at], recv_sem=recv.at[at], device_id=where, device_id_type=MESH
            )
            at += 1
            return exists, copy

        if n_gx > 1:
            for step in (1, -1):
                to = -step if landing else step
                src, dst = x_parts
                face = (1 - step) // 2
                yield make(src.at[face], dst.at[face], x_side(to), {"gx": gx + to})
        for side, (_, _, _, _, exists, there, other) in enumerate(strips):
            mine = side if not landing else side
            target = side if landing else other
            slot = at
            lanes_dst = y_dst.at[target]
            own = pl.ds(PAD, nx)
            yield exists, pltpu.make_async_remote_copy(
                src_ref=y_src.at[mine].at[(*y_lead(y_src), own)],
                dst_ref=lanes_dst.at[(*y_lead(y_src), own)],
                send_sem=send.at[slot],
                recv_sem=recv.at[y_slot(slot, side, other, landing)],
                device_id={"gy": there},
                device_id_type=MESH,
            )
            at += 1
            if n_gx > 1:
                for step in (1, -1):
                    to = -step if landing else step
                    src, dst = x_rows(step, DEPTH)
                    yield both(exists, x_side(to)), pltpu.make_async_remote_copy(
                        src_ref=y_src.at[mine].at[(*y_lead(y_src), src)],
                        dst_ref=lanes_dst.at[(*y_lead(y_src), dst)],
                        send_sem=send.at[at],
                        recv_sem=recv.at[y_slot(at, side, other, landing)],
                        device_id={"gx": gx + to, "gy": there},
                        device_id_type=MESH,
                    )
                    at += 1

    stride = 3 if n_gx > 1 else 1

    def y_lead(ref):
        return (slice(None),) if len(ref.shape) == 4 else ()

    def y_slot(at, side, other, landing):
        if len(strips) < 2 or landing:
            return at
        return at + (other - side) * stride

    fields_a = [(kh.at[a], n) for a, n in enumerate(X_ROWS)]
    fields_b = [(post, DEPTH)]

    def x_pack(buf, fields, first, many):
        def slab(i, carry):
            for face, step in enumerate((1, -1)):
                at = i * sum(n for _, n in fields)
                for ref, n in fields:
                    src, _ = x_rows(step, n)
                    buf[face, pl.ds(at, n), :] = ref[i + first, src, :]
                    at = at + n
            return carry

        if n_gx > 1:
            loop(many, slab, 0)

    def x_unpack(buf, fields, first, many):
        for face, step in enumerate((1, -1)):
            def slab(i, carry):
                at = i * sum(n for _, n in fields)
                for ref, n in fields:
                    _, dst = x_rows(step, n)
                    ref[i + first, dst, :] = buf[face, pl.ds(at, n), :]
                    at = at + n
                return carry

            def side(slab=slab):
                loop(many, slab, 0)

            if n_gx > 1:
                pl.when(x_side(-step))(side)

    def own_columns(value, z, packs):
        result = []
        n = value.shape[0]
        for (edge, own, _, _, _, _, _), pack in zip(strips, packs):
            to = z * GROUP + own
            result.append(jnp.where(lane[:n] == to, spin(value, to - edge), pack))
        return tuple(result)

    def own_mask(own):
        return jnp.logical_and(column == own, zgroup < pairs + 2 * halo)

    x_pack(xs, fields_a, halo + 1, pairs)
    a_args = ((xs, xr), ps, sh, a_send, a_recv)
    e_args = ((xs2, xr2), pe, re, e_send, e_recv)
    pl.semaphore_wait(barrier, n_friends if near else count - 1)

    z_edge = (nz - DEPTH) * (1 - gz)
    z_copies = [
        pltpu.make_async_remote_copy(
            src_ref=src.at[pl.ds(z_edge, DEPTH)],
            dst_ref=dst,
            send_sem=z_send.at[i],
            recv_sem=z_recv.at[i],
            device_id={"gz": 1 - gz},
            device_id_type=MESH,
        )
        for i, (src, dst) in enumerate(((mat, zmat), (heat, zheat)))
    ]
    for copy in z_copies:
        copy.start()
    for exists, copy in messages(*a_args, False):
        guarded(exists, copy.start)
    relay(0)
    for copy in z_copies:
        copy.wait_recv()
    beyond = 1 + (pairs + halo) * (1 - gz)
    packs = [nothing for _ in strips]
    for g in range(halo):
        values = store_pair(beyond + g, zmat[2 * g], zmat[2 * g + 1], zheat[2 * g], zheat[2 * g + 1])
        for side, at in enumerate(strips):
            for a in range(4):
                to = a * (ny // 4) + g * GROUP + 1
                here = jnp.logical_and(lane_own >= to, lane_own < to + DEPTH)
                packs[side] = jnp.where(here, spin(values[a], to - at[3]), packs[side])
    for side, pack in enumerate(packs):
        pe[side, pl.ds(PAD, nx), :] = pack
    x_pack(xs2, fields_a, beyond, halo)
    for exists, copy in messages(*e_args, False):
        guarded(exists, copy.start)

    blank = jnp.zeros((full, ny), jnp.float32)
    for field in (red, black, post):
        for slab in (0, 1 + (pairs + halo) * gz, 2 + (pairs + halo) * gz, pairs + 2 * halo + 1):
            field[slab] = jnp.zeros((nx + 2 * PAD, ny), jnp.float32)

        def clear(z, carry):
            field[z, pl.ds(0, PAD), :] = jnp.zeros((PAD, ny), jnp.float32)
            field[z, pl.ds(PAD + nx, PAD), :] = jnp.zeros((PAD, ny), jnp.float32)
            return carry

        loop(pairs + 2 * halo + 2, clear, 0)
    for side in range(len(strips)):
        for buf in (sred, sblack):
            buf[side] = jnp.zeros((nx + 2 * PAD, ny), jnp.float32)
        for row in (PAD - DEPTH - 1, PAD + nx + DEPTH):
            spost[side, pl.ds(row, 1), :] = jnp.zeros((1, ny), jnp.float32)

    def calm(slab, carry):
        for a in range(2):
            for row in (PAD - DEPTH - 1, PAD + nx + DEPTH):
                kh[a, slab, pl.ds(row, 1), :] = jnp.ones((1, ny), jnp.float32)
        return carry

    loop(pairs + 2 * halo + 2, calm, 0)
    for side in range(len(strips)):
        for a in range(2):
            for row in (PAD - DEPTH - 1, PAD + nx + DEPTH):
                sh[side, a, pl.ds(row, 1), :] = jnp.ones((1, ny), jnp.float32)

    def fill(start):
        def slab(z, carry):
            for a in range(4):
                kh[a, z, pl.ds(start, DEPTH), :] = jnp.full((DEPTH, ny), 1.0 if a < 2 else 0.0, jnp.float32)
            return carry

        loop(pairs + 2 * halo + 2, slab, 0)
        for side in range(len(strips)):
            for a in range(4):
                sh[side, a, pl.ds(start, DEPTH), :] = jnp.full((DEPTH, ny), 1.0 if a < 2 else 0.0, jnp.float32)

    pl.when(gx == 0)(lambda: fill(PAD - DEPTH))
    pl.when(gx == n_gx - 1)(lambda: fill(PAD + nx))
    for side, strip_of in enumerate(strips):
        if strip_of[4] is not None:
            def vacant(side=side):
                for a in range(4):
                    sh[side, a] = jnp.full((nx + 2 * PAD, ny), 1.0 if a < 2 else 0.0, jnp.float32)

            pl.when(jnp.logical_not(strip_of[4]))(vacant)

    def losses(z, carry):
        low = jnp.where(jnp.logical_and(z == 0, gz == 0), 1.0, 0.0)
        high = jnp.where(jnp.logical_and(z == pairs - 1, gz == n_gz - 1), 1.0, 0.0)
        faces = faces_open + jnp.where(even_own, low, high)
        leak[z] = faces * rcp(kh[1, z + halo + 1, pl.ds(PAD, nx), :])
        return carry

    loop(pairs, losses, 0, 4)
    for layer in range(lz):
        def add(z, total):
            return total + heat[layer * BLOCK + z]
        hsum[layer] = loop(BLOCK, add, jnp.zeros((nx, ny), jnp.float32), 4)

    def own_resist(rows):
        def step(z, packs):
            z = z + halo * (1 - gz)
            return tuple(own_columns(kh[a, z + 1, rows, :], z, packs[a]) for a in range(2))

        fresh = jnp.ones((rows.size, ny), jnp.float32)
        packs = loop(pairs + halo, step, (tuple(fresh for _ in strips),) * 2)
        for side in range(len(strips)):
            for a in range(2):
                oc[side, a, rows, :] = packs[a][side]

    own_resist(pl.ds(PAD, nx))

    relay(1)
    for args in (a_args, e_args):
        for exists, copy in messages(*args, True):
            guarded(exists, copy.wait_recv)
    x_unpack(xr, fields_a, halo + 1, pairs)
    x_unpack(xr2, fields_a, beyond, halo)
    own_resist(pl.ds(zero + (PAD - DEPTH), 8))
    own_resist(pl.ds(zero + (PAD + nx + DEPTH - 8), 8))
    wall, wall_own = halo + (pairs + 1) * gz, halo + 1 + (pairs - 1) * gz
    for a in range(2):
        kh[a, wall, rows_of(full), :] = kh[1 - a, wall_own, rows_of(full), :]
    x_first = beyond - 1
    came = jnp.logical_and(zgroup >= x_first, zgroup < x_first + halo)
    for side, at in enumerate(strips):
        extra = re[side, rows_of(full), :]
        whole = []
        for a in range(4):
            value = jnp.where(came, spin(extra, x_first * GROUP - a * (ny // 4)), sh[side, a, rows_of(full), :])
            if a < 2:
                value = jnp.where(own_mask(at[1]), oc[side, a, rows_of(full), :], value)
            whole.append(value)
        for a in range(4):
            value = whole[a]
            if a < 2:
                value = jnp.where(zgroup == wall - 1, spin(whole[1 - a], GROUP * (2 * gz - 1)), value)
            sh[side, a, rows_of(full), :] = value

    def mirror(outer, inner):
        def slab(z, carry):
            for a in range(2):
                kh[a, z + 1, outer, :] = kh[1 - a, z + 1, inner, :]
            return carry

        loop(pairs + 2 * halo, slab, 0)
        for side in range(len(strips)):
            for a in range(2):
                sh[side, a, outer, :] = sh[side, 1 - a, inner, :]

    pl.when(gx == 0)(lambda: mirror(pl.ds(PAD - 1, 1), pl.ds(PAD, 1)))
    pl.when(gx == n_gx - 1)(lambda: mirror(pl.ds(PAD + nx, 1), pl.ds(PAD + nx - 1, 1)))

    wide, inner = [(True, t) for t in range(full // 8)], [(False, t) for t in range(nx // 8)]
    even8, lane8, column_step = even_own[:8], lane_own[:8], lax.rem(lane_own[:8], BLOCK) == 0
    open8 = open_lane(8)
    closed8 = jnp.where(open8, 0.0, 1.0)

    def at(tile, shift=0):
        deep, t = tile
        if not deep and shift == 0:
            return pl.ds(PAD + 8 * t, 8)
        return pl.ds(zero + (PAD - (DEPTH if deep else 0) + 8 * t + shift), 8)

    def cut(tile):
        deep, t = tile
        return pl.ds(8 * t, 8) if deep else pl.ds(zero + (DEPTH + 8 * t), 8)

    def halos_of(refs, tiles):
        return [[ref[at(tile), :] for ref in refs] for tile in tiles]

    def beside(value, halos, z, walls):
        low, high = pltpu.roll(value, 1, 1), pltpu.roll(value, ny - 1, 1)
        ends = [
            spin(near_by, edge - (z * GROUP + adj))
            for near_by, (edge, _, adj, _, _, _, _) in zip(halos, strips)
        ]
        ends = ends or [value]
        if walls is None:
            ends = [end * closed8 for end in ends]
        else:
            ends = [jnp.where(open8, walls, end) for end in ends]
        return jnp.where(lane8 == 0, ends[0], low), jnp.where(lane8 == ny - 1, ends[-1], high)

    def around(field, color, z, tile, halos, walls=None):
        here = z + 1
        same = field[here, at(tile), :]
        before, after = field[here - 1, at(tile), :], field[here + 1, at(tile), :]
        low, high = beside(same, halos, z, walls)
        return (
            same,
            jnp.where(even8, before, after) if color == 0 else jnp.where(even8, after, before),
            field[here, at(tile, -1), :],
            field[here, at(tile, 1), :],
            low,
            high,
        )

    def tile_packs(values, z, packs):
        return tuple(own_columns(value, z, pack) for value, pack in zip(values, packs))

    blank8 = jnp.zeros((8, ny), jnp.float32)
    no_packs = tuple(tuple(blank8 for _ in strips) for _ in wide)

    def joined(packs, side):
        return jnp.concatenate([pack[side] for pack in packs], axis=0)

    def strip_around(ref, color):
        same = ref[rows_of(full), :]
        before, after = pltpu.roll(same, GROUP, 1), pltpu.roll(same, ny - GROUP, 1)
        return (
            same,
            jnp.where(even, after, before) if color == 0 else jnp.where(even, before, after),
            ref[rows_of(full, -1), :],
            ref[rows_of(full, 1), :],
            pltpu.roll(same, 1, 1),
            pltpu.roll(same, ny - 1, 1),
        )

    def shares(center, others):
        parts = [rcp(center + other) for other in others]
        total = parts[0]
        for part in parts[1:]:
            total = total + part
        return parts, total

    def strip_weigh(color):
        for side in range(len(strips)):
            a = 1 - color
            center = sh[side, a, rows_of(full), :]
            parts, total = shares(center, strip_around(sh.at[side, 1 - a], color))
            inverse = jnp.where(in_strip, rcp(total), 0.0)
            if strips[side][4] is not None:
                inverse = jnp.where(strips[side][4], inverse, 0.0)
            for face in range(6):
                swd[side, color, face] = parts[face] * inverse
            shd[side, color] = sh[side, 2 + color, rows_of(full), :] * (0.5 * inverse)

    def weigh(color):
        a = 1 - color
        halos = halos_of([sh.at[side, 1 - a] for side in range(len(strips))], wide)

        def step(i, packs):
            z = i + halo * (1 - gz)
            ratios = []
            for tile in wide:
                t = tile[1]
                center = kh[a, z + 1, at(tile), :]
                parts, total = shares(center, around(kh.at[1 - a], color, z, tile, halos[t], center))
                inverse = rcp(total)
                if t in (0, len(wide) - 1):
                    inverse = jnp.where(inside_row[8 * t : 8 * t + 8], inverse, 0.0)
                for face in range(6):
                    wd[color, face, z, cut(tile), :] = parts[face] * inverse
                ratio = kh[2 + color, z + 1, at(tile), :] * (0.5 * inverse)
                hd[color, z, cut(tile), :] = ratio
                if color == 1:
                    dg[z, cut(tile), :] = total * 2.0
                else:
                    red[z + 1, at(tile), :] = ratio
                    ratios.append(ratio)
            return packs if color == 1 else tile_packs(ratios, z, packs)

        return loop(pairs + halo, step, no_packs, WEIGH_UNROLL)

    for color in range(2):
        strip_weigh(color)
    packs = weigh(0)
    for side, (_, own, _, _, _, _, _) in enumerate(strips):
        sred[side, rows_of(full), :] = jnp.where(own_mask(own), joined(packs, side), shd[side, 0])
    relay(2)
    weigh(1)

    def weights_of(color, z, tile):
        return hd[color, z, cut(tile), :], [wd[color, face, z, cut(tile), :] for face in range(6)]

    def total_of(source, weights, others):
        result = source
        for weight, other in zip(weights, others):
            result = result + weight * other
        return result

    def stage(color, src, strip_src, dst, strip_dst, reach):
        halos = halos_of([strip_src.at[side] for side in range(len(strips))], wide)

        def step(i, packs):
            first = i + halo - reach * gz
            values = []
            for z in [first + k for k in range(pairs + reach)]:
                values.append([])
                for tile in wide:
                    source, weights = weights_of(color, z, tile)
                    values[-1].append(total_of(source, weights, around(src, color, z, tile, halos[tile[1]])))
            for k, row in enumerate(values):
                for tile, value in zip(wide, row):
                    dst[first + k + 1, at(tile), :] = value
            for k, row in enumerate(values):
                packs = tile_packs(row, first + k, packs)
            return packs

        packs = step(0, no_packs)
        for side, (_, own, _, _, _, _, _) in enumerate(strips):
            value = total_of(
                shd[side, color],
                [swd[side, color, face] for face in range(6)],
                strip_around(strip_src.at[side], color),
            )
            strip_dst[side, rows_of(full), :] = jnp.where(own_mask(own), joined(packs, side), value)

    stage(1, red, sred, black, sblack, 2)
    stage(0, black, sblack, red, sred, 2)

    halos = halos_of([sred.at[side] for side in range(len(strips))], inner)
    tiles = BLOCK // 8
    none = jnp.zeros((nx, ny), jnp.float32)
    sums = []
    for layer in range(lz):
        def flow(i, carry):
            z = i + layer * (BLOCK // 2) + halo
            result = []
            for tile, (own_sum, x_sum, y_sum) in zip(inner, carry):
                t = tile[1]
                source, weights = weights_of(1, z, tile)
                others = around(red, 1, z, tile, halos[t])
                value = total_of(source, weights, others)
                post[z + 1, at(tile), :] = value
                spare = dg[z, cut(tile), :]
                face = 2 if t % tiles == 0 else 3
                own_sum = own_sum + leak[z - halo, pl.ds(8 * t, 8), :] * others[0]
                if t % tiles in (0, tiles - 1):
                    x_sum = x_sum + spare * ((value - others[face]) * weights[face])
                aside, weight = (
                    jnp.where(column_step, pair[0], pair[1]) for pair in (others[4:], weights[4:])
                )
                y_sum = y_sum + spare * ((value - aside) * weight)
                result.append((own_sum, x_sum, y_sum))
            return tuple(result)

        parts = loop(BLOCK // 2, flow, tuple((blank8,) * 3 for _ in inner), FLOW_UNROLL)
        sums.append(tuple(jnp.concatenate([part[i] for part in parts], axis=0) for i in range(3)))

    z_from, z_to = halo + 1 + (pairs - halo) * (1 - gz), 1 + (pairs + halo) * gz
    z_back = 1 + (pairs + halo) * (1 - gz)
    own = pl.ds(PAD, nx)
    z_copy = [
        pltpu.make_async_remote_copy(
            src_ref=post.at[pl.ds(z_from, halo), own],
            dst_ref=post.at[pl.ds(to, halo), own],
            send_sem=z_send.at[2],
            recv_sem=z_recv.at[2],
            device_id={"gz": 1 - gz},
            device_id_type=MESH,
        )
        for to in (z_to, z_back)
    ]
    z_copy[0].start()

    totals = [none, *(hsum[layer] - sums[layer][0] for layer in range(lz)), none]
    for layer in range(lz):
        for late in range(2):
            z = halo + layer * (BLOCK // 2) + (BLOCK // 2 - 1) * late
            beyond_z = red[z + 2, own, :] if late else red[z, own, :]
            deep_rows = pl.ds(zero + DEPTH, nx)
            flux = dg[z, deep_rows, :] * wd[1, 1, z, deep_rows, :] * (post[z + 1, own, :] - beyond_z)
            flux = jnp.where(even_own, flux, 0.0) if late else jnp.where(even_own, 0.0, flux)
            totals[layer + 1] = totals[layer + 1] - flux
            to = layer + 2 if late else layer
            totals[to] = totals[to] + flux
    for i, value in enumerate((*totals, *(s[2] for s in sums))):
        vsum[:, i * ny : (i + 1) * ny] = value
    for copy in fetch:
        copy.wait()
    part = jnp.dot(shrink[0], vsum[...], precision=HIGH, preferred_element_type=jnp.float32)
    for layer in range(lz):
        vsum[:, layer * ny : (layer + 1) * ny] = sums[layer][1]
    bent = jnp.dot(shrink[1], vsum[:, : lz * ny], precision=HIGH, preferred_element_type=jnp.float32)
    turned_part = [part[:, i * ny : (i + 1) * ny] for i in range(2 * lz + 2)]
    for layer in range(lz):
        turned_part[layer + 1] = turned_part[layer + 1] + bent[:, layer * ny : (layer + 1) * ny]
    part = times(jnp.concatenate(turned_part, axis=1), (gather[0], gather[1]))
    got[me] = part

    def gathering(step, start):
        other, where = peer_of(step)
        copy = pltpu.make_async_remote_copy(
            src_ref=got.at[me],
            dst_ref=got.at[me if start else other],
            send_sem=gsend.at[step],
            recv_sem=grecv.at[me if start else other],
            device_id=where,
            device_id_type=MESH,
        )
        return copy

    relay(3)
    each_peer(lambda step: gathering(step, True).start())

    z_copy[1].wait_recv()

    def pack_post(z, packs):
        z = z + halo * (1 - gz)
        value = post[z + 1, own, :]
        return tuple(gather_strip(value, z, s[3], pack) for s, pack in zip(strips, packs))

    packs = loop(pairs + halo, pack_post, tuple(none for _ in strips))
    for side, pack in enumerate(packs):
        psb[side, own, :] = pack
    x_pack(xsb, fields_b, 1 + halo * (1 - gz), pairs + halo)
    b_args = ((xsb, xrb), psb, spost, b_send, b_recv)
    for exists, copy in messages(*b_args, False):
        guarded(exists, copy.start)

    each_peer(lambda step: gathering(step, False).wait_recv())
    if count <= 32:
        hat = got[0]
        for i in range(1, count):
            hat = hat + got[i]
    else:
        hat = lax.fori_loop(1, count, lambda i, acc: acc + got[i], got[0])
    kbar = table[0]
    for m in range(1, table.shape[0]):
        kbar = kbar + table[m]
    kbar = kbar / table.shape[0]
    hat = hat * scale[...] / kbar
    hat = times(hat, (spread[0], spread[1]))
    rise = jnp.dot(expand[...], hat, precision=HIGH, preferred_element_type=jnp.float32)
    for i in range(corr.shape[0]):
        corr[i] = rise[:, i * ny : (i + 1) * ny]

    z_copy[0].wait_send()
    for exists, copy in messages(*b_args, False):
        guarded(exists, copy.wait_send)
    for exists, copy in messages(*b_args, True):
        guarded(exists, copy.wait_recv)
    x_unpack(xrb, fields_b, 1 + halo * (1 - gz), pairs + halo)

    def correct(i, packs):
        z = i + halo * (1 - gz)
        layer = (z + BLOCK // 2 - halo) // (BLOCK // 2)
        value = post[z + 1, rows_of(full), :]
        value = value + corr[layer, rows_of(full), :]
        post[z + 1, rows_of(full), :] = value
        return own_columns(value, z, packs)

    packs = loop(pairs + halo, correct, tuple(blank for _ in strips))
    for side, (_, own_c, _, _, exists, _, _) in enumerate(strips):
        value = spost[side, rows_of(full), :] + corr[lz + 2 + side, rows_of(full), :]
        value = jnp.where(in_strip, value, 0.0)
        if exists is not None:
            value = jnp.where(exists, value, 0.0)
        spost[side, rows_of(full), :] = jnp.where(own_mask(own_c), packs[side], value)

    stage(0, post, spost, red, sred, 2)
    stage(1, red, sred, black, sblack, 2)
    stage(0, black, sblack, red, sred, 2)

    halos = halos_of([sred.at[side] for side in range(len(strips))], inner)

    def finish(i, carry):
        z = i + halo
        for tile in inner:
            source, weights = weights_of(1, z, tile)
            others = around(red, 1, z, tile, halos[tile[1]])
            last = total_of(source, weights, others)
            rows = pl.ds(8 * tile[1], 8)
            out[2 * i, rows, :] = jnp.where(even8, others[0], last)
            out[2 * i + 1, rows, :] = jnp.where(even8, last, others[0])
        return carry

    loop(pairs, finish, 0, FINISH_UNROLL)

    for copy in z_copies:
        copy.wait_send()
    for args in (a_args, e_args):
        for exists, copy in messages(*args, False):
            guarded(exists, copy.wait_send)
    each_peer(lambda step: gathering(step, True).wait_send())


def per_device(sizes, heat, material, table):
    shape = heat.shape
    nz, nx, ny = shape
    n_gx, n_gy, n_gz = sizes
    assert n_gz == 2
    consts = tables(shape, *sizes)
    spread, gather, expand, shrink, scale = consts
    count = n_gx * n_gy * n_gz
    rows = nx + 2 * PAD
    full = nx + 2 * DEPTH
    sides = max(sides_of(n_gy), 1)
    pairs = nz // 2
    lz = nz // BLOCK
    deep = pairs + DEPTH
    f32 = jnp.float32
    vmem = pl.BlockSpec(memory_space=pltpu.VMEM)
    hbm = pl.BlockSpec(memory_space=pltpu.HBM)
    field = pltpu.VMEM((deep + 2, rows, ny), f32)
    strip = pltpu.VMEM((sides, rows, ny), f32)
    sems = pltpu.SemaphoreType.DMA
    return pl.pallas_call(
        functools.partial(kernel, sizes, shape),
        out_shape=pltpu.VMEM(shape, f32),
        in_specs=[hbm] * 8,
        out_specs=vmem,
        scratch_shapes=[
            pltpu.VMEM(shape, f32),
            pltpu.VMEM(shape, jnp.int32),
            pltpu.VMEM((DEPTH, nx, ny), f32),
            pltpu.VMEM((DEPTH, nx, ny), jnp.int32),
            pltpu.SMEM(table.shape, f32),
            pltpu.VMEM((4, deep + 2, rows, ny), f32),
            pltpu.VMEM((sides, 4, rows, ny), f32),
            pltpu.VMEM((sides, 4, rows, ny), f32),
            strip, strip,
            pltpu.VMEM((sides, 2, rows, ny), f32),
            *[pltpu.VMEM((2, pairs * sum(X_ROWS), ny), f32)] * 2,
            *[pltpu.VMEM((2, DEPTH // 2 * sum(X_ROWS), ny), f32)] * 2,
            *[pltpu.VMEM((2, (deep - DEPTH // 2) * DEPTH, ny), f32)] * 2,
            field, field, field,
            strip, strip, strip, strip,
            pltpu.VMEM((2, 6, deep, full, ny), f32),
            pltpu.VMEM((2, deep, full, ny), f32),
            pltpu.VMEM((deep, full, ny), f32),
            pltpu.VMEM((pairs, nx, ny), f32),
            pltpu.VMEM((sides, 2, 6, full, ny), f32),
            pltpu.VMEM((sides, 2, full, ny), f32),
            pltpu.VMEM((lz, nx, ny), f32),
            pltpu.VMEM((nx, gather.shape[3]), f32),
            pltpu.VMEM((spread.shape[4] // ny, rows, ny), f32),
            pltpu.VMEM(spread.shape[2:], jnp.bfloat16),
            pltpu.VMEM(gather.shape[2:], jnp.bfloat16),
            pltpu.VMEM(expand.shape[1:], f32),
            pltpu.VMEM(shrink.shape[1:], f32),
            pltpu.VMEM(scale.shape, f32),
            pltpu.VMEM((count, *scale.shape), f32),
            sems((8,)),
            sems((3,)),
            sems((3,)),
            sems((8,)),
            sems((8,)),
            sems((8,)),
            sems((8,)),
            sems((8,)),
            sems((8,)),
            sems((count,)),
            sems((count,)),
            pltpu.SemaphoreType.REGULAR((RELAYS,)),
        ],
        compiler_params=pltpu.CompilerParams(
            collective_id=0, has_side_effects=True, vmem_limit_bytes=64 * 1024 * 1024 - 3 * nz * nx * ny * 2
        ),
    )(heat, material, table, *(jnp.asarray(c) for c in consts))


def solution(mesh):
    sizes = (mesh.shape["gx"], mesh.shape["gy"], mesh.shape["gz"])
    spec = P("gz", ("groups", "gx"), "gy")
    return jax.shard_map(
        functools.partial(per_device, sizes),
        mesh=mesh,
        in_specs=(spec, spec, P()),
        out_specs=spec,
        check_vma=False,
    )
```

```python
import functools
import math

import jax
import jax.numpy as jnp
import numpy as np
from jax import lax
from jax.experimental import pallas as pl
from jax.experimental.pallas import tpu as pltpu
from jax.sharding import PartitionSpec as P

BLOCK = 16
PAD = 8
DEPTH = 4
GROUP = DEPTH + 2
X_ROWS = (DEPTH, DEPTH - 1, DEPTH - 1, DEPTH - 2)
MESH = pl.DeviceIdType.MESH
HIGH = lax.Precision.HIGHEST
UNROLL = 18
RELAYS = 3
WEIGH_UNROLL = 9
FLOW_UNROLL = 8
FINISH_UNROLL = 16


def sine_rows(count):
    j = np.arange(-1, count + 1)[:, None] + 1.0
    k = np.arange(count)[None, :] + 1.0
    rows = np.sin(math.pi * j * k / (count + 1))
    rows[0] = 0.0
    rows[-1] = 0.0
    return rows


def split(table):
    first = table.astype(jnp.bfloat16)
    return np.stack([first, (table - first.astype(np.float32)).astype(jnp.bfloat16)], axis=-3)


def times(value, pair):
    rows = value.shape[0]
    first = value.astype(jnp.bfloat16).astype(jnp.float32)
    both = jnp.concatenate([first, value - first], axis=0).astype(jnp.bfloat16)
    main = jnp.dot(both, pair[0], preferred_element_type=jnp.float32)
    rest = jnp.dot(both, pair[1], preferred_element_type=jnp.float32)
    return main[:rows] + main[rows:] + rest[:rows]


def sides_of(n_gy):
    return 0 if n_gy == 1 else 1 if n_gy == 2 else 2


def tables(shape, n_gx, n_gy, n_gz):
    nz, nx, ny = shape
    lz, lx, ly = (s // BLOCK for s in shape)
    fz, fx, fy = lz * n_gz, lx * n_gx, ly * n_gy
    cols = fz * fy
    wide = -(-cols // 128) * 128
    sz, sx, sy = sine_rows(fz), sine_rows(fx), sine_rows(fy)
    n_sides = sides_of(n_gy)
    lane = np.arange(ny)
    spread = np.zeros((n_gy, n_gz, wide, (lz + 2 + n_sides) * ny))
    gather = np.zeros((n_gy, n_gz, (2 * lz + 2) * ny, wide))
    for a in range(n_gy):
        yrow = np.floor_divide(np.arange(-1, ny + 1) + a * ny, BLOCK) + 1
        own, prev, after = sy[yrow[1:-1]], sy[yrow[:-2]], sy[yrow[2:]]
        ends = np.where((lane % BLOCK == 0)[:, None], prev - own, 0.0)
        ends = np.where((lane % BLOCK == BLOCK - 1)[:, None], after - own, ends)
        for b in range(n_gz):
            zrow = np.arange(-1, lz + 1) + b * lz + 1
            for i, row in enumerate(zrow):
                block = np.einsum("p,yq->pqy", sz[row], own).reshape(cols, -1)
                spread[a, b, :cols, i * ny : (i + 1) * ny] = block
                gather[a, b, i * ny : (i + 1) * ny, :cols] = block.T
                if 1 <= i <= lz:
                    at = (lz + 1 + i) * ny
                    block = np.einsum("p,yq->pqy", sz[row], ends).reshape(cols, -1)
                    gather[a, b, at : at + ny, :cols] = block.T
            count = (nz // 2 + DEPTH) * GROUP
            zi, c = np.arange(count) // GROUP, np.arange(count) % GROUP
            fine = np.floor_divide(2 * zi - DEPTH + b * nz, BLOCK) + 1
            for side in range(n_sides):
                high = a == 0 if n_sides == 1 else side == 1
                base = ny - 1 if high else -DEPTH - 1
                column = np.floor_divide(base + c + a * ny, BLOCK) + 1
                block = np.einsum("lp,lq->pql", sz[fine], sy[column]).reshape(cols, -1)
                at = (lz + 2 + side) * ny
                spread[a, b, :cols, at : at + count] = block
    rows = nx + 2 * PAD
    expand = np.zeros((n_gx, rows, fx))
    shrink = np.zeros((n_gx, 2, fx, nx))
    for a in range(n_gx):
        xs = np.arange(-DEPTH, nx + DEPTH) + a * nx
        expand[a, PAD - DEPTH : PAD + nx + DEPTH] = sx[np.floor_divide(xs, BLOCK) + 1]
        block = np.arange(nx) // BLOCK + a * lx + 1
        shrink[a, 0] = sx[block].T
        step = np.where(np.arange(nx) % BLOCK == 0, -1, 0) + np.where(np.arange(nx) % BLOCK == BLOCK - 1, 1, 0)
        shrink[a, 1] = (sx[block + step] - sx[block]).T
    lam = lambda n: 2.0 - 2.0 * np.cos(math.pi * (np.arange(n) + 1.0) / (n + 1))
    total = lam(fx)[:, None] + (lam(fz)[:, None] + lam(fy)[None, :]).reshape(1, -1)
    scale = np.zeros((fx, wide))
    scale[:, :cols] = BLOCK * BLOCK * 8.0 / ((fz + 1) * (fx + 1) * (fy + 1)) / total / BLOCK**3
    spread, gather, expand, shrink, scale = (t.astype(np.float32) for t in (spread, gather, expand, shrink, scale))
    return split(spread), split(gather), expand, shrink, scale


def kernel(
    sizes, shape, heat_hbm, mat_hbm, table_hbm, spread_hbm, gather_hbm, expand_hbm, shrink_hbm, scale_hbm,
    out, heat, mat, zheat, zmat, table, kh, sh, ps, pe, re, oc, xs, xr, xs2, xr2, xsb, xrb, red, black, post, sred, sblack, spost, psb, wd, hd, dg, leak,
    swd, shd, hsum, vsum, corr, spread, gather, expand, shrink, scale, got,
    in_sem, z_send, z_recv, a_send, a_recv, e_send, e_recv, b_send, b_recv, gsend, grecv, relays,
):
    n_gx, n_gy, n_gz = sizes
    nz, nx, ny = shape
    lz = nz // BLOCK
    pairs = nz // 2
    halo = DEPTH // 2
    full = nx + 2 * DEPTH
    gx, gy, gz = lax.axis_index("gx"), lax.axis_index("gy"), lax.axis_index("gz")
    count = n_gx * n_gy * n_gz
    me = (gx * n_gy + gy) * n_gz + gz
    zero = gx // n_gx
    rcp = functools.partial(pltpu.reciprocal, approx=True)

    few = count <= 32
    offsets = sorted(
        ((a, b, c) for a in range(n_gx) for b in range(n_gy) for c in range(n_gz) if a or b or c),
        key=lambda o: (-min(o[0], n_gx - o[0]), -min(o[1], n_gy - o[1]), -o[2]),
    )

    def turned(position, step, size):
        at = position + step
        return jnp.where(at >= size, at - size, at)

    def peer_of(step):
        if few:
            a, b, c = offsets[step - 1]
            at = turned(gx, a, n_gx), turned(gy, b, n_gy), turned(gz, c, n_gz)
            return (at[0] * n_gy + at[1]) * n_gz + at[2], dict(zip(("gx", "gy", "gz"), at))
        other = lax.rem(me + step, count)
        return other, {
            "gx": other // (n_gy * n_gz),
            "gy": lax.rem(other // n_gz, n_gy),
            "gz": lax.rem(other, n_gz),
        }

    def each_peer(action):
        if few:
            for step in range(1, count):
                action(step)
            return

        def one(step, carry):
            action(step)
            return carry

        lax.fori_loop(1, count, one, 0)

    inputs = [
        pltpu.make_async_copy(table_hbm, table, in_sem.at[5]),
        pltpu.make_async_copy(mat_hbm, mat, in_sem.at[6]),
        pltpu.make_async_copy(heat_hbm, heat, in_sem.at[7]),
    ]
    for copy in inputs:
        copy.start()
    barrier = pltpu.get_barrier_semaphore()

    def greet(step):
        _, where = peer_of(step)
        pl.semaphore_signal(barrier, inc=1, device_id=where, device_id_type=MESH)

    near = n_gx <= RELAYS + 1 and n_gy == 2
    friends = [(None, {"gz": 1 - gz}), (None, {"gy": 1 - gy})]
    for step in (-1, 1):
        beside_x = (gx > 0) if step < 0 else (gx < n_gx - 1)
        friends.append((beside_x, {"gx": gx + step}))
        friends.append((beside_x, {"gx": gx + step, "gy": 1 - gy}))
    n_friends = 2 + 2 * (jnp.where(gx > 0, 1, 0) + jnp.where(gx < n_gx - 1, 1, 0))

    def tell(sem):
        for exists, where in friends:
            def signal(where=where):
                pl.semaphore_signal(sem, inc=1, device_id=where, device_id_type=MESH)

            if exists is None:
                signal()
            else:
                pl.when(exists)(signal)

    def relay(step):
        if near:
            if step > 0:
                pl.semaphore_wait(relays.at[step - 1], n_friends)
            if step < RELAYS:
                tell(relays.at[step])

    if near:
        tell(barrier)
    else:
        each_peer(greet)

    fetch = [
        pltpu.make_async_copy(spread_hbm.at[gy, gz], spread, in_sem.at[0]),
        pltpu.make_async_copy(gather_hbm.at[gy, gz], gather, in_sem.at[1]),
        pltpu.make_async_copy(expand_hbm.at[gx], expand, in_sem.at[2]),
        pltpu.make_async_copy(shrink_hbm.at[gx], shrink, in_sem.at[3]),
        pltpu.make_async_copy(scale_hbm, scale, in_sem.at[4]),
    ]
    for copy in fetch:
        copy.start()

    if n_gy == 1:
        strips = []
    elif n_gy == 2:
        strips = [((ny - 1) * (1 - gy), (DEPTH + 1) * gy, 1 + (DEPTH - 1) * gy, (ny - DEPTH) * (1 - gy), None, 1 - gy, 0)]
    else:
        strips = [
            (0, DEPTH + 1, DEPTH, 0, gy > 0, gy - 1, 1),
            (ny - 1, 0, 1, ny - DEPTH, gy < n_gy - 1, gy + 1, 0),
        ]

    def guarded(exists, action):
        if exists is None:
            action()
        else:
            pl.when(exists)(action)

    def both(a, b):
        return b if a is None else a if b is None else jnp.logical_and(a, b)

    def lanes(n):
        return lax.broadcasted_iota(jnp.int32, (n, ny), 1)

    def sublanes(n):
        return lax.broadcasted_iota(jnp.int32, (n, ny), 0)

    lane = lanes(full)
    even = lax.rem(lane + sublanes(full), 2) == 0
    lane_own = lanes(nx)
    even_own = lax.rem(lane_own + sublanes(nx), 2) == 0
    row_x = sublanes(full) - DEPTH
    inside_row = jnp.logical_and(row_x + gx * nx >= 0, row_x + gx * nx < n_gx * nx)
    column = lax.rem(lane, GROUP)
    zgroup = lane // GROUP
    inner_group = jnp.where(jnp.logical_and(column >= 1, column <= DEPTH), zgroup, -1)
    first_z, last_z = halo * (1 - gz), pairs + halo + halo * (1 - gz)
    in_strip = jnp.logical_and(
        jnp.logical_and(inside_row, inner_group >= 0), jnp.logical_and(zgroup >= first_z, zgroup < last_z)
    )
    low_open, high_open = gy == 0, gy == n_gy - 1

    def open_lane(n):
        at = lanes(n)
        return jnp.logical_or(
            jnp.logical_and(at == 0, low_open), jnp.logical_and(at == ny - 1, high_open)
        )

    closed = {n: jnp.where(open_lane(n), 0.0, 1.0) for n in (full, nx)}

    def rows_of(n, shift=0):
        if n == nx and shift == 0:
            return pl.ds(PAD, nx)
        return pl.ds(zero + (PAD - (n - nx) // 2 + shift), n)

    def loop(count, step, carry, unroll=UNROLL):
        return lax.fori_loop(0, count, step, carry, unroll=unroll)

    def spin(value, amount):
        return pltpu.roll(value, lax.rem(amount + 4 * ny, ny), 1)

    inputs[0].wait()
    small = lax.broadcasted_iota(jnp.int32, (8, ny), 1)
    values = jnp.full((8, ny), table[0], jnp.float32)
    for m in range(1, table.shape[0]):
        values = jnp.where(small == m, table[m], values)
    resist = rcp(values)

    def look(ids):
        parts = [
            jnp.take_along_axis(resist, ids[8 * t : 8 * t + 8], axis=1) for t in range(nx // 8)
        ]
        return jnp.concatenate(parts, axis=0)

    x_open = jnp.logical_or(
        jnp.logical_and(sublanes(nx) == 0, gx == 0), jnp.logical_and(sublanes(nx) == nx - 1, gx == n_gx - 1)
    )
    faces_open = jnp.where(x_open, 1.0, 0.0) + jnp.where(open_lane(nx), 1.0, 0.0)

    def store_pair(slab, ids0, ids1, heat0, heat1):
        r0, r1 = look(ids0), look(ids1)
        values = (
            jnp.where(even_own, r1, r0),
            jnp.where(even_own, r0, r1),
            jnp.where(even_own, heat0, heat1),
            jnp.where(even_own, heat1, heat0),
        )
        for a, value in enumerate(values):
            kh[a, slab, pl.ds(PAD, nx), :] = value
        return values

    def gather_strip(value, z, col0, pack):
        n = value.shape[0]
        return jnp.where(inner_group[:n] == z, spin(value, z * GROUP + 1 - col0), pack)

    def own_pair(z, carry):
        store_pair(z + halo + 1, mat[2 * z], mat[2 * z + 1], heat[2 * z], heat[2 * z + 1])
        return carry

    inputs[1].wait()
    inputs[2].wait()
    loop(pairs, own_pair, 0, 4)

    def own_strip(z, packs):
        values = [kh[a, z + halo + 1, pl.ds(PAD, nx), :] for a in range(4)]
        return tuple(
            tuple(gather_strip(value, z + halo, at[3], old) for value, old in zip(values, pack))
            for at, pack in zip(strips, packs)
        )

    ones, nothing = jnp.ones((nx, ny), jnp.float32), jnp.zeros((nx, ny), jnp.float32)

    def x_side(step):
        return (gx > 0) if step < 0 else (gx < n_gx - 1)

    def x_rows(step, n):
        if step > 0:
            return pl.ds(PAD + nx - n, n), pl.ds(PAD - n, n)
        return pl.ds(PAD, n), pl.ds(PAD + nx, n)

    def messages(x_parts, y_src, y_dst, send, recv, landing):
        at = 0

        def make(src, dst, exists, where):
            nonlocal at
            copy = pltpu.make_async_remote_copy(
                src_ref=src, dst_ref=dst, send_sem=send.at[at], recv_sem=recv.at[at], device_id=where, device_id_type=MESH
            )
            at += 1
            return exists, copy

        if n_gx > 1:
            for step in (1, -1):
                to = -step if landing else step
                src, dst = x_parts
                face = (1 - step) // 2
                yield make(src.at[face], dst.at[face], x_side(to), {"gx": gx + to})
        for side, (_, _, _, _, exists, there, other) in enumerate(strips):
            mine = side if not landing else side
            target = side if landing else other
            slot = at
            lanes_dst = y_dst.at[target]
            own = pl.ds(PAD, nx)
            yield exists, pltpu.make_async_remote_copy(
                src_ref=y_src.at[mine].at[(*y_lead(y_src), own)],
                dst_ref=lanes_dst.at[(*y_lead(y_src), own)],
                send_sem=send.at[slot],
                recv_sem=recv.at[y_slot(slot, side, other, landing)],
                device_id={"gy": there},
                device_id_type=MESH,
            )
            at += 1
            if n_gx > 1:
                for step in (1, -1):
                    to = -step if landing else step
                    src, dst = x_rows(step, DEPTH)
                    yield both(exists, x_side(to)), pltpu.make_async_remote_copy(
                        src_ref=y_src.at[mine].at[(*y_lead(y_src), src)],
                        dst_ref=lanes_dst.at[(*y_lead(y_src), dst)],
                        send_sem=send.at[at],
                        recv_sem=recv.at[y_slot(at, side, other, landing)],
                        device_id={"gx": gx + to, "gy": there},
                        device_id_type=MESH,
                    )
                    at += 1

    stride = 3 if n_gx > 1 else 1

    def y_lead(ref):
        return (slice(None),) if len(ref.shape) == 4 else ()

    def y_slot(at, side, other, landing):
        if len(strips) < 2 or landing:
            return at
        return at + (other - side) * stride

    fields_a = [(kh.at[a], n) for a, n in enumerate(X_ROWS)]
    fields_b = [(post, DEPTH)]

    def x_pack(buf, fields, first, many):
        def slab(i, carry):
            for face, step in enumerate((1, -1)):
                at = i * sum(n for _, n in fields)
                for ref, n in fields:
                    src, _ = x_rows(step, n)
                    buf[face, pl.ds(at, n), :] = ref[i + first, src, :]
                    at = at + n
            return carry

        if n_gx > 1:
            loop(many, slab, 0)

    def x_unpack(buf, fields, first, many):
        for face, step in enumerate((1, -1)):
            def slab(i, carry):
                at = i * sum(n for _, n in fields)
                for ref, n in fields:
                    _, dst = x_rows(step, n)
                    ref[i + first, dst, :] = buf[face, pl.ds(at, n), :]
                    at = at + n
                return carry

            def side(slab=slab):
                loop(many, slab, 0)

            if n_gx > 1:
                pl.when(x_side(-step))(side)

    def own_columns(value, z, packs):
        result = []
        n = value.shape[0]
        for (edge, own, _, _, _, _, _), pack in zip(strips, packs):
            to = z * GROUP + own
            result.append(jnp.where(lane[:n] == to, spin(value, to - edge), pack))
        return tuple(result)

    def own_mask(own):
        return jnp.logical_and(column == own, zgroup < pairs + 2 * halo)

    x_pack(xs, fields_a, halo + 1, pairs)
    a_args = ((xs, xr), ps, sh, a_send, a_recv)
    e_args = ((xs2, xr2), pe, re, e_send, e_recv)
    pl.semaphore_wait(barrier, n_friends if near else count - 1)

    z_edge = (nz - DEPTH) * (1 - gz)
    z_copies = [
        pltpu.make_async_remote_copy(
            src_ref=src.at[pl.ds(z_edge, DEPTH)],
            dst_ref=dst,
            send_sem=z_send.at[i],
            recv_sem=z_recv.at[i],
            device_id={"gz": 1 - gz},
            device_id_type=MESH,
        )
        for i, (src, dst) in enumerate(((mat, zmat), (heat, zheat)))
    ]
    for copy in z_copies:
        copy.start()
    first_copies = list(messages(*a_args, False))
    to_x = 2 if n_gx > 1 else 0
    for exists, copy in first_copies[:to_x]:
        guarded(exists, copy.start)
    packs = loop(pairs, own_strip, tuple((ones, ones, nothing, nothing) for _ in strips), 8)
    for side, pack in enumerate(packs):
        for a in range(4):
            ps[side, a, pl.ds(PAD, nx), :] = pack[a]
    for exists, copy in first_copies[to_x:]:
        guarded(exists, copy.start)
    relay(0)
    for copy in z_copies:
        copy.wait_recv()
    beyond = 1 + (pairs + halo) * (1 - gz)
    packs = [nothing for _ in strips]
    for g in range(halo):
        values = store_pair(beyond + g, zmat[2 * g], zmat[2 * g + 1], zheat[2 * g], zheat[2 * g + 1])
        for side, at in enumerate(strips):
            for a in range(4):
                to = a * (ny // 4) + g * GROUP + 1
                here = jnp.logical_and(lane_own >= to, lane_own < to + DEPTH)
                packs[side] = jnp.where(here, spin(values[a], to - at[3]), packs[side])
    for side, pack in enumerate(packs):
        pe[side, pl.ds(PAD, nx), :] = pack
    x_pack(xs2, fields_a, beyond, halo)
    for exists, copy in messages(*e_args, False):
        guarded(exists, copy.start)

    blank = jnp.zeros((full, ny), jnp.float32)
    for field in (red, black, post):
        for slab in (0, 1 + (pairs + halo) * gz, 2 + (pairs + halo) * gz, pairs + 2 * halo + 1):
            field[slab] = jnp.zeros((nx + 2 * PAD, ny), jnp.float32)

        def clear(z, carry):
            field[z, pl.ds(0, PAD), :] = jnp.zeros((PAD, ny), jnp.float32)
            field[z, pl.ds(PAD + nx, PAD), :] = jnp.zeros((PAD, ny), jnp.float32)
            return carry

        loop(pairs + 2 * halo + 2, clear, 0)
    for side in range(len(strips)):
        for buf in (sred, sblack):
            buf[side] = jnp.zeros((nx + 2 * PAD, ny), jnp.float32)
        for row in (PAD - DEPTH - 1, PAD + nx + DEPTH):
            spost[side, pl.ds(row, 1), :] = jnp.zeros((1, ny), jnp.float32)

    def calm(slab, carry):
        for a in range(2):
            for row in (PAD - DEPTH - 1, PAD + nx + DEPTH):
                kh[a, slab, pl.ds(row, 1), :] = jnp.ones((1, ny), jnp.float32)
        return carry

    loop(pairs + 2 * halo + 2, calm, 0)
    for side in range(len(strips)):
        for a in range(2):
            for row in (PAD - DEPTH - 1, PAD + nx + DEPTH):
                sh[side, a, pl.ds(row, 1), :] = jnp.ones((1, ny), jnp.float32)

    def fill(start):
        def slab(z, carry):
            for a in range(4):
                kh[a, z, pl.ds(start, DEPTH), :] = jnp.full((DEPTH, ny), 1.0 if a < 2 else 0.0, jnp.float32)
            return carry

        loop(pairs + 2 * halo + 2, slab, 0)
        for side in range(len(strips)):
            for a in range(4):
                sh[side, a, pl.ds(start, DEPTH), :] = jnp.full((DEPTH, ny), 1.0 if a < 2 else 0.0, jnp.float32)

    pl.when(gx == 0)(lambda: fill(PAD - DEPTH))
    pl.when(gx == n_gx - 1)(lambda: fill(PAD + nx))
    for side, strip_of in enumerate(strips):
        if strip_of[4] is not None:
            def vacant(side=side):
                for a in range(4):
                    sh[side, a] = jnp.full((nx + 2 * PAD, ny), 1.0 if a < 2 else 0.0, jnp.float32)

            pl.when(jnp.logical_not(strip_of[4]))(vacant)

    def losses(z, carry):
        low = jnp.where(jnp.logical_and(z == 0, gz == 0), 1.0, 0.0)
        high = jnp.where(jnp.logical_and(z == pairs - 1, gz == n_gz - 1), 1.0, 0.0)
        faces = faces_open + jnp.where(even_own, low, high)
        leak[z] = faces * rcp(kh[1, z + halo + 1, pl.ds(PAD, nx), :])
        return carry

    loop(pairs, losses, 0, 4)
    for layer in range(lz):
        def add(z, total):
            return total + heat[layer * BLOCK + z]
        hsum[layer] = loop(BLOCK, add, jnp.zeros((nx, ny), jnp.float32), 4)

    def own_resist(rows):
        def step(z, packs):
            z = z + halo * (1 - gz)
            return tuple(own_columns(kh[a, z + 1, rows, :], z, packs[a]) for a in range(2))

        fresh = jnp.ones((rows.size, ny), jnp.float32)
        packs = loop(pairs + halo, step, (tuple(fresh for _ in strips),) * 2)
        for side in range(len(strips)):
            for a in range(2):
                oc[side, a, rows, :] = packs[a][side]

    own_resist(pl.ds(PAD, nx))

    relay(1)
    for args in (a_args, e_args):
        for exists, copy in messages(*args, True):
            guarded(exists, copy.wait_recv)
    x_unpack(xr, fields_a, halo + 1, pairs)
    x_unpack(xr2, fields_a, beyond, halo)
    own_resist(pl.ds(zero + (PAD - DEPTH), 8))
    own_resist(pl.ds(zero + (PAD + nx + DEPTH - 8), 8))
    wall, wall_own = halo + (pairs + 1) * gz, halo + 1 + (pairs - 1) * gz
    for a in range(2):
        kh[a, wall, rows_of(full), :] = kh[1 - a, wall_own, rows_of(full), :]
    x_first = beyond - 1
    came = jnp.logical_and(zgroup >= x_first, zgroup < x_first + halo)
    for side, at in enumerate(strips):
        extra = re[side, rows_of(full), :]
        whole = []
        for a in range(4):
            value = jnp.where(came, spin(extra, x_first * GROUP - a * (ny // 4)), sh[side, a, rows_of(full), :])
            if a < 2:
                value = jnp.where(own_mask(at[1]), oc[side, a, rows_of(full), :], value)
            whole.append(value)
        for a in range(4):
            value = whole[a]
            if a < 2:
                value = jnp.where(zgroup == wall - 1, spin(whole[1 - a], GROUP * (2 * gz - 1)), value)
            sh[side, a, rows_of(full), :] = value

    def mirror(outer, inner):
        def slab(z, carry):
            for a in range(2):
                kh[a, z + 1, outer, :] = kh[1 - a, z + 1, inner, :]
            return carry

        loop(pairs + 2 * halo, slab, 0)
        for side in range(len(strips)):
            for a in range(2):
                sh[side, a, outer, :] = sh[side, 1 - a, inner, :]

    pl.when(gx == 0)(lambda: mirror(pl.ds(PAD - 1, 1), pl.ds(PAD, 1)))
    pl.when(gx == n_gx - 1)(lambda: mirror(pl.ds(PAD + nx, 1), pl.ds(PAD + nx - 1, 1)))

    wide, inner = [(True, t) for t in range(full // 8)], [(False, t) for t in range(nx // 8)]
    even8, lane8, column_step = even_own[:8], lane_own[:8], lax.rem(lane_own[:8], BLOCK) == 0
    open8 = open_lane(8)
    closed8 = jnp.where(open8, 0.0, 1.0)

    def at(tile, shift=0):
        deep, t = tile
        if not deep and shift == 0:
            return pl.ds(PAD + 8 * t, 8)
        return pl.ds(zero + (PAD - (DEPTH if deep else 0) + 8 * t + shift), 8)

    def cut(tile):
        deep, t = tile
        return pl.ds(8 * t, 8) if deep else pl.ds(zero + (DEPTH + 8 * t), 8)

    def halos_of(refs, tiles):
        return [[ref[at(tile), :] for ref in refs] for tile in tiles]

    def beside(value, halos, z, walls):
        low, high = pltpu.roll(value, 1, 1), pltpu.roll(value, ny - 1, 1)
        ends = [
            spin(near_by, edge - (z * GROUP + adj))
            for near_by, (edge, _, adj, _, _, _, _) in zip(halos, strips)
        ]
        ends = ends or [value]
        if walls is None:
            ends = [end * closed8 for end in ends]
        else:
            ends = [jnp.where(open8, walls, end) for end in ends]
        return jnp.where(lane8 == 0, ends[0], low), jnp.where(lane8 == ny - 1, ends[-1], high)

    def around(field, color, z, tile, halos, walls=None):
        here = z + 1
        same = field[here, at(tile), :]
        before, after = field[here - 1, at(tile), :], field[here + 1, at(tile), :]
        low, high = beside(same, halos, z, walls)
        return (
            same,
            jnp.where(even8, before, after) if color == 0 else jnp.where(even8, after, before),
            field[here, at(tile, -1), :],
            field[here, at(tile, 1), :],
            low,
            high,
        )

    def tile_packs(values, z, packs):
        return tuple(own_columns(value, z, pack) for value, pack in zip(values, packs))

    blank8 = jnp.zeros((8, ny), jnp.float32)
    no_packs = tuple(tuple(blank8 for _ in strips) for _ in wide)

    def joined(packs, side):
        return jnp.concatenate([pack[side] for pack in packs], axis=0)

    def strip_around(ref, color):
        same = ref[rows_of(full), :]
        before, after = pltpu.roll(same, GROUP, 1), pltpu.roll(same, ny - GROUP, 1)
        return (
            same,
            jnp.where(even, after, before) if color == 0 else jnp.where(even, before, after),
            ref[rows_of(full, -1), :],
            ref[rows_of(full, 1), :],
            pltpu.roll(same, 1, 1),
            pltpu.roll(same, ny - 1, 1),
        )

    def shares(center, others):
        parts = [rcp(center + other) for other in others]
        total = parts[0]
        for part in parts[1:]:
            total = total + part
        return parts, total

    def strip_weigh(color):
        for side in range(len(strips)):
            a = 1 - color
            center = sh[side, a, rows_of(full), :]
            parts, total = shares(center, strip_around(sh.at[side, 1 - a], color))
            inverse = jnp.where(in_strip, rcp(total), 0.0)
            if strips[side][4] is not None:
                inverse = jnp.where(strips[side][4], inverse, 0.0)
            for face in range(6):
                swd[side, color, face] = parts[face] * inverse
            shd[side, color] = sh[side, 2 + color, rows_of(full), :] * (0.5 * inverse)

    def weigh(color):
        a = 1 - color
        halos = halos_of([sh.at[side, 1 - a] for side in range(len(strips))], wide)

        def step(i, packs):
            z = i + halo * (1 - gz)
            ratios = []
            for tile in wide:
                t = tile[1]
                center = kh[a, z + 1, at(tile), :]
                parts, total = shares(center, around(kh.at[1 - a], color, z, tile, halos[t], center))
                inverse = rcp(total)
                if t in (0, len(wide) - 1):
                    inverse = jnp.where(inside_row[8 * t : 8 * t + 8], inverse, 0.0)
                for face in range(6):
                    wd[color, face, z, cut(tile), :] = parts[face] * inverse
                ratio = kh[2 + color, z + 1, at(tile), :] * (0.5 * inverse)
                hd[color, z, cut(tile), :] = ratio
                if color == 1:
                    dg[z, cut(tile), :] = total * 2.0
                else:
                    red[z + 1, at(tile), :] = ratio
                    ratios.append(ratio)
            return packs if color == 1 else tile_packs(ratios, z, packs)

        return loop(pairs + halo, step, no_packs, WEIGH_UNROLL)

    for color in range(2):
        strip_weigh(color)
    packs = weigh(0)
    for side, (_, own, _, _, _, _, _) in enumerate(strips):
        sred[side, rows_of(full), :] = jnp.where(own_mask(own), joined(packs, side), shd[side, 0])
    relay(2)
    weigh(1)

    def weights_of(color, z, tile):
        return hd[color, z, cut(tile), :], [wd[color, face, z, cut(tile), :] for face in range(6)]

    def total_of(source, weights, others):
        result = source
        for weight, other in zip(weights, others):
            result = result + weight * other
        return result

    def stage(color, src, strip_src, dst, strip_dst, reach):
        halos = halos_of([strip_src.at[side] for side in range(len(strips))], wide)

        def step(i, packs):
            first = i + halo - reach * gz
            values = []
            for z in [first + k for k in range(pairs + reach)]:
                values.append([])
                for tile in wide:
                    source, weights = weights_of(color, z, tile)
                    values[-1].append(total_of(source, weights, around(src, color, z, tile, halos[tile[1]])))
            for k, row in enumerate(values):
                for tile, value in zip(wide, row):
                    dst[first + k + 1, at(tile), :] = value
            for k, row in enumerate(values):
                packs = tile_packs(row, first + k, packs)
            return packs

        packs = step(0, no_packs)
        for side, (_, own, _, _, _, _, _) in enumerate(strips):
            value = total_of(
                shd[side, color],
                [swd[side, color, face] for face in range(6)],
                strip_around(strip_src.at[side], color),
            )
            strip_dst[side, rows_of(full), :] = jnp.where(own_mask(own), joined(packs, side), value)

    stage(1, red, sred, black, sblack, 2)
    stage(0, black, sblack, red, sred, 2)

    halos = halos_of([sred.at[side] for side in range(len(strips))], inner)
    tiles = BLOCK // 8
    none = jnp.zeros((nx, ny), jnp.float32)
    sums = []
    for layer in range(lz):
        def flow(i, carry):
            z = i + layer * (BLOCK // 2) + halo
            result = []
            for tile, (own_sum, x_sum, y_sum) in zip(inner, carry):
                t = tile[1]
                source, weights = weights_of(1, z, tile)
                others = around(red, 1, z, tile, halos[t])
                value = total_of(source, weights, others)
                post[z + 1, at(tile), :] = value
                spare = dg[z, cut(tile), :]
                face = 2 if t % tiles == 0 else 3
                own_sum = own_sum + leak[z - halo, pl.ds(8 * t, 8), :] * others[0]
                if t % tiles in (0, tiles - 1):
                    x_sum = x_sum + spare * ((value - others[face]) * weights[face])
                aside, weight = (
                    jnp.where(column_step, pair[0], pair[1]) for pair in (others[4:], weights[4:])
                )
                y_sum = y_sum + spare * ((value - aside) * weight)
                result.append((own_sum, x_sum, y_sum))
            return tuple(result)

        parts = loop(BLOCK // 2, flow, tuple((blank8,) * 3 for _ in inner), FLOW_UNROLL)
        sums.append(tuple(jnp.concatenate([part[i] for part in parts], axis=0) for i in range(3)))

    z_from, z_to = halo + 1 + (pairs - halo) * (1 - gz), 1 + (pairs + halo) * gz
    z_back = 1 + (pairs + halo) * (1 - gz)
    own = pl.ds(PAD, nx)
    z_copy = [
        pltpu.make_async_remote_copy(
            src_ref=post.at[pl.ds(z_from, halo), own],
            dst_ref=post.at[pl.ds(to, halo), own],
            send_sem=z_send.at[2],
            recv_sem=z_recv.at[2],
            device_id={"gz": 1 - gz},
            device_id_type=MESH,
        )
        for to in (z_to, z_back)
    ]
    z_copy[0].start()

    totals = [none, *(hsum[layer] - sums[layer][0] for layer in range(lz)), none]
    for layer in range(lz):
        for late in range(2):
            z = halo + layer * (BLOCK // 2) + (BLOCK // 2 - 1) * late
            beyond_z = red[z + 2, own, :] if late else red[z, own, :]
            deep_rows = pl.ds(zero + DEPTH, nx)
            flux = dg[z, deep_rows, :] * wd[1, 1, z, deep_rows, :] * (post[z + 1, own, :] - beyond_z)
            flux = jnp.where(even_own, flux, 0.0) if late else jnp.where(even_own, 0.0, flux)
            totals[layer + 1] = totals[layer + 1] - flux
            to = layer + 2 if late else layer
            totals[to] = totals[to] + flux
    for i, value in enumerate((*totals, *(s[2] for s in sums))):
        vsum[:, i * ny : (i + 1) * ny] = value
    for copy in fetch:
        copy.wait()
    part = jnp.dot(shrink[0], vsum[...], precision=HIGH, preferred_element_type=jnp.float32)
    for layer in range(lz):
        vsum[:, layer * ny : (layer + 1) * ny] = sums[layer][1]
    bent = jnp.dot(shrink[1], vsum[:, : lz * ny], precision=HIGH, preferred_element_type=jnp.float32)
    turned_part = [part[:, i * ny : (i + 1) * ny] for i in range(2 * lz + 2)]
    for layer in range(lz):
        turned_part[layer + 1] = turned_part[layer + 1] + bent[:, layer * ny : (layer + 1) * ny]
    part = times(jnp.concatenate(turned_part, axis=1), (gather[0], gather[1]))
    got[me] = part

    def gathering(step, start):
        other, where = peer_of(step)
        copy = pltpu.make_async_remote_copy(
            src_ref=got.at[me],
            dst_ref=got.at[me if start else other],
            send_sem=gsend.at[step],
            recv_sem=grecv.at[me if start else other],
            device_id=where,
            device_id_type=MESH,
        )
        return copy

    relay(3)
    each_peer(lambda step: gathering(step, True).start())

    z_copy[1].wait_recv()

    def pack_post(z, packs):
        z = z + halo * (1 - gz)
        value = post[z + 1, own, :]
        return tuple(gather_strip(value, z, s[3], pack) for s, pack in zip(strips, packs))

    packs = loop(pairs + halo, pack_post, tuple(none for _ in strips))
    for side, pack in enumerate(packs):
        psb[side, own, :] = pack
    x_pack(xsb, fields_b, 1 + halo * (1 - gz), pairs + halo)
    b_args = ((xsb, xrb), psb, spost, b_send, b_recv)
    for exists, copy in messages(*b_args, False):
        guarded(exists, copy.start)

    each_peer(lambda step: gathering(step, False).wait_recv())
    if count <= 32:
        hat = got[0]
        for i in range(1, count):
            hat = hat + got[i]
    else:
        hat = lax.fori_loop(1, count, lambda i, acc: acc + got[i], got[0])
    kbar = table[0]
    for m in range(1, table.shape[0]):
        kbar = kbar + table[m]
    kbar = kbar / table.shape[0]
    hat = hat * scale[...] / kbar
    hat = times(hat, (spread[0], spread[1]))
    rise = jnp.dot(expand[...], hat, precision=HIGH, preferred_element_type=jnp.float32)
    for i in range(corr.shape[0]):
        corr[i] = rise[:, i * ny : (i + 1) * ny]

    z_copy[0].wait_send()
    for exists, copy in messages(*b_args, False):
        guarded(exists, copy.wait_send)
    for exists, copy in messages(*b_args, True):
        guarded(exists, copy.wait_recv)
    x_unpack(xrb, fields_b, 1 + halo * (1 - gz), pairs + halo)

    def correct(i, packs):
        z = i + halo * (1 - gz)
        layer = (z + BLOCK // 2 - halo) // (BLOCK // 2)
        value = post[z + 1, rows_of(full), :]
        value = value + corr[layer, rows_of(full), :]
        post[z + 1, rows_of(full), :] = value
        return own_columns(value, z, packs)

    packs = loop(pairs + halo, correct, tuple(blank for _ in strips))
    for side, (_, own_c, _, _, exists, _, _) in enumerate(strips):
        value = spost[side, rows_of(full), :] + corr[lz + 2 + side, rows_of(full), :]
        value = jnp.where(in_strip, value, 0.0)
        if exists is not None:
            value = jnp.where(exists, value, 0.0)
        spost[side, rows_of(full), :] = jnp.where(own_mask(own_c), packs[side], value)

    stage(0, post, spost, red, sred, 2)
    stage(1, red, sred, black, sblack, 2)
    stage(0, black, sblack, red, sred, 2)

    halos = halos_of([sred.at[side] for side in range(len(strips))], inner)

    def finish(i, carry):
        z = i + halo
        for tile in inner:
            source, weights = weights_of(1, z, tile)
            others = around(red, 1, z, tile, halos[tile[1]])
            last = total_of(source, weights, others)
            rows = pl.ds(8 * tile[1], 8)
            out[2 * i, rows, :] = jnp.where(even8, others[0], last)
            out[2 * i + 1, rows, :] = jnp.where(even8, last, others[0])
        return carry

    loop(pairs, finish, 0, FINISH_UNROLL)

    for copy in z_copies:
        copy.wait_send()
    for args in (a_args, e_args):
        for exists, copy in messages(*args, False):
            guarded(exists, copy.wait_send)
    each_peer(lambda step: gathering(step, True).wait_send())


def per_device(sizes, heat, material, table):
    shape = heat.shape
    nz, nx, ny = shape
    n_gx, n_gy, n_gz = sizes
    assert n_gz == 2
    consts = tables(shape, *sizes)
    spread, gather, expand, shrink, scale = consts
    count = n_gx * n_gy * n_gz
    rows = nx + 2 * PAD
    full = nx + 2 * DEPTH
    sides = max(sides_of(n_gy), 1)
    pairs = nz // 2
    lz = nz // BLOCK
    deep = pairs + DEPTH
    f32 = jnp.float32
    vmem = pl.BlockSpec(memory_space=pltpu.VMEM)
    hbm = pl.BlockSpec(memory_space=pltpu.HBM)
    field = pltpu.VMEM((deep + 2, rows, ny), f32)
    strip = pltpu.VMEM((sides, rows, ny), f32)
    sems = pltpu.SemaphoreType.DMA
    return pl.pallas_call(
        functools.partial(kernel, sizes, shape),
        out_shape=pltpu.VMEM(shape, f32),
        in_specs=[hbm] * 8,
        out_specs=vmem,
        scratch_shapes=[
            pltpu.VMEM(shape, f32),
            pltpu.VMEM(shape, jnp.int32),
            pltpu.VMEM((DEPTH, nx, ny), f32),
            pltpu.VMEM((DEPTH, nx, ny), jnp.int32),
            pltpu.SMEM(table.shape, f32),
            pltpu.VMEM((4, deep + 2, rows, ny), f32),
            pltpu.VMEM((sides, 4, rows, ny), f32),
            pltpu.VMEM((sides, 4, rows, ny), f32),
            strip, strip,
            pltpu.VMEM((sides, 2, rows, ny), f32),
            *[pltpu.VMEM((2, pairs * sum(X_ROWS), ny), f32)] * 2,
            *[pltpu.VMEM((2, DEPTH // 2 * sum(X_ROWS), ny), f32)] * 2,
            *[pltpu.VMEM((2, (deep - DEPTH // 2) * DEPTH, ny), f32)] * 2,
            field, field, field,
            strip, strip, strip, strip,
            pltpu.VMEM((2, 6, deep, full, ny), f32),
            pltpu.VMEM((2, deep, full, ny), f32),
            pltpu.VMEM((deep, full, ny), f32),
            pltpu.VMEM((pairs, nx, ny), f32),
            pltpu.VMEM((sides, 2, 6, full, ny), f32),
            pltpu.VMEM((sides, 2, full, ny), f32),
            pltpu.VMEM((lz, nx, ny), f32),
            pltpu.VMEM((nx, gather.shape[3]), f32),
            pltpu.VMEM((spread.shape[4] // ny, rows, ny), f32),
            pltpu.VMEM(spread.shape[2:], jnp.bfloat16),
            pltpu.VMEM(gather.shape[2:], jnp.bfloat16),
            pltpu.VMEM(expand.shape[1:], f32),
            pltpu.VMEM(shrink.shape[1:], f32),
            pltpu.VMEM(scale.shape, f32),
            pltpu.VMEM((count, *scale.shape), f32),
            sems((8,)),
            sems((3,)),
            sems((3,)),
            sems((8,)),
            sems((8,)),
            sems((8,)),
            sems((8,)),
            sems((8,)),
            sems((8,)),
            sems((count,)),
            sems((count,)),
            pltpu.SemaphoreType.REGULAR((RELAYS,)),
        ],
        compiler_params=pltpu.CompilerParams(
            collective_id=0, has_side_effects=True, vmem_limit_bytes=64 * 1024 * 1024 - 3 * nz * nx * ny * 2
        ),
    )(heat, material, table, *(jnp.asarray(c) for c in consts))


def solution(mesh):
    sizes = (mesh.shape["gx"], mesh.shape["gy"], mesh.shape["gz"])
    spec = P("gz", ("groups", "gx"), "gy")
    return jax.shard_map(
        functools.partial(per_device, sizes),
        mesh=mesh,
        in_specs=(spec, spec, P()),
        out_specs=spec,
        check_vma=False,
    )
```

```python
import functools
import math

import jax
import jax.numpy as jnp
import numpy as np
from jax import lax
from jax.experimental import pallas as pl
from jax.experimental.pallas import tpu as pltpu
from jax.sharding import PartitionSpec as P

BLOCK = 16
PAD = 8
DEPTH = 4
GROUP = DEPTH + 2
X_ROWS = (DEPTH, DEPTH - 1, DEPTH - 1, DEPTH - 2)
MESH = pl.DeviceIdType.MESH
HIGH = lax.Precision.HIGHEST
UNROLL = 18
RELAYS = 3
WEIGH_UNROLL = 9
FLOW_UNROLL = 8
FINISH_UNROLL = 16


def sine_rows(count):
    j = np.arange(-1, count + 1)[:, None] + 1.0
    k = np.arange(count)[None, :] + 1.0
    rows = np.sin(math.pi * j * k / (count + 1))
    rows[0] = 0.0
    rows[-1] = 0.0
    return rows


def split(table):
    first = table.astype(jnp.bfloat16)
    return np.stack([first, (table - first.astype(np.float32)).astype(jnp.bfloat16)], axis=-3)


def times(value, pair):
    rows = value.shape[0]
    first = value.astype(jnp.bfloat16).astype(jnp.float32)
    both = jnp.concatenate([first, value - first], axis=0).astype(jnp.bfloat16)
    main = jnp.dot(both, pair[0], preferred_element_type=jnp.float32)
    rest = jnp.dot(both, pair[1], preferred_element_type=jnp.float32)
    return main[:rows] + main[rows:] + rest[:rows]


def sides_of(n_gy):
    return 0 if n_gy == 1 else 1 if n_gy == 2 else 2


def tables(shape, n_gx, n_gy, n_gz):
    nz, nx, ny = shape
    lz, lx, ly = (s // BLOCK for s in shape)
    fz, fx, fy = lz * n_gz, lx * n_gx, ly * n_gy
    cols = fz * fy
    wide = -(-cols // 128) * 128
    sz, sx, sy = sine_rows(fz), sine_rows(fx), sine_rows(fy)
    n_sides = sides_of(n_gy)
    lane = np.arange(ny)
    spread = np.zeros((n_gy, n_gz, wide, (lz + 2 + n_sides) * ny))
    gather = np.zeros((n_gy, n_gz, (2 * lz + 2) * ny, wide))
    for a in range(n_gy):
        yrow = np.floor_divide(np.arange(-1, ny + 1) + a * ny, BLOCK) + 1
        own, prev, after = sy[yrow[1:-1]], sy[yrow[:-2]], sy[yrow[2:]]
        ends = np.where((lane % BLOCK == 0)[:, None], prev - own, 0.0)
        ends = np.where((lane % BLOCK == BLOCK - 1)[:, None], after - own, ends)
        for b in range(n_gz):
            zrow = np.arange(-1, lz + 1) + b * lz + 1
            for i, row in enumerate(zrow):
                block = np.einsum("p,yq->pqy", sz[row], own).reshape(cols, -1)
                spread[a, b, :cols, i * ny : (i + 1) * ny] = block
                gather[a, b, i * ny : (i + 1) * ny, :cols] = block.T
                if 1 <= i <= lz:
                    at = (lz + 1 + i) * ny
                    block = np.einsum("p,yq->pqy", sz[row], ends).reshape(cols, -1)
                    gather[a, b, at : at + ny, :cols] = block.T
            count = (nz // 2 + DEPTH) * GROUP
            zi, c = np.arange(count) // GROUP, np.arange(count) % GROUP
            fine = np.floor_divide(2 * zi - DEPTH + b * nz, BLOCK) + 1
            for side in range(n_sides):
                high = a == 0 if n_sides == 1 else side == 1
                base = ny - 1 if high else -DEPTH - 1
                column = np.floor_divide(base + c + a * ny, BLOCK) + 1
                block = np.einsum("lp,lq->pql", sz[fine], sy[column]).reshape(cols, -1)
                at = (lz + 2 + side) * ny
                spread[a, b, :cols, at : at + count] = block
    rows = nx + 2 * PAD
    expand = np.zeros((n_gx, rows, fx))
    shrink = np.zeros((n_gx, 2, fx, nx))
    for a in range(n_gx):
        xs = np.arange(-DEPTH, nx + DEPTH) + a * nx
        expand[a, PAD - DEPTH : PAD + nx + DEPTH] = sx[np.floor_divide(xs, BLOCK) + 1]
        block = np.arange(nx) // BLOCK + a * lx + 1
        shrink[a, 0] = sx[block].T
        step = np.where(np.arange(nx) % BLOCK == 0, -1, 0) + np.where(np.arange(nx) % BLOCK == BLOCK - 1, 1, 0)
        shrink[a, 1] = (sx[block + step] - sx[block]).T
    lam = lambda n: 2.0 - 2.0 * np.cos(math.pi * (np.arange(n) + 1.0) / (n + 1))
    total = lam(fx)[:, None] + (lam(fz)[:, None] + lam(fy)[None, :]).reshape(1, -1)
    scale = np.zeros((fx, wide))
    scale[:, :cols] = BLOCK * BLOCK * 8.0 / ((fz + 1) * (fx + 1) * (fy + 1)) / total / BLOCK**3
    spread, gather, expand, shrink, scale = (t.astype(np.float32) for t in (spread, gather, expand, shrink, scale))
    return split(spread), split(gather), expand, shrink, scale


def kernel(
    sizes, shape, heat_hbm, mat_hbm, table_hbm, spread_hbm, gather_hbm, expand_hbm, shrink_hbm, scale_hbm,
    out, heat, mat, zheat, zmat, table, kh, sh, ps, pe, re, oc, xs, xr, xs2, xr2, xsb, xrb, red, black, post, sred, sblack, spost, psb, wd, hd, dg, leak,
    swd, shd, hsum, vsum, corr, spread, gather, expand, shrink, scale, got,
    in_sem, z_send, z_recv, a_send, a_recv, e_send, e_recv, b_send, b_recv, gsend, grecv, relays,
):
    n_gx, n_gy, n_gz = sizes
    nz, nx, ny = shape
    lz = nz // BLOCK
    pairs = nz // 2
    halo = DEPTH // 2
    full = nx + 2 * DEPTH
    gx, gy, gz = lax.axis_index("gx"), lax.axis_index("gy"), lax.axis_index("gz")
    count = n_gx * n_gy * n_gz
    me = (gx * n_gy + gy) * n_gz + gz
    zero = gx // n_gx
    rcp = functools.partial(pltpu.reciprocal, approx=True)

    few = count <= 32
    offsets = sorted(
        ((a, b, c) for a in range(n_gx) for b in range(n_gy) for c in range(n_gz) if a or b or c),
        key=lambda o: (-min(o[0], n_gx - o[0]), -min(o[1], n_gy - o[1]), -o[2]),
    )

    def turned(position, step, size):
        at = position + step
        return jnp.where(at >= size, at - size, at)

    def peer_of(step):
        if few:
            a, b, c = offsets[step - 1]
            at = turned(gx, a, n_gx), turned(gy, b, n_gy), turned(gz, c, n_gz)
            return (at[0] * n_gy + at[1]) * n_gz + at[2], dict(zip(("gx", "gy", "gz"), at))
        other = lax.rem(me + step, count)
        return other, {
            "gx": other // (n_gy * n_gz),
            "gy": lax.rem(other // n_gz, n_gy),
            "gz": lax.rem(other, n_gz),
        }

    def each_peer(action):
        if few:
            for step in range(1, count):
                action(step)
            return

        def one(step, carry):
            action(step)
            return carry

        lax.fori_loop(1, count, one, 0)

    inputs = [
        pltpu.make_async_copy(table_hbm, table, in_sem.at[5]),
        pltpu.make_async_copy(mat_hbm, mat, in_sem.at[6]),
        pltpu.make_async_copy(heat_hbm, heat, in_sem.at[7]),
    ]
    for copy in inputs:
        copy.start()
    barrier = pltpu.get_barrier_semaphore()

    def greet(step):
        _, where = peer_of(step)
        pl.semaphore_signal(barrier, inc=1, device_id=where, device_id_type=MESH)

    near = n_gx <= RELAYS + 1 and n_gy == 2
    friends = [(None, {"gz": 1 - gz}), (None, {"gy": 1 - gy})]
    for step in (-1, 1):
        beside_x = (gx > 0) if step < 0 else (gx < n_gx - 1)
        friends.append((beside_x, {"gx": gx + step}))
        friends.append((beside_x, {"gx": gx + step, "gy": 1 - gy}))
    n_friends = 2 + 2 * (jnp.where(gx > 0, 1, 0) + jnp.where(gx < n_gx - 1, 1, 0))

    def tell(sem):
        for exists, where in friends:
            def signal(where=where):
                pl.semaphore_signal(sem, inc=1, device_id=where, device_id_type=MESH)

            if exists is None:
                signal()
            else:
                pl.when(exists)(signal)

    def relay(step):
        if near:
            if step > 0:
                pl.semaphore_wait(relays.at[step - 1], n_friends)
            if step < RELAYS:
                tell(relays.at[step])

    if near:
        tell(barrier)
    else:
        each_peer(greet)

    fetch = [
        pltpu.make_async_copy(spread_hbm.at[gy, gz], spread, in_sem.at[0]),
        pltpu.make_async_copy(gather_hbm.at[gy, gz], gather, in_sem.at[1]),
        pltpu.make_async_copy(expand_hbm.at[gx], expand, in_sem.at[2]),
        pltpu.make_async_copy(shrink_hbm.at[gx], shrink, in_sem.at[3]),
        pltpu.make_async_copy(scale_hbm, scale, in_sem.at[4]),
    ]
    for copy in fetch:
        copy.start()

    if n_gy == 1:
        strips = []
    elif n_gy == 2:
        strips = [((ny - 1) * (1 - gy), (DEPTH + 1) * gy, 1 + (DEPTH - 1) * gy, (ny - DEPTH) * (1 - gy), None, 1 - gy, 0)]
    else:
        strips = [
            (0, DEPTH + 1, DEPTH, 0, gy > 0, gy - 1, 1),
            (ny - 1, 0, 1, ny - DEPTH, gy < n_gy - 1, gy + 1, 0),
        ]

    def guarded(exists, action):
        if exists is None:
            action()
        else:
            pl.when(exists)(action)

    def both(a, b):
        return b if a is None else a if b is None else jnp.logical_and(a, b)

    def lanes(n):
        return lax.broadcasted_iota(jnp.int32, (n, ny), 1)

    def sublanes(n):
        return lax.broadcasted_iota(jnp.int32, (n, ny), 0)

    lane = lanes(full)
    even = lax.rem(lane + sublanes(full), 2) == 0
    lane_own = lanes(nx)
    even_own = lax.rem(lane_own + sublanes(nx), 2) == 0
    row_x = sublanes(full) - DEPTH
    inside_row = jnp.logical_and(row_x + gx * nx >= 0, row_x + gx * nx < n_gx * nx)
    column = lax.rem(lane, GROUP)
    zgroup = lane // GROUP
    inner_group = jnp.where(jnp.logical_and(column >= 1, column <= DEPTH), zgroup, -1)
    first_z, last_z = halo * (1 - gz), pairs + halo + halo * (1 - gz)
    in_strip = jnp.logical_and(
        jnp.logical_and(inside_row, inner_group >= 0), jnp.logical_and(zgroup >= first_z, zgroup < last_z)
    )
    low_open, high_open = gy == 0, gy == n_gy - 1

    def open_lane(n):
        at = lanes(n)
        return jnp.logical_or(
            jnp.logical_and(at == 0, low_open), jnp.logical_and(at == ny - 1, high_open)
        )

    closed = {n: jnp.where(open_lane(n), 0.0, 1.0) for n in (full, nx)}

    def rows_of(n, shift=0):
        if n == nx and shift == 0:
            return pl.ds(PAD, nx)
        return pl.ds(zero + (PAD - (n - nx) // 2 + shift), n)

    def loop(count, step, carry, unroll=UNROLL):
        return lax.fori_loop(0, count, step, carry, unroll=unroll)

    def spin(value, amount):
        return pltpu.roll(value, lax.rem(amount + 4 * ny, ny), 1)

    inputs[0].wait()
    small = lax.broadcasted_iota(jnp.int32, (8, ny), 1)
    values = jnp.full((8, ny), table[0], jnp.float32)
    for m in range(1, table.shape[0]):
        values = jnp.where(small == m, table[m], values)
    resist = rcp(values)

    def look(ids):
        parts = [
            jnp.take_along_axis(resist, ids[8 * t : 8 * t + 8], axis=1) for t in range(nx // 8)
        ]
        return jnp.concatenate(parts, axis=0)

    x_open = jnp.logical_or(
        jnp.logical_and(sublanes(nx) == 0, gx == 0), jnp.logical_and(sublanes(nx) == nx - 1, gx == n_gx - 1)
    )
    faces_open = jnp.where(x_open, 1.0, 0.0) + jnp.where(open_lane(nx), 1.0, 0.0)

    def store_pair(slab, ids0, ids1, heat0, heat1):
        r0, r1 = look(ids0), look(ids1)
        values = (
            jnp.where(even_own, r1, r0),
            jnp.where(even_own, r0, r1),
            jnp.where(even_own, heat0, heat1),
            jnp.where(even_own, heat1, heat0),
        )
        for a, value in enumerate(values):
            kh[a, slab, pl.ds(PAD, nx), :] = value
        return values

    def gather_strip(value, z, col0, pack):
        n = value.shape[0]
        return jnp.where(inner_group[:n] == z, spin(value, z * GROUP + 1 - col0), pack)

    def own_pair(z, carry):
        store_pair(z + halo + 1, mat[2 * z], mat[2 * z + 1], heat[2 * z], heat[2 * z + 1])
        return carry

    inputs[1].wait()
    inputs[2].wait()
    loop(pairs, own_pair, 0, 8)

    def own_strip(z, packs):
        values = [kh[a, z + halo + 1, pl.ds(PAD, nx), :] for a in range(4)]
        return tuple(
            tuple(gather_strip(value, z + halo, at[3], old) for value, old in zip(values, pack))
            for at, pack in zip(strips, packs)
        )

    ones, nothing = jnp.ones((nx, ny), jnp.float32), jnp.zeros((nx, ny), jnp.float32)

    def x_side(step):
        return (gx > 0) if step < 0 else (gx < n_gx - 1)

    def x_rows(step, n):
        if step > 0:
            return pl.ds(PAD + nx - n, n), pl.ds(PAD - n, n)
        return pl.ds(PAD, n), pl.ds(PAD + nx, n)

    def messages(x_parts, y_src, y_dst, send, recv, landing):
        at = 0

        def make(src, dst, exists, where):
            nonlocal at
            copy = pltpu.make_async_remote_copy(
                src_ref=src, dst_ref=dst, send_sem=send.at[at], recv_sem=recv.at[at], device_id=where, device_id_type=MESH
            )
            at += 1
            return exists, copy

        if n_gx > 1:
            for step in (1, -1):
                to = -step if landing else step
                src, dst = x_parts
                face = (1 - step) // 2
                yield make(src.at[face], dst.at[face], x_side(to), {"gx": gx + to})
        for side, (_, _, _, _, exists, there, other) in enumerate(strips):
            mine = side if not landing else side
            target = side if landing else other
            slot = at
            lanes_dst = y_dst.at[target]
            own = pl.ds(PAD, nx)
            yield exists, pltpu.make_async_remote_copy(
                src_ref=y_src.at[mine].at[(*y_lead(y_src), own)],
                dst_ref=lanes_dst.at[(*y_lead(y_src), own)],
                send_sem=send.at[slot],
                recv_sem=recv.at[y_slot(slot, side, other, landing)],
                device_id={"gy": there},
                device_id_type=MESH,
            )
            at += 1
            if n_gx > 1:
                for step in (1, -1):
                    to = -step if landing else step
                    src, dst = x_rows(step, DEPTH)
                    yield both(exists, x_side(to)), pltpu.make_async_remote_copy(
                        src_ref=y_src.at[mine].at[(*y_lead(y_src), src)],
                        dst_ref=lanes_dst.at[(*y_lead(y_src), dst)],
                        send_sem=send.at[at],
                        recv_sem=recv.at[y_slot(at, side, other, landing)],
                        device_id={"gx": gx + to, "gy": there},
                        device_id_type=MESH,
                    )
                    at += 1

    stride = 3 if n_gx > 1 else 1

    def y_lead(ref):
        return (slice(None),) if len(ref.shape) == 4 else ()

    def y_slot(at, side, other, landing):
        if len(strips) < 2 or landing:
            return at
        return at + (other - side) * stride

    fields_a = [(kh.at[a], n) for a, n in enumerate(X_ROWS)]
    fields_b = [(post, DEPTH)]

    def x_pack(buf, fields, first, many):
        def slab(i, carry):
            for face, step in enumerate((1, -1)):
                at = i * sum(n for _, n in fields)
                for ref, n in fields:
                    src, _ = x_rows(step, n)
                    buf[face, pl.ds(at, n), :] = ref[i + first, src, :]
                    at = at + n
            return carry

        if n_gx > 1:
            loop(many, slab, 0)

    def x_unpack(buf, fields, first, many):
        for face, step in enumerate((1, -1)):
            def slab(i, carry):
                at = i * sum(n for _, n in fields)
                for ref, n in fields:
                    _, dst = x_rows(step, n)
                    ref[i + first, dst, :] = buf[face, pl.ds(at, n), :]
                    at = at + n
                return carry

            def side(slab=slab):
                loop(many, slab, 0)

            if n_gx > 1:
                pl.when(x_side(-step))(side)

    def own_columns(value, z, packs):
        result = []
        n = value.shape[0]
        for (edge, own, _, _, _, _, _), pack in zip(strips, packs):
            to = z * GROUP + own
            result.append(jnp.where(lane[:n] == to, spin(value, to - edge), pack))
        return tuple(result)

    def own_mask(own):
        return jnp.logical_and(column == own, zgroup < pairs + 2 * halo)

    x_pack(xs, fields_a, halo + 1, pairs)
    a_args = ((xs, xr), ps, sh, a_send, a_recv)
    e_args = ((xs2, xr2), pe, re, e_send, e_recv)
    pl.semaphore_wait(barrier, n_friends if near else count - 1)

    z_edge = (nz - DEPTH) * (1 - gz)
    z_copies = [
        pltpu.make_async_remote_copy(
            src_ref=src.at[pl.ds(z_edge, DEPTH)],
            dst_ref=dst,
            send_sem=z_send.at[i],
            recv_sem=z_recv.at[i],
            device_id={"gz": 1 - gz},
            device_id_type=MESH,
        )
        for i, (src, dst) in enumerate(((mat, zmat), (heat, zheat)))
    ]
    for copy in z_copies:
        copy.start()
    first_copies = list(messages(*a_args, False))
    to_x = 2 if n_gx > 1 else 0
    for exists, copy in first_copies[:to_x]:
        guarded(exists, copy.start)
    packs = loop(pairs, own_strip, tuple((ones, ones, nothing, nothing) for _ in strips), 8)
    for side, pack in enumerate(packs):
        for a in range(4):
            ps[side, a, pl.ds(PAD, nx), :] = pack[a]
    for exists, copy in first_copies[to_x:]:
        guarded(exists, copy.start)
    relay(0)
    for copy in z_copies:
        copy.wait_recv()
    beyond = 1 + (pairs + halo) * (1 - gz)
    packs = [nothing for _ in strips]
    for g in range(halo):
        values = store_pair(beyond + g, zmat[2 * g], zmat[2 * g + 1], zheat[2 * g], zheat[2 * g + 1])
        for side, at in enumerate(strips):
            for a in range(4):
                to = a * (ny // 4) + g * GROUP + 1
                here = jnp.logical_and(lane_own >= to, lane_own < to + DEPTH)
                packs[side] = jnp.where(here, spin(values[a], to - at[3]), packs[side])
    for side, pack in enumerate(packs):
        pe[side, pl.ds(PAD, nx), :] = pack
    x_pack(xs2, fields_a, beyond, halo)
    for exists, copy in messages(*e_args, False):
        guarded(exists, copy.start)

    blank = jnp.zeros((full, ny), jnp.float32)
    for field in (red, black, post):
        for slab in (0, 1 + (pairs + halo) * gz, 2 + (pairs + halo) * gz, pairs + 2 * halo + 1):
            field[slab] = jnp.zeros((nx + 2 * PAD, ny), jnp.float32)

        def clear(z, carry):
            field[z, pl.ds(0, PAD), :] = jnp.zeros((PAD, ny), jnp.float32)
            field[z, pl.ds(PAD + nx, PAD), :] = jnp.zeros((PAD, ny), jnp.float32)
            return carry

        loop(pairs + 2 * halo + 2, clear, 0)
    for side in range(len(strips)):
        for buf in (sred, sblack):
            buf[side] = jnp.zeros((nx + 2 * PAD, ny), jnp.float32)
        for row in (PAD - DEPTH - 1, PAD + nx + DEPTH):
            spost[side, pl.ds(row, 1), :] = jnp.zeros((1, ny), jnp.float32)

    def calm(slab, carry):
        for a in range(2):
            for row in (PAD - DEPTH - 1, PAD + nx + DEPTH):
                kh[a, slab, pl.ds(row, 1), :] = jnp.ones((1, ny), jnp.float32)
        return carry

    loop(pairs + 2 * halo + 2, calm, 0)
    for side in range(len(strips)):
        for a in range(2):
            for row in (PAD - DEPTH - 1, PAD + nx + DEPTH):
                sh[side, a, pl.ds(row, 1), :] = jnp.ones((1, ny), jnp.float32)

    def fill(start):
        def slab(z, carry):
            for a in range(4):
                kh[a, z, pl.ds(start, DEPTH), :] = jnp.full((DEPTH, ny), 1.0 if a < 2 else 0.0, jnp.float32)
            return carry

        loop(pairs + 2 * halo + 2, slab, 0)
        for side in range(len(strips)):
            for a in range(4):
                sh[side, a, pl.ds(start, DEPTH), :] = jnp.full((DEPTH, ny), 1.0 if a < 2 else 0.0, jnp.float32)

    pl.when(gx == 0)(lambda: fill(PAD - DEPTH))
    pl.when(gx == n_gx - 1)(lambda: fill(PAD + nx))
    for side, strip_of in enumerate(strips):
        if strip_of[4] is not None:
            def vacant(side=side):
                for a in range(4):
                    sh[side, a] = jnp.full((nx + 2 * PAD, ny), 1.0 if a < 2 else 0.0, jnp.float32)

            pl.when(jnp.logical_not(strip_of[4]))(vacant)

    def losses(z, carry):
        low = jnp.where(jnp.logical_and(z == 0, gz == 0), 1.0, 0.0)
        high = jnp.where(jnp.logical_and(z == pairs - 1, gz == n_gz - 1), 1.0, 0.0)
        faces = faces_open + jnp.where(even_own, low, high)
        leak[z] = faces * rcp(kh[1, z + halo + 1, pl.ds(PAD, nx), :])
        return carry

    loop(pairs, losses, 0, 4)
    for layer in range(lz):
        def add(z, total):
            return total + heat[layer * BLOCK + z]
        hsum[layer] = loop(BLOCK, add, jnp.zeros((nx, ny), jnp.float32), 4)

    def own_resist(rows):
        def step(z, packs):
            z = z + halo * (1 - gz)
            return tuple(own_columns(kh[a, z + 1, rows, :], z, packs[a]) for a in range(2))

        fresh = jnp.ones((rows.size, ny), jnp.float32)
        packs = loop(pairs + halo, step, (tuple(fresh for _ in strips),) * 2)
        for side in range(len(strips)):
            for a in range(2):
                oc[side, a, rows, :] = packs[a][side]

    own_resist(pl.ds(PAD, nx))

    relay(1)
    for args in (a_args, e_args):
        for exists, copy in messages(*args, True):
            guarded(exists, copy.wait_recv)
    x_unpack(xr, fields_a, halo + 1, pairs)
    x_unpack(xr2, fields_a, beyond, halo)
    own_resist(pl.ds(zero + (PAD - DEPTH), 8))
    own_resist(pl.ds(zero + (PAD + nx + DEPTH - 8), 8))
    wall, wall_own = halo + (pairs + 1) * gz, halo + 1 + (pairs - 1) * gz
    for a in range(2):
        kh[a, wall, rows_of(full), :] = kh[1 - a, wall_own, rows_of(full), :]
    x_first = beyond - 1
    came = jnp.logical_and(zgroup >= x_first, zgroup < x_first + halo)
    for side, at in enumerate(strips):
        extra = re[side, rows_of(full), :]
        whole = []
        for a in range(4):
            value = jnp.where(came, spin(extra, x_first * GROUP - a * (ny // 4)), sh[side, a, rows_of(full), :])
            if a < 2:
                value = jnp.where(own_mask(at[1]), oc[side, a, rows_of(full), :], value)
            whole.append(value)
        for a in range(4):
            value = whole[a]
            if a < 2:
                value = jnp.where(zgroup == wall - 1, spin(whole[1 - a], GROUP * (2 * gz - 1)), value)
            sh[side, a, rows_of(full), :] = value

    def mirror(outer, inner):
        def slab(z, carry):
            for a in range(2):
                kh[a, z + 1, outer, :] = kh[1 - a, z + 1, inner, :]
            return carry

        loop(pairs + 2 * halo, slab, 0)
        for side in range(len(strips)):
            for a in range(2):
                sh[side, a, outer, :] = sh[side, 1 - a, inner, :]

    pl.when(gx == 0)(lambda: mirror(pl.ds(PAD - 1, 1), pl.ds(PAD, 1)))
    pl.when(gx == n_gx - 1)(lambda: mirror(pl.ds(PAD + nx, 1), pl.ds(PAD + nx - 1, 1)))

    wide, inner = [(True, t) for t in range(full // 8)], [(False, t) for t in range(nx // 8)]
    even8, lane8, column_step = even_own[:8], lane_own[:8], lax.rem(lane_own[:8], BLOCK) == 0
    open8 = open_lane(8)
    closed8 = jnp.where(open8, 0.0, 1.0)

    def at(tile, shift=0):
        deep, t = tile
        if not deep and shift == 0:
            return pl.ds(PAD + 8 * t, 8)
        return pl.ds(zero + (PAD - (DEPTH if deep else 0) + 8 * t + shift), 8)

    def cut(tile):
        deep, t = tile
        return pl.ds(8 * t, 8) if deep else pl.ds(zero + (DEPTH + 8 * t), 8)

    def halos_of(refs, tiles):
        return [[ref[at(tile), :] for ref in refs] for tile in tiles]

    def beside(value, halos, z, walls):
        low, high = pltpu.roll(value, 1, 1), pltpu.roll(value, ny - 1, 1)
        ends = [
            spin(near_by, edge - (z * GROUP + adj))
            for near_by, (edge, _, adj, _, _, _, _) in zip(halos, strips)
        ]
        ends = ends or [value]
        if walls is None:
            ends = [end * closed8 for end in ends]
        else:
            ends = [jnp.where(open8, walls, end) for end in ends]
        return jnp.where(lane8 == 0, ends[0], low), jnp.where(lane8 == ny - 1, ends[-1], high)

    def around(field, color, z, tile, halos, walls=None):
        here = z + 1
        same = field[here, at(tile), :]
        before, after = field[here - 1, at(tile), :], field[here + 1, at(tile), :]
        low, high = beside(same, halos, z, walls)
        return (
            same,
            jnp.where(even8, before, after) if color == 0 else jnp.where(even8, after, before),
            field[here, at(tile, -1), :],
            field[here, at(tile, 1), :],
            low,
            high,
        )

    def tile_packs(values, z, packs):
        return tuple(own_columns(value, z, pack) for value, pack in zip(values, packs))

    blank8 = jnp.zeros((8, ny), jnp.float32)
    no_packs = tuple(tuple(blank8 for _ in strips) for _ in wide)

    def joined(packs, side):
        return jnp.concatenate([pack[side] for pack in packs], axis=0)

    def strip_around(ref, color):
        same = ref[rows_of(full), :]
        before, after = pltpu.roll(same, GROUP, 1), pltpu.roll(same, ny - GROUP, 1)
        return (
            same,
            jnp.where(even, after, before) if color == 0 else jnp.where(even, before, after),
            ref[rows_of(full, -1), :],
            ref[rows_of(full, 1), :],
            pltpu.roll(same, 1, 1),
            pltpu.roll(same, ny - 1, 1),
        )

    def shares(center, others):
        parts = [rcp(center + other) for other in others]
        total = parts[0]
        for part in parts[1:]:
            total = total + part
        return parts, total

    def strip_weigh(color):
        for side in range(len(strips)):
            a = 1 - color
            center = sh[side, a, rows_of(full), :]
            parts, total = shares(center, strip_around(sh.at[side, 1 - a], color))
            inverse = jnp.where(in_strip, rcp(total), 0.0)
            if strips[side][4] is not None:
                inverse = jnp.where(strips[side][4], inverse, 0.0)
            for face in range(6):
                swd[side, color, face] = parts[face] * inverse
            shd[side, color] = sh[side, 2 + color, rows_of(full), :] * (0.5 * inverse)

    def weigh(color):
        a = 1 - color
        halos = halos_of([sh.at[side, 1 - a] for side in range(len(strips))], wide)

        def step(i, packs):
            z = i + halo * (1 - gz)
            ratios = []
            for tile in wide:
                t = tile[1]
                center = kh[a, z + 1, at(tile), :]
                parts, total = shares(center, around(kh.at[1 - a], color, z, tile, halos[t], center))
                inverse = rcp(total)
                if t in (0, len(wide) - 1):
                    inverse = jnp.where(inside_row[8 * t : 8 * t + 8], inverse, 0.0)
                for face in range(6):
                    wd[color, face, z, cut(tile), :] = parts[face] * inverse
                ratio = kh[2 + color, z + 1, at(tile), :] * (0.5 * inverse)
                hd[color, z, cut(tile), :] = ratio
                if color == 1:
                    dg[z, cut(tile), :] = total * 2.0
                else:
                    red[z + 1, at(tile), :] = ratio
                    ratios.append(ratio)
            return packs if color == 1 else tile_packs(ratios, z, packs)

        return loop(pairs + halo, step, no_packs, WEIGH_UNROLL)

    for color in range(2):
        strip_weigh(color)
    packs = weigh(0)
    for side, (_, own, _, _, _, _, _) in enumerate(strips):
        sred[side, rows_of(full), :] = jnp.where(own_mask(own), joined(packs, side), shd[side, 0])
    relay(2)
    weigh(1)

    def weights_of(color, z, tile):
        return hd[color, z, cut(tile), :], [wd[color, face, z, cut(tile), :] for face in range(6)]

    def total_of(source, weights, others):
        result = source
        for weight, other in zip(weights, others):
            result = result + weight * other
        return result

    def stage(color, src, strip_src, dst, strip_dst, reach):
        halos = halos_of([strip_src.at[side] for side in range(len(strips))], wide)

        def step(i, packs):
            first = i + halo - reach * gz
            values = []
            for z in [first + k for k in range(pairs + reach)]:
                values.append([])
                for tile in wide:
                    source, weights = weights_of(color, z, tile)
                    values[-1].append(total_of(source, weights, around(src, color, z, tile, halos[tile[1]])))
            for k, row in enumerate(values):
                for tile, value in zip(wide, row):
                    dst[first + k + 1, at(tile), :] = value
            for k, row in enumerate(values):
                packs = tile_packs(row, first + k, packs)
            return packs

        packs = step(0, no_packs)
        for side, (_, own, _, _, _, _, _) in enumerate(strips):
            value = total_of(
                shd[side, color],
                [swd[side, color, face] for face in range(6)],
                strip_around(strip_src.at[side], color),
            )
            strip_dst[side, rows_of(full), :] = jnp.where(own_mask(own), joined(packs, side), value)

    stage(1, red, sred, black, sblack, 2)
    stage(0, black, sblack, red, sred, 2)

    halos = halos_of([sred.at[side] for side in range(len(strips))], inner)
    tiles = BLOCK // 8
    none = jnp.zeros((nx, ny), jnp.float32)
    sums = []
    for layer in range(lz):
        def flow(i, carry):
            z = i + layer * (BLOCK // 2) + halo
            result = []
            for tile, (own_sum, x_sum, y_sum) in zip(inner, carry):
                t = tile[1]
                source, weights = weights_of(1, z, tile)
                others = around(red, 1, z, tile, halos[t])
                value = total_of(source, weights, others)
                post[z + 1, at(tile), :] = value
                spare = dg[z, cut(tile), :]
                face = 2 if t % tiles == 0 else 3
                own_sum = own_sum + leak[z - halo, pl.ds(8 * t, 8), :] * others[0]
                if t % tiles in (0, tiles - 1):
                    x_sum = x_sum + spare * ((value - others[face]) * weights[face])
                aside, weight = (
                    jnp.where(column_step, pair[0], pair[1]) for pair in (others[4:], weights[4:])
                )
                y_sum = y_sum + spare * ((value - aside) * weight)
                result.append((own_sum, x_sum, y_sum))
            return tuple(result)

        parts = loop(BLOCK // 2, flow, tuple((blank8,) * 3 for _ in inner), FLOW_UNROLL)
        sums.append(tuple(jnp.concatenate([part[i] for part in parts], axis=0) for i in range(3)))

    z_from, z_to = halo + 1 + (pairs - halo) * (1 - gz), 1 + (pairs + halo) * gz
    z_back = 1 + (pairs + halo) * (1 - gz)
    own = pl.ds(PAD, nx)
    z_copy = [
        pltpu.make_async_remote_copy(
            src_ref=post.at[pl.ds(z_from, halo), own],
            dst_ref=post.at[pl.ds(to, halo), own],
            send_sem=z_send.at[2],
            recv_sem=z_recv.at[2],
            device_id={"gz": 1 - gz},
            device_id_type=MESH,
        )
        for to in (z_to, z_back)
    ]
    z_copy[0].start()

    totals = [none, *(hsum[layer] - sums[layer][0] for layer in range(lz)), none]
    for layer in range(lz):
        for late in range(2):
            z = halo + layer * (BLOCK // 2) + (BLOCK // 2 - 1) * late
            beyond_z = red[z + 2, own, :] if late else red[z, own, :]
            deep_rows = pl.ds(zero + DEPTH, nx)
            flux = dg[z, deep_rows, :] * wd[1, 1, z, deep_rows, :] * (post[z + 1, own, :] - beyond_z)
            flux = jnp.where(even_own, flux, 0.0) if late else jnp.where(even_own, 0.0, flux)
            totals[layer + 1] = totals[layer + 1] - flux
            to = layer + 2 if late else layer
            totals[to] = totals[to] + flux
    for i, value in enumerate((*totals, *(s[2] for s in sums))):
        vsum[:, i * ny : (i + 1) * ny] = value
    for copy in fetch:
        copy.wait()
    part = jnp.dot(shrink[0], vsum[...], precision=HIGH, preferred_element_type=jnp.float32)
    for layer in range(lz):
        vsum[:, layer * ny : (layer + 1) * ny] = sums[layer][1]
    bent = jnp.dot(shrink[1], vsum[:, : lz * ny], precision=HIGH, preferred_element_type=jnp.float32)
    turned_part = [part[:, i * ny : (i + 1) * ny] for i in range(2 * lz + 2)]
    for layer in range(lz):
        turned_part[layer + 1] = turned_part[layer + 1] + bent[:, layer * ny : (layer + 1) * ny]
    part = times(jnp.concatenate(turned_part, axis=1), (gather[0], gather[1]))
    got[me] = part

    def gathering(step, start):
        other, where = peer_of(step)
        copy = pltpu.make_async_remote_copy(
            src_ref=got.at[me],
            dst_ref=got.at[me if start else other],
            send_sem=gsend.at[step],
            recv_sem=grecv.at[me if start else other],
            device_id=where,
            device_id_type=MESH,
        )
        return copy

    relay(3)
    each_peer(lambda step: gathering(step, True).start())

    z_copy[1].wait_recv()

    def pack_post(z, packs):
        z = z + halo * (1 - gz)
        value = post[z + 1, own, :]
        return tuple(gather_strip(value, z, s[3], pack) for s, pack in zip(strips, packs))

    packs = loop(pairs + halo, pack_post, tuple(none for _ in strips))
    for side, pack in enumerate(packs):
        psb[side, own, :] = pack
    x_pack(xsb, fields_b, 1 + halo * (1 - gz), pairs + halo)
    b_args = ((xsb, xrb), psb, spost, b_send, b_recv)
    for exists, copy in messages(*b_args, False):
        guarded(exists, copy.start)

    each_peer(lambda step: gathering(step, False).wait_recv())
    if count <= 32:
        hat = got[0]
        for i in range(1, count):
            hat = hat + got[i]
    else:
        hat = lax.fori_loop(1, count, lambda i, acc: acc + got[i], got[0])
    kbar = table[0]
    for m in range(1, table.shape[0]):
        kbar = kbar + table[m]
    kbar = kbar / table.shape[0]
    hat = hat * scale[...] / kbar
    hat = times(hat, (spread[0], spread[1]))
    rise = jnp.dot(expand[...], hat, precision=HIGH, preferred_element_type=jnp.float32)
    for i in range(corr.shape[0]):
        corr[i] = rise[:, i * ny : (i + 1) * ny]

    z_copy[0].wait_send()
    for exists, copy in messages(*b_args, False):
        guarded(exists, copy.wait_send)
    for exists, copy in messages(*b_args, True):
        guarded(exists, copy.wait_recv)
    x_unpack(xrb, fields_b, 1 + halo * (1 - gz), pairs + halo)

    def correct(i, packs):
        z = i + halo * (1 - gz)
        layer = (z + BLOCK // 2 - halo) // (BLOCK // 2)
        value = post[z + 1, rows_of(full), :]
        value = value + corr[layer, rows_of(full), :]
        post[z + 1, rows_of(full), :] = value
        return own_columns(value, z, packs)

    packs = loop(pairs + halo, correct, tuple(blank for _ in strips))
    for side, (_, own_c, _, _, exists, _, _) in enumerate(strips):
        value = spost[side, rows_of(full), :] + corr[lz + 2 + side, rows_of(full), :]
        value = jnp.where(in_strip, value, 0.0)
        if exists is not None:
            value = jnp.where(exists, value, 0.0)
        spost[side, rows_of(full), :] = jnp.where(own_mask(own_c), packs[side], value)

    stage(0, post, spost, red, sred, 2)
    stage(1, red, sred, black, sblack, 2)
    stage(0, black, sblack, red, sred, 2)

    halos = halos_of([sred.at[side] for side in range(len(strips))], inner)

    def finish(i, carry):
        z = i + halo
        for tile in inner:
            source, weights = weights_of(1, z, tile)
            others = around(red, 1, z, tile, halos[tile[1]])
            last = total_of(source, weights, others)
            rows = pl.ds(8 * tile[1], 8)
            out[2 * i, rows, :] = jnp.where(even8, others[0], last)
            out[2 * i + 1, rows, :] = jnp.where(even8, last, others[0])
        return carry

    loop(pairs, finish, 0, FINISH_UNROLL)

    for copy in z_copies:
        copy.wait_send()
    for args in (a_args, e_args):
        for exists, copy in messages(*args, False):
            guarded(exists, copy.wait_send)
    each_peer(lambda step: gathering(step, True).wait_send())


def per_device(sizes, heat, material, table):
    shape = heat.shape
    nz, nx, ny = shape
    n_gx, n_gy, n_gz = sizes
    assert n_gz == 2
    consts = tables(shape, *sizes)
    spread, gather, expand, shrink, scale = consts
    count = n_gx * n_gy * n_gz
    rows = nx + 2 * PAD
    full = nx + 2 * DEPTH
    sides = max(sides_of(n_gy), 1)
    pairs = nz // 2
    lz = nz // BLOCK
    deep = pairs + DEPTH
    f32 = jnp.float32
    vmem = pl.BlockSpec(memory_space=pltpu.VMEM)
    hbm = pl.BlockSpec(memory_space=pltpu.HBM)
    field = pltpu.VMEM((deep + 2, rows, ny), f32)
    strip = pltpu.VMEM((sides, rows, ny), f32)
    sems = pltpu.SemaphoreType.DMA
    return pl.pallas_call(
        functools.partial(kernel, sizes, shape),
        out_shape=pltpu.VMEM(shape, f32),
        in_specs=[hbm] * 8,
        out_specs=vmem,
        scratch_shapes=[
            pltpu.VMEM(shape, f32),
            pltpu.VMEM(shape, jnp.int32),
            pltpu.VMEM((DEPTH, nx, ny), f32),
            pltpu.VMEM((DEPTH, nx, ny), jnp.int32),
            pltpu.SMEM(table.shape, f32),
            pltpu.VMEM((4, deep + 2, rows, ny), f32),
            pltpu.VMEM((sides, 4, rows, ny), f32),
            pltpu.VMEM((sides, 4, rows, ny), f32),
            strip, strip,
            pltpu.VMEM((sides, 2, rows, ny), f32),
            *[pltpu.VMEM((2, pairs * sum(X_ROWS), ny), f32)] * 2,
            *[pltpu.VMEM((2, DEPTH // 2 * sum(X_ROWS), ny), f32)] * 2,
            *[pltpu.VMEM((2, (deep - DEPTH // 2) * DEPTH, ny), f32)] * 2,
            field, field, field,
            strip, strip, strip, strip,
            pltpu.VMEM((2, 6, deep, full, ny), f32),
            pltpu.VMEM((2, deep, full, ny), f32),
            pltpu.VMEM((deep, full, ny), f32),
            pltpu.VMEM((pairs, nx, ny), f32),
            pltpu.VMEM((sides, 2, 6, full, ny), f32),
            pltpu.VMEM((sides, 2, full, ny), f32),
            pltpu.VMEM((lz, nx, ny), f32),
            pltpu.VMEM((nx, gather.shape[3]), f32),
            pltpu.VMEM((spread.shape[4] // ny, rows, ny), f32),
            pltpu.VMEM(spread.shape[2:], jnp.bfloat16),
            pltpu.VMEM(gather.shape[2:], jnp.bfloat16),
            pltpu.VMEM(expand.shape[1:], f32),
            pltpu.VMEM(shrink.shape[1:], f32),
            pltpu.VMEM(scale.shape, f32),
            pltpu.VMEM((count, *scale.shape), f32),
            sems((8,)),
            sems((3,)),
            sems((3,)),
            sems((8,)),
            sems((8,)),
            sems((8,)),
            sems((8,)),
            sems((8,)),
            sems((8,)),
            sems((count,)),
            sems((count,)),
            pltpu.SemaphoreType.REGULAR((RELAYS,)),
        ],
        compiler_params=pltpu.CompilerParams(
            collective_id=0, has_side_effects=True, vmem_limit_bytes=64 * 1024 * 1024 - 3 * nz * nx * ny * 2
        ),
    )(heat, material, table, *(jnp.asarray(c) for c in consts))


def solution(mesh):
    sizes = (mesh.shape["gx"], mesh.shape["gy"], mesh.shape["gz"])
    spec = P("gz", ("groups", "gx"), "gy")
    return jax.shard_map(
        functools.partial(per_device, sizes),
        mesh=mesh,
        in_specs=(spec, spec, P()),
        out_specs=spec,
        check_vma=False,
    )
```
